32 devices in a mesh: dp: 8 (over y, x, core), tensor: 4 (over z).
Axes of the slice: x: 2, y: 2, z: 4, core: 2. Of those that a mesh axis runs over, the one named last changes fastest.
Arguments:
- frames: bfloat16 [8192, 1024], P('dp'), may hold values from -6 to 6
- skip_in: bfloat16 [8192, 1024], P('dp'), may hold values from -6 to 6
- flow_time: float32 [8], P('dp'), may hold values from 0 to 1
- segment_ids: int32 [8, 1024], P('dp'), may hold values from 0 to 3, never falling along the last dimension, each value on 1 to 512 neighbouring positions
- w_skip: bfloat16 [2048, 1024], P(None, 'tensor'), may hold values from -0.125 to 0.125
- b_skip: float32 [1024], P('tensor'), may hold values from -1.5 to 1.5
- w_modulation: bfloat16 [1024, 6144], P(None, 'tensor'), may hold values from -0.1875 to 0.1875
- b_modulation: float32 [6144], P('tensor'), may hold values from -4 to 4
- w_query: bfloat16 [1024, 1024], P(None, 'tensor'), may hold values from -0.1875 to 0.1875
- w_key: bfloat16 [1024, 1024], P(None, 'tensor'), may hold values from -0.1875 to 0.1875
- w_value: bfloat16 [1024, 1024], P(None, 'tensor'), may hold values from -0.1875 to 0.1875
- w_out: bfloat16 [1024, 1024], P('tensor'), may hold values from -0.75 to 0.75
- w_up: bfloat16 [1024, 4096], P(None, 'tensor'), may hold values from -0.1875 to 0.1875
- b_up: float32 [4096], P('tensor'), may hold values from -2.5 to 2.5
- w_down: bfloat16 [4096, 1024], P('tensor'), may hold values from -0.09375 to 0.09375
- b_down: float32 [1024], replicated, may hold values from -2.5 to 2.5
- out_grad: bfloat16 [8192, 1024], P('dp'), may hold values from -6 to 6
Outputs:
- output: float32 [8192, 1024], P('dp', 'tensor')
- grad_frames: float32 [8192, 1024], P('dp', 'tensor')
- grad_skip: float32 [8192, 1024], P('dp', 'tensor')
- grad_w_skip: float32 [2048, 1024], P('dp', 'tensor')
- grad_b_skip: float32 [1024], P(('tensor', 'dp'))
- grad_w_modulation: float32 [1024, 6144], P('dp', 'tensor')
- grad_b_modulation: float32 [6144], P(('tensor', 'dp'))
- grad_w_query: float32 [1024, 1024], P('dp', 'tensor')
- grad_w_key: float32 [1024, 1024], P('dp', 'tensor')
- grad_w_value: float32 [1024, 1024], P('dp', 'tensor')
- grad_w_out: float32 [1024, 1024], P('tensor', 'dp')
- grad_w_up: float32 [1024, 4096], P('dp', 'tensor')
- grad_b_up: float32 [4096], P(('tensor', 'dp'))
- grad_w_down: float32 [4096, 1024], P('tensor', 'dp')
- grad_b_down: float32 [1024], P('dp')
The draws below stay inside these ranges and needn't reach their ends.
Inputs may be any that keep to these rules, and one draw needn't show every extreme that they name: `segment_ids`: within each packed row of 1024 frames the ids run 0 to 3 in order and never fall; each utterance has 1 to 512 frames, one exactly that many.
All inputs are finite; a program needn't handle non-finite values.
Results may differ from the reference program's by a relative error of at most 0.018.
Values sent between devices are 32-bit elements; how exact they have to be, the bound alone decides.
A program may use at most 192 MiB of HBM per device.

```python
import math
import jax
import jax.numpy as jnp
import numpy as np
from jax import lax

D = 1024
HEAD_DIM = 64
FF = 4096
ROW_LEN = 1024
SEGS = 4
ROWS = 8
TOKENS = 8192


def spiked(entries, rng, source, target, shards_of, factor):
    def block_of(axis_at):
        return (jnp.arange(entries.shape[axis_at]) // (entries.shape[axis_at] // shards_of)).reshape((-1,) + (1,) * (entries.ndim - 1 - axis_at))

    one_side = jax.random.permutation(rng, shards_of)[block_of(target)]
    far = (block_of(target) + shards_of // 2) % shards_of
    return jnp.where((block_of(source) == one_side) | (block_of(source) == far), factor * entries, entries)


def block_levels(own_key, shape, shards, smallest, high):
    loudness, own = 1.0, jax.random.fold_in(own_key, 6)
    for axis_at, parts in shards:
        steps = jnp.exp(jax.random.uniform(jax.random.fold_in(own, axis_at), (parts,), jnp.float32, smallest / len(shards), high / len(shards)))
        loudness = loudness * jnp.repeat(steps, shape[axis_at] // parts).reshape([-1 if axis == axis_at else 1 for axis in range(len(shape))])
    return loudness


def split_up(count, total, most, lean):
    portions = [(1 << 20) // math.isqrt(grade ** lean) + 1 for grade in range(2, count + 1)]
    spare, counts = total - most - (count - 1), [1] * (count - 1)
    while spare > 0:
        free = [i for i in range(count - 1) if counts[i] < most]
        mass, remaining = sum([portions[i] for i in free]), spare
        for i in free:
            addition = min(most - counts[i], max(1, remaining * portions[i] // mass), spare)
            counts[i] = counts[i] + addition
            spare = spare - addition
    return np.array([most] + counts)


def ragged(rng, number_of, total, most, lean):
    if number_of == 2:
        one = jax.random.randint(rng, (), max(1, total - most), min(most, total - 1) + 1)
        return jnp.stack([one, total - one])
    sizes = jnp.asarray(split_up(number_of, total, most, lean), jnp.int32)
    twos = (number_of - 1) // 2
    donor, taker = sizes[1:1 + 2 * twos:2], sizes[2:2 + 2 * twos:2]
    room = jnp.minimum(donor - 1, most - taker)
    passed = jax.random.randint(jax.random.fold_in(rng, 1), (twos,), 0, 1 << 20) % (room + 1)
    sizes = sizes.at[1:1 + 2 * twos:2].set(donor - passed).at[2:2 + 2 * twos:2].set(taker + passed)
    return sizes[jax.random.permutation(jax.random.fold_in(rng, 2), number_of)]


def normal_values(key, shape, scale, most, split=(), held_as=jnp.bfloat16):
    array = scale * jax.random.normal(key, shape, jnp.float32)
    if split:
        array = array * block_levels(key, shape, split, -0.22, 0.18)
    return jnp.clip(array, -most, most).astype(held_as)


def bell_draw_with(stream_key, extent, deviation, most, split, heavy, kind=jnp.bfloat16):
    entries = deviation * jax.random.normal(stream_key, extent, jnp.float32)
    if split:
        entries = entries * block_levels(stream_key, extent, split, -0.22, 0.18)
    return jnp.clip(spiked(entries, jax.random.fold_in(stream_key, 3), *heavy), -most, most).astype(kind)


def setup_inputs(seed: int = 0) -> dict:
    splits = jax.random.split(jax.random.key(seed), 18)
    return {
        "frames": bell_draw_with(splits[0], (TOKENS, D), 1.0, 6.0, ((0, 8),), (0, 1, 8, 2.0)),
        "skip_in": bell_draw_with(splits[1], (TOKENS, D), 1.0, 6.0, ((0, 8),), (0, 1, 8, 2.0)),
        "flow_time": jnp.clip(1.0 * jax.random.uniform(splits[2], (ROWS,), jnp.float32) ** block_levels(splits[2], (ROWS,), ((0, 8),), -0.2, 0.2), 0.0, 1.0),
        "segment_ids": jax.vmap(lambda own: jnp.searchsorted(jnp.cumsum(ragged(own, SEGS, ROW_LEN, ROW_LEN // 2, 0)), jnp.arange(ROW_LEN), side="right"))(jax.random.split(splits[3], ROWS)).reshape((ROWS, ROW_LEN)).astype(jnp.int32),
        "w_skip": normal_values(splits[4], (2 * D, D), (2 * D) ** -0.5, 0.125, ((1, 4),)),
        "b_skip": normal_values(splits[5], (D,), 0.3, 1.5, ((0, 4),), jnp.float32),
        "w_modulation": normal_values(splits[6], (D, 6 * D), D ** -0.5, 0.1875, ((1, 4),)),
        "b_modulation": normal_values(splits[7], (6 * D,), 1.0, 4.0, ((0, 4),), jnp.float32),
        "w_query": normal_values(splits[8], (D, D), D ** -0.5, 0.1875, ((1, 4),)),
        "w_key": normal_values(splits[9], (D, D), D ** -0.5, 0.1875, ((1, 4),)),
        "w_value": normal_values(splits[10], (D, D), D ** -0.5, 0.1875, ((1, 4),)),
        "w_out": normal_values(splits[11], (D, D), (D // 16) ** -0.5, 0.75, ((0, 4),)),
        "w_up": normal_values(splits[12], (D, FF), D ** -0.5, 0.1875, ((1, 4),)),
        "b_up": normal_values(splits[13], (FF,), 0.5, 2.5, ((0, 4),), jnp.float32),
        "w_down": normal_values(splits[14], (FF, D), FF ** -0.5, 0.09375, ((0, 4),)),
        "b_down": normal_values(splits[15], (D,), 0.5, 2.5, (), jnp.float32),
        "out_grad": bell_draw_with(splits[16], (TOKENS, D), 1.0, 6.0, ((0, 8),), (0, 1, 8, 2.0)),
    }


@jax.custom_vjp
def low(v):
    return lax.optimization_barrier(v.astype(jnp.bfloat16)).astype(jnp.float32)

@jax.custom_vjp
def low_back(v):
    return v

def low_keep(v):
    return (low(v), None)

def low_pass(kept, grad):
    return (grad,)

def back_keep(v):
    return (v, None)

def back_low(kept, grad):
    return (low(grad),)
low.defvjp(low_keep, low_pass)
low_back.defvjp(back_keep, back_low)
EPS = 1e-06
HIGH = lax.Precision.HIGHEST

def normalize(values):
    mean_val = lax.optimization_barrier(jnp.mean(values, axis=-1, keepdims=True))
    centred = values - mean_val
    var_val = lax.optimization_barrier(jnp.mean(centred * centred, axis=-1, keepdims=True))
    return centred * lax.rsqrt(var_val + EPS)

def modulate(hidden, shift, scale):
    return normalize(hidden) * (1.0 + scale[:, None, :]) + shift[:, None, :]

def time_embed(flow_time, width):
    half = width // 2
    freqs = jnp.exp(-math.log(10000.0) * jnp.arange(half, dtype=jnp.float32) / half)
    angles = 1000.0 * flow_time[:, None] * freqs[None, :]
    return jnp.concatenate([jnp.cos(angles), jnp.sin(angles)], axis=1)

def rotary_tables(segment_ids, head_dim):
    length = segment_ids.shape[1]
    steps = jnp.arange(length, dtype=jnp.int32)[None, :]
    starts_here = jnp.concatenate([jnp.ones_like(segment_ids[:, :1], dtype=bool), segment_ids[:, 1:] != segment_ids[:, :-1]], axis=1)
    first = lax.cummax(jnp.where(starts_here, steps, 0).astype(jnp.int32), axis=1)
    places = (steps - first).astype(jnp.float32)
    half = head_dim // 2
    inverse = jnp.exp(-math.log(10000.0) * 2.0 * jnp.arange(half, dtype=jnp.float32) / head_dim)
    angles = places[:, :, None] * inverse[None, None, :]
    return (jnp.cos(angles), jnp.sin(angles))

def rotate(values, cos_t, sin_t):
    half = values.shape[-1] // 2
    first = values[..., :half]
    second = values[..., half:]
    cos_e = cos_t[:, :, None, :]
    sin_e = sin_t[:, :, None, :]
    return jnp.concatenate([first * cos_e - second * sin_e, second * cos_e + first * sin_e], axis=-1)

def attend_row(q_row, k_row, v_row, seg_row):
    scores = jnp.einsum('qhd,khd->hqk', q_row, k_row, precision=HIGH) * q_row.shape[-1] ** (-0.5)
    scores = low_back(scores)
    same = seg_row[:, None] == seg_row[None, :]
    scores = jnp.where(same[None], scores, -1e+30)
    top = lax.optimization_barrier(jnp.max(scores, axis=-1, keepdims=True))
    expo = jnp.exp(scores - top)
    probs = low(expo / lax.optimization_barrier(jnp.sum(expo, axis=-1, keepdims=True)))
    return jnp.einsum('hqk,khd->qhd', probs, v_row, precision=HIGH)

def attend_item(item):
    return jax.checkpoint(attend_row)(item[0], item[1], item[2], item[3])

def group_layer(weights, joined, mod, seg):
    w_skip, b_skip, w_query, w_key, w_value, w_out, w_up, b_up, w_down, b_down = weights
    rows, length = seg.shape
    width = w_out.shape[1]
    heads = width // HEAD_DIM
    hidden = low_back(jnp.einsum('rlc,cd->rld', joined, w_skip, precision=HIGH)) + b_skip
    shift1, scale1, gate1, shift2, scale2, gate2 = [mod[:, i * width:(i + 1) * width] for i in range(6)]
    normed = low(modulate(hidden, shift1, scale1))
    cos_t, sin_t = rotary_tables(seg, HEAD_DIM)

    def project(weight):
        return jnp.einsum('rld,de->rle', normed, weight, precision=HIGH)
    query = low(rotate(low_back(project(w_query)).reshape(rows, length, heads, HEAD_DIM), cos_t, sin_t))
    key = low(rotate(low_back(project(w_key)).reshape(rows, length, heads, HEAD_DIM), cos_t, sin_t))
    value = low(low_back(project(w_value))).reshape(rows, length, heads, HEAD_DIM)
    attended = lax.map(attend_item, (query, key, value, seg))
    attended = low(low_back(attended.reshape(rows, length, width)))
    branch = low_back(jnp.einsum('rle,ed->rld', attended, w_out, precision=HIGH))
    mid = hidden + gate1[:, None, :] * branch
    normed2 = low(modulate(mid, shift2, scale2))
    pre = low_back(jnp.einsum('rld,df->rlf', normed2, w_up, precision=HIGH) + b_up)
    act = low(jax.nn.gelu(pre, approximate=True))
    ffn = low_back(jnp.einsum('rlf,fd->rld', act, w_down, precision=HIGH)) + b_down
    return mid + gate2[:, None, :] * ffn

def group_size(rows, length):
    limit = max(1, 4096 // length)
    best = 1
    for size in range(1, rows + 1):
        if rows % size == 0 and size <= limit:
            best = size
    return best

def reference(frames, skip_in, flow_time, segment_ids, w_skip, b_skip, w_modulation, b_modulation, w_query, w_key, w_value, w_out, w_up, b_up, w_down, b_down, out_grad):
    rows, length = segment_ids.shape
    width = frames.shape[1]
    group = group_size(rows, length)
    embed = low(jax.nn.silu(time_embed(flow_time, width)))

    def layer(frames_f, skip_f, weights, w_mod, b_mod):
        mod = low_back(jnp.dot(embed, w_mod, precision=HIGH)) + b_mod
        joined = jnp.concatenate([frames_f, skip_f], axis=1).reshape(rows // group, group, length, 2 * width)
        mods = mod.reshape(rows // group, group, 6 * width)
        segs = segment_ids.reshape(rows // group, group, length)

        def run(item):
            return group_layer(weights, item[0], item[1], item[2])
        outs = lax.map(jax.checkpoint(run), (joined, mods, segs))
        return outs.reshape(rows * length, width)
    weights = (w_skip.astype(jnp.float32), b_skip, w_query.astype(jnp.float32), w_key.astype(jnp.float32), w_value.astype(jnp.float32), w_out.astype(jnp.float32), w_up.astype(jnp.float32), b_up, w_down.astype(jnp.float32), b_down)
    output, pullback = jax.vjp(layer, frames.astype(jnp.float32), skip_in.astype(jnp.float32), weights, w_modulation.astype(jnp.float32), b_modulation)
    grad_frames, grad_skip, grad_weights, grad_w_mod, grad_b_mod = pullback(out_grad.astype(jnp.float32))
    g_w_skip, g_b_skip, g_w_query, g_w_key, g_w_value, g_w_out, g_w_up, g_b_up, g_w_down, g_b_down = grad_weights
    return (output, grad_frames, grad_skip, g_w_skip, g_b_skip, grad_w_mod, grad_b_mod, g_w_query, g_w_key, g_w_value, g_w_out, g_w_up, g_b_up, g_w_down, g_b_down)
```

```python
import functools
import math

import jax
import jax.numpy as jnp
from jax import lax
from jax.experimental import pallas as pl
from jax.experimental.pallas import tpu as pltpu
from jax.sharding import PartitionSpec as P

HEAD_DIM = 64
EPS = 1e-06
F32 = jnp.float32
BF16 = jnp.bfloat16
MESH = pl.DeviceIdType.MESH
ANY = pl.BlockSpec(memory_space=pl.ANY)
VMEM = pl.BlockSpec(memory_space=pltpu.VMEM)
GROUP = 8
NT = (((1,), (1,)), ((), ()))
NN = (((1,), (0,)), ((), ()))


def dot(a, b, dims=NN, precision=None):
    return lax.dot_general(a, b, dims, precision=precision, preferred_element_type=F32)


def remote(src, dst, send, recv, device):
    return pltpu.make_async_remote_copy(
        src_ref=src,
        dst_ref=dst,
        send_sem=send,
        recv_sem=recv,
        device_id=device,
        device_id_type=MESH,
    )


def gather_kernel(chunks, nz, *refs):
    n = len(chunks)
    (p_skip, p_qkv, p_o, p_up, p_dn, own_skip, own_small) = refs[:7]
    (o_skip, o_qkv, o_o, o_up, o_dn, o_small) = refs[7:13]
    zs, zr, ps, pr, ls = refs[13:]
    dp = lax.axis_index("dp")
    z = lax.axis_index("tensor")
    p = lax.rem(dp, GROUP)
    core = lax.rem(dp, 2)
    xb = lax.rem(dp // 2, 2)
    yb = lax.rem(dp // 4, 2)
    ds_ = 1 - 2 * core
    dx = 2 - 4 * xb
    dy = 4 - 8 * yb
    d1 = dy + core * (dx - dy)
    d2 = dx + core * (dy - dx)
    near = {1: (dp + d1, z), 2: (dp + d2, z), 3: (dp + ds_, z)}
    far = {k: (dp, lax.rem(z + nz - k, nz)) for k in range(1, nz)}
    bar = pltpu.get_barrier_semaphore()
    for device in list(near.values()) + list(far.values()):
        pl.semaphore_signal(bar, inc=1, device_id=device, device_id_type=MESH)
    pl.semaphore_wait(bar, 3 + nz - 1)
    pieces = {"skip": p_skip, "qkv": p_qkv, "o": p_o, "up": p_up, "dn": p_dn}
    outs = {"skip": o_skip, "qkv": o_qkv, "o": o_o, "up": o_up, "dn": o_dn}

    def src(ch):
        name, a, off, r = ch
        if name == "qkv":
            return pieces[name].at[a]
        return pieces[name].at[pl.ds(off, r)]

    def view(ch, k, q, zz):
        name, a, off, r = ch
        if name == "skip":
            width = p_skip.shape[1]
            return o_skip.at[pl.ds(q * p_skip.shape[0] + off, r), pl.ds(zz * width, width)]
        if name == "qkv":
            r = p_qkv.shape[1]
            return o_qkv.at[k - 1, a, pl.ds(q * r, r)]
        return outs[name].at[k - 1, pl.ds(q * pieces[name].shape[0] + off, r)]

    kk = nz - 1
    local = [
        lambda: pltpu.make_async_copy(
            own_skip, o_skip.at[:, pl.ds(z * own_skip.shape[1], own_skip.shape[1])], ls.at[0]
        ),
        lambda: pltpu.make_async_copy(own_small, o_small.at[z], ls.at[1]),
    ]

    def small(k, zz):
        return remote(own_small, o_small.at[zz], zs.at[n, k - 1], zr.at[n, k - 1], far[k])

    def zcopy(i, k, zz):
        return remote(
            src(chunks[i]),
            view(chunks[i], k, p, zz),
            zs.at[i, k - 1],
            zr.at[i, k - 1],
            far[k],
        )

    stages = {
        1: ([p], d1, 0),
        2: ([p, p + d1], d2, 1),
        3: ([p, p + d1, p + d2, p + d1 + d2], ds_, 3),
    }

    def copies(i, stage, inward):
        qs, shift, base = stages[stage]
        out = []
        for j, q in enumerate(qs):
            if inward:
                q = q + shift
            for k in range(1, nz):
                ref = view(chunks[i], k, q, lax.rem(z + k, nz))
                s = (base + j) * kk + k - 1
                out.append(remote(ref, ref, ps.at[i, s], pr.at[i, s], near[stage]))
        return out

    for c in local:
        c().start()
    for k in range(1, nz):
        small(k, z).start()
    for t in range(n + 4):
        if t < n:
            for k in range(1, nz):
                zcopy(t, k, z).start()
        if 0 <= t - 1 < n:
            for k in range(1, nz):
                zcopy(t - 1, k, lax.rem(z + k, nz)).wait_recv()
            for c in copies(t - 1, 1, False):
                c.start()
        for stage in (2, 3):
            if 0 <= t - stage < n:
                for c in copies(t - stage, stage - 1, True):
                    c.wait_recv()
                for c in copies(t - stage, stage, False):
                    c.start()
        if 0 <= t - 4 < n:
            for c in copies(t - 4, 3, True):
                c.wait_recv()
    for i in range(n):
        for k in range(1, nz):
            zcopy(i, k, z).wait_send()
        for stage in (1, 2, 3):
            for c in copies(i, stage, False):
                c.wait_send()
    for k in range(1, nz):
        small(k, z).wait_send()
        small(k, lax.rem(z + k, nz)).wait_recv()
    for c in local:
        c().wait()


def gather(p_skip, p_qkv, p_o, p_up, p_dn, own_skip, own_small, nz):
    chunks = []

    def rows(name, arr, parts):
        r = arr.shape[0] // parts
        for j in range(parts):
            chunks.append((name, 0, j * r, r))

    rows("skip", p_skip, 2)
    for a in range(3):
        chunks.append(("qkv", a, 0, 0))
    rows("o", p_o, 1)
    rows("up", p_up, 4)
    rows("dn", p_dn, 4)
    n = len(chunks)
    sd = jax.ShapeDtypeStruct
    kk = nz - 1
    outs = [
        sd((p_skip.shape[0] * GROUP, p_skip.shape[1] * nz), F32),
        sd((kk, 3, p_qkv.shape[1] * GROUP, p_qkv.shape[2]), F32),
        sd((kk, p_o.shape[0] * GROUP, p_o.shape[1]), F32),
        sd((kk, p_up.shape[0] * GROUP, p_up.shape[1]), F32),
        sd((kk, p_dn.shape[0] * GROUP, p_dn.shape[1]), F32),
        sd((nz,) + own_small.shape, F32),
    ]
    dma = pltpu.SemaphoreType.DMA
    return pl.pallas_call(
        functools.partial(gather_kernel, chunks, nz),
        out_shape=outs,
        in_specs=[ANY] * 7,
        out_specs=[ANY] * 6,
        scratch_shapes=[dma((n + 1, kk)), dma((n + 1, kk)), dma((n, 7 * kk)), dma((n, 7 * kk)), dma((2,))],
        compiler_params=pltpu.CompilerParams(collective_id=0, has_side_effects=True),
    )(p_skip, p_qkv, p_o, p_up, p_dn, own_skip, own_small)


def reduce_kernel(ndp, nz, na, *refs):
    bits = ndp.bit_length() - 1
    ins = refs[:na]
    small, part = refs[na : na + 2]
    outs = refs[na + 2 : 2 * na + 2]
    all_small, all_part = refs[2 * na + 2 : 2 * na + 4]
    rest = refs[2 * na + 4 :]
    recv0, lev0 = rest[:na], rest[na : 2 * na]
    half_refs = rest[2 * na : -8]
    gz, s_send, s_recv, q_send, q_recv, z_send, z_recv, l_sem = rest[-8:]
    dp = lax.axis_index("dp")
    z = lax.axis_index("tensor")
    mine = [lax.rem(dp // (1 << b), 2) for b in range(bits)]
    partner = [(dp + (1 << b) * (1 - 2 * mine[b]), z) for b in range(bits)]
    bar = pltpu.get_barrier_semaphore()

    def others(j):
        return lax.rem(dp + j, ndp)

    for j in range(1, ndp):
        pl.semaphore_signal(bar, inc=1, device_id=(others(j), z), device_id_type=MESH)
    for k in range(1, nz):
        pl.semaphore_signal(bar, inc=1, device_id=(dp, lax.rem(z + k, nz)), device_id_type=MESH)
    pl.semaphore_wait(bar, ndp - 1 + nz - 1)

    def gzc(k, zz):
        return remote(part, gz.at[zz], z_send.at[k - 1], z_recv.at[k - 1], (dp, lax.rem(z + nz - k, nz)))

    for k in range(1, nz):
        gzc(k, z).start()

    def first(a, i):
        s = 2 * i + 1 - mine[0]
        return remote(ins[a].at[s], recv0[a].at[i], s_send.at[a, i], s_recv.at[a, i], partner[0])

    for a in range(na):
        for i in range(ndp // 2):
            first(a, i).start()
    gz[z] = part[...]

    def sml(j, row):
        return remote(small, all_small.at[row], q_send.at[0, j - 1], q_recv.at[0, j - 1], (others(j), z))

    def prt(j, row):
        return remote(gz, all_part.at[row], q_send.at[1, j - 1], q_recv.at[1, j - 1], (others(j), z))

    own = [
        lambda: pltpu.make_async_copy(small, all_small.at[dp], l_sem.at[0]),
        lambda: pltpu.make_async_copy(gz, all_part.at[dp], l_sem.at[1]),
    ]
    for j in range(1, ndp):
        sml(j, dp).start()
    own[0]().start()
    for k in range(1, nz):
        gzc(k, lax.rem(z + k, nz)).wait_recv()
    for j in range(1, ndp):
        prt(j, dp).start()
    own[1]().start()
    for a in range(na):
        for i in range(ndp // 2):
            first(a, i).wait_recv()
            lev0[a][i] = ins[a][2 * i + mine[0]] + recv0[a][i]
    orders = [list(range(1, bits)), list(range(bits - 1, 0, -1))]
    state = {}
    pos = 0
    for a in range(na):
        for h in range(2):
            cw = ins[a].shape[2] // 2
            state[a, h] = (lev0[a].at[:, :, pl.ds(h * cw, cw)], list(range(1, bits)))
    pending = []
    for step in range(bits - 1):
        todo = []
        for a in range(na):
            for h in range(2):
                src, free = state[a, h]
                b = orders[h][step]
                at = free.index(b)
                lo = 1 << at
                left = [f for f in free if f != b]
                cnt = 1 << len(left)
                recv, out = half_refs[pos], half_refs[pos + 1]
                sem_s, sem_r = half_refs[pos + 2], half_refs[pos + 3]
                pos += 4
                items = []
                for i in range(cnt):
                    base = (i // lo) * 2 * lo + i % lo
                    keep = base + lo * mine[b]
                    give = base + lo * (1 - mine[b])
                    c = functools.partial(
                        remote, src.at[give], recv.at[i], sem_s.at[i], sem_r.at[i], partner[b]
                    )
                    c().start()
                    items.append((c, keep, i))
                todo.append((a, h, src, recv, out, items))
                state[a, h] = (out, left)
        for a, h, src, recv, out, items in todo:
            cw = ins[a].shape[2] // 2
            for c, keep, i in items:
                c().wait_recv()
                if step == bits - 2:
                    outs[a][:, pl.ds(h * cw, cw)] = src[keep] + recv[i]
                else:
                    out[i] = src[keep] + recv[i]
                pending.append(c)
    for c in pending:
        c().wait_send()
    for a in range(na):
        for i in range(ndp // 2):
            first(a, i).wait_send()
    for k in range(1, nz):
        gzc(k, z).wait_send()
    for j in range(1, ndp):
        sml(j, dp).wait_send()
        prt(j, dp).wait_send()
        row = lax.rem(dp + ndp - j, ndp)
        sml(j, row).wait_recv()
        prt(j, row).wait_recv()
    for c in own:
        c().wait()


def reduce_over_dp(arrays, small, part, ndp, nz, cid):
    na = len(arrays)
    bits = ndp.bit_length() - 1
    sd = jax.ShapeDtypeStruct
    dma = pltpu.SemaphoreType.DMA
    scratch = [pltpu.VMEM((ndp // 2,) + a.shape[1:], F32) for a in arrays] * 2
    for step in range(bits - 1):
        cnt = ndp >> (step + 2)
        for a in arrays:
            for h in range(2):
                shape = (cnt, a.shape[1], a.shape[2] // 2)
                scratch += [pltpu.VMEM(shape, F32), pltpu.VMEM(shape, F32), dma((cnt,)), dma((cnt,))]
    scratch += [
        pltpu.VMEM((nz,) + part.shape, F32),
        dma((na, ndp // 2)),
        dma((na, ndp // 2)),
        dma((2, ndp - 1)),
        dma((2, ndp - 1)),
        dma((nz - 1,)),
        dma((nz - 1,)),
        dma((2,)),
    ]
    return pl.pallas_call(
        functools.partial(reduce_kernel, ndp, nz, na),
        out_shape=[sd(a.shape[1:], F32) for a in arrays]
        + [sd((ndp,) + small.shape, F32), sd((ndp, nz) + part.shape, F32)],
        in_specs=[VMEM] * (na + 2),
        out_specs=[VMEM] * (na + 2),
        scratch_shapes=scratch,
        compiler_params=pltpu.CompilerParams(
            collective_id=cid, has_side_effects=True, vmem_limit_bytes=56 << 20
        ),
    )(*arrays, small, part)


def swap_halves(u):
    n = u.shape[1]
    lane = lax.broadcasted_iota(jnp.int32, u.shape, 1)
    half = HEAD_DIM // 2
    return jnp.where(
        lane % HEAD_DIM < half, pltpu.roll(u, n - half, 1), pltpu.roll(u, half, 1)
    )


def qkv_kernel(x_ref, wq_ref, wk_ref, wv_ref, w_ref, cos_ref, sin_ref, q_ref, k_ref, v_ref):
    g = pl.program_id(0)
    own = (wq_ref, wk_ref, wv_ref)
    outs = (q_ref, k_ref, v_ref)

    def run(weights):
        x = x_ref[...]
        for a in range(3):
            u = dot(x, weights[a])
            if a < 2:
                u = u * cos_ref[...] + swap_halves(u) * sin_ref[...]
            u = u.astype(BF16)
            if a == 0:
                u = u * (HEAD_DIM**-0.5)
            outs[a][...] = u

    @pl.when(g == 0)
    def _():
        run([w[...] for w in own])

    @pl.when(g > 0)
    def _():
        run([w_ref[0, a].astype(BF16) for a in range(3)])


def qkv(x, wq, wk, wv, w, cos, sin):
    t, d = x.shape
    e = wq.shape[1]
    groups = w.shape[0] + 1
    full = lambda s: pl.BlockSpec(s, lambda g: (0, 0))
    out = jax.ShapeDtypeStruct((t, groups * e), BF16)
    return pl.pallas_call(
        qkv_kernel,
        grid=(groups,),
        out_shape=[out] * 3,
        in_specs=[full((t, d))]
        + [full((d, e))] * 3
        + [pl.BlockSpec((1, 3, d, e), lambda g: (jnp.maximum(g - 1, 0), 0, 0, 0))]
        + [full((t, e))] * 2,
        out_specs=[pl.BlockSpec((t, e), lambda g: (0, g))] * 3,
        compiler_params=pltpu.CompilerParams(vmem_limit_bytes=56 << 20),
    )(x, wq, wk, wv, w, cos, sin)


QB = 256
KB = 128
NEG = -1e30


def head_mask(shape, h):
    lane = lax.broadcasted_iota(jnp.int32, shape, 1)
    return (lane // HEAD_DIM) == h


def attn_fwd_kernel(heads, lo_ref, hi_ref, q_ref, k_ref, v_ref, segq_ref, segk_ref, o_ref, lse_ref, vt_ref):
    i = pl.program_id(1)

    @pl.when(i == 0)
    def _():
        vt_ref[...] = v_ref[...].T

    q = q_ref[...]
    qm = [jnp.where(head_mask(q.shape, h), q, jnp.zeros_like(q)) for h in range(heads)]
    segq = segq_ref[0, pl.ds(0, 1)]
    rows = q.shape[0]

    def body(j, carry):
        ms, ls, os_ = carry
        start = pl.multiple_of(j * KB, KB)
        kb = k_ref[pl.ds(start, KB), :]
        segk = segk_ref[pl.ds(start, KB), :]
        same = jnp.concatenate([segk] * (rows // 128), axis=1) == segq
        nm, nl, no = [], [], []
        for h in range(heads):
            s = jnp.where(same, dot(kb, qm[h], NT), NEG)
            m = jnp.maximum(ms[h], jnp.max(s, axis=0, keepdims=True))
            alpha = jnp.exp(ms[h] - m)
            p = jnp.exp(s - m)
            nl.append(ls[h] * alpha + jnp.sum(p, axis=0, keepdims=True))
            vt = vt_ref[pl.ds(h * HEAD_DIM, HEAD_DIM), pl.ds(start, KB)]
            no.append(os_[h] * alpha + dot(vt, p.astype(BF16)))
            nm.append(m)
        return nm, nl, no

    init = (
        [jnp.full((1, rows), NEG, F32)] * heads,
        [jnp.zeros((1, rows), F32)] * heads,
        [jnp.zeros((HEAD_DIM, rows), F32)] * heads,
    )
    ms, ls, os_ = lax.fori_loop(lo_ref[i], hi_ref[i], body, init)
    out = jnp.concatenate([os_[h] / ls[h] for h in range(heads)], axis=0)
    o_ref[...] = out.T.astype(BF16)
    lse = [ms[h] + jnp.log(ls[h]) for h in range(heads)]
    lse_ref[0] = jnp.concatenate(lse + [jnp.zeros((8 - heads, rows), F32)], axis=0)


def attn_fwd(q, k, v, seg_row, seg_col, lo, hi, groups):
    t = q.shape[0]
    e = q.shape[1] // groups
    heads = e // HEAD_DIM
    return pl.pallas_call(
        functools.partial(attn_fwd_kernel, heads),
        out_shape=[
            jax.ShapeDtypeStruct(q.shape, BF16),
            jax.ShapeDtypeStruct((groups, 8, t), F32),
        ],
        grid_spec=pltpu.PrefetchScalarGridSpec(
            num_scalar_prefetch=2,
            grid=(groups, t // QB),
            in_specs=[
                pl.BlockSpec((QB, e), lambda g, i, *_: (i, g)),
                pl.BlockSpec((t, e), lambda g, i, *_: (0, g)),
                pl.BlockSpec((t, e), lambda g, i, *_: (0, g)),
                pl.BlockSpec((1, 8, QB), lambda g, i, *_: (0, 0, i)),
                pl.BlockSpec((t, 128), lambda g, i, *_: (0, 0)),
            ],
            out_specs=[
                pl.BlockSpec((QB, e), lambda g, i, *_: (i, g)),
                pl.BlockSpec((1, 8, QB), lambda g, i, *_: (g, 0, i)),
            ],
            scratch_shapes=[pltpu.VMEM((e, t), BF16)],
        ),
        compiler_params=pltpu.CompilerParams(vmem_limit_bytes=48 << 20),
    )(lo, hi, q, k, v, seg_row, seg_col)


def attn_bwd_kernel(
    heads,
    lo_ref,
    hi_ref,
    q_ref,
    k_ref,
    v_ref,
    att_ref,
    g_ref,
    lse_ref,
    segq_ref,
    segk_ref,
    cos_ref,
    sin_ref,
    gq_ref,
    gk_ref,
    gv_ref,
    kt_ref,
    dk_ref,
    dv_ref,
):
    t, e = k_ref.shape
    kt_ref[...] = k_ref[...].T
    dk_ref[...] = jnp.zeros_like(dk_ref)
    dv_ref[...] = jnp.zeros_like(dv_ref)
    row = lax.broadcasted_iota(jnp.int32, (8, e), 0)
    lane = lax.broadcasted_iota(jnp.int32, (8, e), 1)
    ind = jnp.where(lane // HEAD_DIM == row, 1.0, 0.0).astype(F32)

    @pl.loop(0, t // QB)
    def _(i):
        qs = pl.multiple_of(i * QB, QB)
        q = q_ref[pl.ds(qs, QB), :]
        g = g_ref[pl.ds(qs, QB), :]
        zero = jnp.zeros_like(q)
        qm = [jnp.where(head_mask(q.shape, h), q, zero) for h in range(heads)]
        gm = [jnp.where(head_mask(q.shape, h), g, zero) for h in range(heads)]
        segq = segq_ref[0, pl.ds(0, 1), pl.ds(qs, QB)]
        prod = g.astype(F32) * att_ref[pl.ds(qs, QB), :].astype(F32)
        delta = dot(ind, prod, NT, lax.Precision.HIGHEST)
        lse = lse_ref[0, :, pl.ds(qs, QB)]

        def body(j, dq):
            start = pl.multiple_of(j * KB, KB)
            kb = k_ref[pl.ds(start, KB), :]
            vb = v_ref[pl.ds(start, KB), :]
            segk = segk_ref[pl.ds(start, KB), :]
            same = jnp.concatenate([segk] * (QB // 128), axis=1) == segq
            ndq = []
            dk = dk_ref[pl.ds(start, KB), :]
            dv = dv_ref[pl.ds(start, KB), :]
            for h in range(heads):
                s = jnp.where(same, dot(kb, qm[h], NT), NEG)
                p = jnp.exp(s - lse[h : h + 1])
                dp_ = dot(vb, gm[h], NT)
                ds = (p * (dp_ - delta[h : h + 1])).astype(BF16)
                dv = dv + dot(p.astype(BF16), gm[h])
                dk = dk + dot(ds, qm[h])
                kt = kt_ref[pl.ds(h * HEAD_DIM, HEAD_DIM), pl.ds(start, KB)]
                ndq.append(dq[h] + dot(kt, ds))
            dk_ref[pl.ds(start, KB), :] = dk
            dv_ref[pl.ds(start, KB), :] = dv
            return ndq

        dq = lax.fori_loop(
            lo_ref[i], hi_ref[i], body, [jnp.zeros((HEAD_DIM, QB), F32)] * heads
        )
        dqf = jnp.concatenate(dq, axis=0).T * (HEAD_DIM**-0.5)
        cos = cos_ref[pl.ds(qs, QB), :]
        sin = sin_ref[pl.ds(qs, QB), :]
        gq_ref[pl.ds(qs, QB), :] = (dqf * cos - swap_halves(dqf) * sin).astype(BF16)

    dk = dk_ref[...]
    gk_ref[...] = (dk * cos_ref[...] - swap_halves(dk) * sin_ref[...]).astype(BF16)
    gv_ref[...] = dv_ref[...].astype(BF16)


def attn_bwd(q, k, v, att, g, lse, seg_row, seg_col, lo, hi, cos, sin, groups):
    t = q.shape[0]
    e = q.shape[1] // groups
    heads = e // HEAD_DIM
    col = pl.BlockSpec((t, e), lambda g, *_: (0, g))
    full = lambda s: pl.BlockSpec(s, lambda g, *_: (0, 0))
    return pl.pallas_call(
        functools.partial(attn_bwd_kernel, heads),
        out_shape=[jax.ShapeDtypeStruct(q.shape, BF16)] * 3,
        grid_spec=pltpu.PrefetchScalarGridSpec(
            num_scalar_prefetch=2,
            grid=(groups,),
            in_specs=[col] * 5
            + [
                pl.BlockSpec((1, 8, t), lambda g, *_: (g, 0, 0)),
                pl.BlockSpec((1, 8, t), lambda g, *_: (0, 0, 0)),
                full((t, 128)),
                full((t, e)),
                full((t, e)),
            ],
            out_specs=[col] * 3,
            scratch_shapes=[
                pltpu.VMEM((e, t), BF16),
                pltpu.VMEM((t, e), F32),
                pltpu.VMEM((t, e), F32),
            ],
        ),
        compiler_params=pltpu.CompilerParams(vmem_limit_bytes=56 << 20),
    )(lo, hi, q, k, v, att, g, lse, seg_row, seg_col, cos, sin)


def gnormed_kernel(gq_ref, gk_ref, gv_ref, wq_ref, wk_ref, wv_ref, w_ref, o_ref):
    g = pl.program_id(0)
    grads = (gq_ref, gk_ref, gv_ref)
    own = (wq_ref, wk_ref, wv_ref)

    @pl.when(g == 0)
    def _():
        o_ref[...] = dot(gq_ref[...], wq_ref[...], NT)
        for a in (1, 2):
            o_ref[...] += dot(grads[a][...], own[a][...], NT)

    @pl.when(g > 0)
    def _():
        for a in range(3):
            o_ref[...] += dot(grads[a][...], w_ref[0, a].astype(BF16), NT)


def gnormed(gq, gk, gv, wq, wk, wv, w):
    t = gq.shape[0]
    d, e = wq.shape
    groups = w.shape[0] + 1
    full = lambda s: pl.BlockSpec(s, lambda g: (0, 0))
    return pl.pallas_call(
        gnormed_kernel,
        grid=(groups,),
        out_shape=jax.ShapeDtypeStruct((t, d), F32),
        in_specs=[pl.BlockSpec((t, e), lambda g: (0, g))] * 3
        + [full((d, e))] * 3
        + [pl.BlockSpec((1, 3, d, e), lambda g: (jnp.maximum(g - 1, 0), 0, 0, 0))],
        out_specs=full((t, d)),
        compiler_params=pltpu.CompilerParams(vmem_limit_bytes=56 << 20),
    )(gq, gk, gv, wq, wk, wv, w)


def stats(values):
    mean_val = jnp.mean(values, axis=-1, keepdims=True)
    centred = values - mean_val
    r = lax.rsqrt(jnp.mean(centred * centred, axis=-1, keepdims=True) + EPS)
    return centred * r, r


def norm_pull(x, r, scale, grad):
    gp = grad * (1.0 + scale)
    return r * (
        gp - jnp.mean(gp, axis=-1, keepdims=True) - x * jnp.mean(gp * x, axis=-1, keepdims=True)
    )


def time_freqs(width):
    half = width // 2
    return jnp.exp(-math.log(10000.0) * jnp.arange(half, dtype=F32) / half)


def time_embed(flow_time, width):
    angles = 1000.0 * flow_time[:, None] * time_freqs(width)[None, :]
    both = jnp.concatenate([jnp.cos(angles), jnp.sin(angles)], axis=1)
    return jax.nn.silu(both).astype(BF16)


def gelu_parts(v):
    c = math.sqrt(2.0 / math.pi)
    v2 = v * v
    th = jnp.tanh(c * v * (1.0 + 0.044715 * v2))
    act = 0.5 * v * (1.0 + th)
    slope = 0.5 * (1.0 + th) + (0.5 * c) * v * (1.0 - th * th) * (1.0 + 3.0 * 0.044715 * v2)
    return act, slope


def per_device(ndp, nz, *args):
    (
        frames,
        skip_in,
        flow_time,
        segment_ids,
        w_skip,
        b_skip,
        w_mod,
        b_mod,
        w_q,
        w_k,
        w_v,
        w_o,
        w_up,
        b_up,
        w_dn,
        b_dn,
        out_grad,
    ) = args
    t, d = frames.shape
    loc = w_q.shape[1]
    fl = w_up.shape[1]
    dp = lax.axis_index("dp")
    z = lax.axis_index("tensor")
    p = dp % GROUP

    def piece(w):
        r = w.shape[0] // GROUP
        return lax.dynamic_slice_in_dim(w, p * r, r, 0).astype(F32)

    embed = time_embed(flow_time, d)
    mod_part = dot(embed, w_mod)[0] + b_mod
    own_small = jnp.concatenate([mod_part, b_skip, b_up])[None, :]
    wskip, wqkv, wo, wup, wdn, small = gather(
        piece(w_skip),
        jnp.stack([piece(w_q), piece(w_k), piece(w_v)]),
        piece(w_o),
        piece(w_up),
        piece(w_dn),
        w_skip.astype(F32),
        own_small,
        nz,
    )
    small = small[:, 0]
    nm = mod_part.shape[0]
    mod = small[:, :nm].reshape(6, d)
    shift1, scale1, gate1, shift2, scale2, gate2 = [mod[i][None, :] for i in range(6)]
    bskip = small[:, nm : nm + loc].reshape(1, d)
    bup = [
        lax.dynamic_index_in_dim(small[:, nm + loc :], (z + k) % nz, 0, keepdims=True)
        for k in range(nz)
    ]
    up = [w_up] + [wup[k].astype(BF16) for k in range(nz - 1)]
    dn = [w_dn] + [wdn[k].astype(BF16) for k in range(nz - 1)]
    wo_all = [w_o] + [wo[k].astype(BF16) for k in range(nz - 1)]

    def own_cols(a):
        return lax.dynamic_slice_in_dim(a, z * loc, loc, a.ndim - 1)

    seg = segment_ids[0]
    idx = jnp.arange(t, dtype=jnp.int32)
    nseg = 4
    starts = jnp.stack([jnp.sum((seg < s).astype(jnp.int32)) for s in range(nseg + 1)])
    first = jnp.zeros_like(seg)
    for s in range(1, nseg):
        first = jnp.where(seg >= s, starts[s], first)
    pos = (idx - first).astype(F32)
    half = HEAD_DIM // 2
    inv = jnp.exp(-math.log(10000.0) * 2.0 * jnp.arange(half, dtype=F32) / HEAD_DIM)
    ang = pos[:, None] * inv[None, :]
    cos_h, sin_h = jnp.cos(ang), jnp.sin(ang)
    cos = jnp.tile(cos_h, (1, loc // half))
    sin = jnp.tile(jnp.concatenate([-sin_h, sin_h], axis=1), (1, loc // HEAD_DIM))
    qb_first, qb_last = seg[::QB], seg[QB - 1 :: QB]
    lo = jnp.take(starts, qb_first) // KB
    hi = (jnp.take(starts, qb_last + 1) + KB - 1) // KB
    seg_row = jnp.broadcast_to(seg[None, None, :], (1, 8, t))
    seg_col = jnp.broadcast_to(seg[:, None], (t, 128))

    hidden = (
        dot(frames, wskip[:d].astype(BF16)) + dot(skip_in, wskip[d:].astype(BF16)) + bskip
    )
    x1, r1 = stats(hidden)
    normed = (x1 * (1.0 + scale1) + shift1).astype(BF16)
    q, k, v = qkv(normed, w_q, w_k, w_v, wqkv, cos, sin)
    att, lse = attn_fwd(q, k, v, seg_row, seg_col, lo, hi, nz)
    branch = sum(dot(att[:, i * loc : (i + 1) * loc], wo_all[i]) for i in range(nz))
    mid = hidden + gate1 * branch
    x2, r2 = stats(mid)
    normed2 = (x2 * (1.0 + scale2) + shift2).astype(BF16)
    g_out = out_grad.astype(F32)
    g_ffn = (gate2 * g_out).astype(BF16)
    ffn_own = own_cols(b_dn)[None, :]
    g_normed2 = 0.0
    for i in range(nz):
        pre = dot(normed2, up[i]) + bup[i]
        act, slope = gelu_parts(pre)
        act = act.astype(BF16)
        ffn_own = ffn_own + dot(act, own_cols(dn[i]))
        g_pre = (dot(g_ffn, dn[i], NT) * slope).astype(BF16)
        g_normed2 = g_normed2 + dot(g_pre, up[i], NT)
        if i == 0:
            act_own, g_pre_own = act, g_pre
    output = own_cols(mid) + own_cols(gate2) * ffn_own
    g_gate2_own = jnp.sum(own_cols(g_out) * ffn_own, axis=0)
    g_b_dn = gate2[0] * jnp.sum(g_out, axis=0)
    tn = (((0,), (0,)), ((), ()))
    g_w_up = dot(normed2, g_pre_own, tn)
    g_w_dn_t = dot(g_ffn, act_own, tn)
    g_b_up = jnp.sum(g_pre_own.astype(F32), axis=0)

    g_shift2 = jnp.sum(g_normed2, axis=0)
    g_scale2 = jnp.sum(g_normed2 * x2, axis=0)
    g_mid = g_out + norm_pull(x2, r2, scale2, g_normed2)
    g_gate1 = jnp.sum(g_mid * branch, axis=0)
    g_branch = (gate1 * g_mid).astype(BF16)
    g_w_o_t = dot(g_branch, att[:, :loc], tn)
    first_sum = jnp.concatenate([g_w_up, g_w_dn_t, g_w_o_t], axis=1)
    first_sum = lax.psum_scatter(first_sum, "dp", scatter_dimension=0, tiled=True)
    g_att = jnp.concatenate(
        [dot(g_branch, wo_all[i], NT).astype(BF16) for i in range(nz)], axis=1
    )
    gq, gk, gv = attn_bwd(q, k, v, att, g_att, lse, seg_row, seg_col, lo, hi, cos, sin, nz)
    g_normed = gnormed(gq, gk, gv, w_q, w_k, w_v, wqkv)
    g_qkv = jnp.concatenate([gq[:, :loc], gk[:, :loc], gv[:, :loc]], axis=1)
    g_w_qkv = dot(normed, g_qkv, tn)
    g_shift1 = jnp.sum(g_normed, axis=0)
    g_scale1 = jnp.sum(g_normed * x1, axis=0)
    g_hidden = g_mid + norm_pull(x1, r1, scale1, g_normed)
    g_low = g_hidden.astype(BF16)
    own_low = own_cols(g_low)
    g_b_skip = jnp.sum(own_cols(g_hidden), axis=0)
    g_w_skip = jnp.concatenate([dot(frames, own_low, tn), dot(skip_in, own_low, tn)], axis=0)

    def rows_of(base):
        return lax.dynamic_slice_in_dim(wskip, base + z * loc, loc, 0).astype(BF16)

    grad_frames = dot(g_low, rows_of(0), NT)
    grad_skip = dot(g_low, rows_of(d), NT)

    g_mod = jnp.concatenate(
        [g_shift1, g_scale1, g_gate1, g_shift2, g_scale2, jnp.zeros((d,), F32)]
    )
    own_mod = lax.dynamic_slice_in_dim(g_mod, z * nm, nm, 0)
    sizes = [nm, loc, fl, d, 128]
    offs = [sum(sizes[:i]) for i in range(len(sizes) + 1)]
    vec = jnp.concatenate(
        [own_mod, g_b_skip, g_b_up, g_b_dn, jnp.broadcast_to(flow_time, (128,))]
    )[None, :]
    s_qkv, s_w_skip, vecs, gates = reduce_over_dp(
        [g_w_qkv.reshape(ndp, d // ndp, 3 * loc), g_w_skip.reshape(ndp, 2 * d // ndp, loc)],
        vec,
        g_gate2_own[None, :],
        ndp,
        nz,
        1,
    )
    vecs = vecs[:, 0]
    gate_all = gates.reshape(ndp, d)
    pad = jnp.concatenate([jnp.zeros((ndp, 5 * d), F32), gate_all], axis=1)
    mod_rows = vecs[:, :nm] + lax.dynamic_slice_in_dim(pad, z * nm, nm, 1)

    def share(i, of):
        n = sizes[i] // ndp
        cols = lax.dynamic_slice_in_dim(of, offs[i] + dp * n, n, 1)
        return jnp.sum(cols, axis=0)

    def mine(v):
        n = v.shape[1] // ndp
        return jnp.sum(lax.dynamic_slice_in_dim(v, dp * n, n, 1), axis=0)

    s_b_mod = mine(mod_rows)
    embeds = time_embed(vecs[:, offs[4]], d)
    rows = d // ndp
    s_w_mod = dot(lax.dynamic_slice_in_dim(embeds, dp * rows, rows, 1), mod_rows.astype(BF16), tn)
    s_up = first_sum[:, :fl]
    s_dn = first_sum[:, fl : 2 * fl].T
    s_o = first_sum[:, 2 * fl :].T
    return (
        output,
        grad_frames,
        grad_skip,
        s_w_skip,
        share(1, vecs),
        s_w_mod,
        s_b_mod,
        s_qkv[:, :loc],
        s_qkv[:, loc : 2 * loc],
        s_qkv[:, 2 * loc :],
        s_o,
        s_up,
        share(2, vecs),
        s_dn,
        share(3, vecs),
    )


def solution(mesh):
    in_specs = (
        P("dp", None),
        P("dp", None),
        P("dp"),
        P("dp", None),
        P(None, "tensor"),
        P("tensor"),
        P(None, "tensor"),
        P("tensor"),
        P(None, "tensor"),
        P(None, "tensor"),
        P(None, "tensor"),
        P("tensor", None),
        P(None, "tensor"),
        P("tensor"),
        P("tensor", None),
        P(),
        P("dp", None),
    )
    out_specs = (
        P("dp", "tensor"),
        P("dp", "tensor"),
        P("dp", "tensor"),
        P("dp", "tensor"),
        P(("tensor", "dp")),
        P("dp", "tensor"),
        P(("tensor", "dp")),
        P("dp", "tensor"),
        P("dp", "tensor"),
        P("dp", "tensor"),
        P("tensor", "dp"),
        P("dp", "tensor"),
        P(("tensor", "dp")),
        P("tensor", "dp"),
        P("dp"),
    )
    return jax.shard_map(
        functools.partial(per_device, mesh.shape["dp"], mesh.shape["tensor"]),
        mesh=mesh,
        in_specs=in_specs,
        out_specs=out_specs,
        check_vma=False,
    )
```

```python
import functools
import math

import jax
import jax.numpy as jnp
from jax import lax
from jax.experimental import pallas as pl
from jax.experimental.pallas import tpu as pltpu
from jax.sharding import PartitionSpec as P

HEAD_DIM = 64
EPS = 1e-06
F32 = jnp.float32
BF16 = jnp.bfloat16
MESH = pl.DeviceIdType.MESH
ANY = pl.BlockSpec(memory_space=pl.ANY)
VMEM = pl.BlockSpec(memory_space=pltpu.VMEM)
GROUP = 8
NT = (((1,), (1,)), ((), ()))
NN = (((1,), (0,)), ((), ()))


def dot(a, b, dims=NN, precision=None):
    return lax.dot_general(a, b, dims, precision=precision, preferred_element_type=F32)


def remote(src, dst, send, recv, device):
    return pltpu.make_async_remote_copy(
        src_ref=src,
        dst_ref=dst,
        send_sem=send,
        recv_sem=recv,
        device_id=device,
        device_id_type=MESH,
    )


class Spread:
    def __init__(self, nz, n, src, view, sems, lags):
        self.nz, self.n, self.src, self.view, self.lags = nz, n, src, view, lags
        self.zs, self.zr, self.ps, self.pr = sems
        dp = lax.axis_index("dp")
        z = lax.axis_index("tensor")
        self.z = z
        p = lax.rem(dp, GROUP)
        self.p = p
        core = lax.rem(dp, 2)
        ds_ = 1 - 2 * core
        dx = 2 - 4 * lax.rem(dp // 2, 2)
        dy = 4 - 8 * lax.rem(dp // 4, 2)
        d1 = dy + core * (dx - dy)
        d2 = dx + core * (dy - dx)
        self.near = {1: (dp + d1, z), 2: (dp + d2, z), 3: (dp + ds_, z)}
        self.far = {k: (dp, lax.rem(z + nz - k, nz)) for k in range(1, nz)}
        self.stages = {
            1: ([p], d1, 0),
            2: ([p, p + d1], d2, 1),
            3: ([p, p + d1, p + d2, p + d1 + d2], ds_, 3),
        }
        self.t = 0
        self.ready = -1

    def barrier(self):
        bar = pltpu.get_barrier_semaphore()
        devices = list(self.near.values()) + list(self.far.values())
        for device in devices:
            pl.semaphore_signal(bar, inc=1, device_id=device, device_id_type=MESH)
        pl.semaphore_wait(bar, len(devices))

    def _far(self, i, k, zz):
        return remote(
            self.src(i),
            self.view(i, k, self.p, zz),
            self.zs.at[i, k - 1],
            self.zr.at[i, k - 1],
            self.far[k],
        )

    def _near(self, i, stage, inward):
        qs, shift, base = self.stages[stage]
        kk = self.nz - 1
        out = []
        for j, q in enumerate(qs):
            if inward:
                q = q + shift
            for k in range(1, self.nz):
                ref = self.view(i, k, q, lax.rem(self.z + k, self.nz))
                s = (base + j) * kk + k - 1
                out.append(
                    functools.partial(
                        remote, ref, ref, self.ps.at[i, s], self.pr.at[i, s], self.near[stage]
                    )
                )
        return out

    def tick(self):
        t, n = self.t, self.n
        l1, l2, l3, l4 = self.lags
        if t < n:
            for k in range(1, self.nz):
                self._far(t, k, self.z).start()
        if 0 <= t - l4 < n:
            for c in self._near(t - l4, 3, True):
                c().wait_recv()
            self.ready = t - l4
        for stage, lag in ((3, l3), (2, l2)):
            if 0 <= t - lag < n:
                for c in self._near(t - lag, stage - 1, True):
                    c().wait_recv()
                for c in self._near(t - lag, stage, False):
                    c().start()
        if 0 <= t - l1 < n:
            for k in range(1, self.nz):
                self._far(t - l1, k, lax.rem(self.z + k, self.nz)).wait_recv()
            for c in self._near(t - l1, 1, False):
                c().start()
        self.t += 1

    def until(self, i):
        while self.ready < i:
            self.tick()

    def drain(self):
        for i in range(self.n):
            for k in range(1, self.nz):
                self._far(i, k, self.z).wait_send()
            for stage in (1, 2, 3):
                for c in self._near(i, stage, False):
                    c().wait_send()


def spread_sems(nz, n):
    dma = pltpu.SemaphoreType.DMA
    kk = nz - 1
    return [dma((n, kk)), dma((n, kk)), dma((n, 7 * kk)), dma((n, 7 * kk))]


def layer_norm(v):
    centred = v - jnp.mean(v, axis=-1, keepdims=True)
    r = lax.rsqrt(jnp.mean(centred * centred, axis=-1, keepdims=True) + EPS)
    return centred * r, r


TB = 512
LB = 128


def first_kernel(nz, chunks, *refs):
    (x_ref, y_ref, wskip_ref, wq_ref, wk_ref, wv_ref, wo_ref, vec_ref, cos_ref, sin_ref) = refs[:10]
    (hid_ref, norm_ref, q_ref, k_ref, v_ref, lskip, lqkv, lo_, small_ref) = refs[10:19]
    (pskip, pqkv, po, fskip, sskip, sqkv, wb, loc_sem, st_sem, vs, vr) = refs[19:30]
    sems = refs[30:34]
    t, d = x_ref.shape
    loc = wq_ref.shape[1]
    own = {"skip": wskip_ref, "qkv": (wq_ref, wk_ref, wv_ref), "o": wo_ref}
    rs, rq, ro = pskip.shape[0], pqkv.shape[1], po.shape[0]

    def src(i):
        name, a, off, r = chunks[i]
        if name == "skip":
            return pskip.at[pl.ds(off, r)]
        if name == "qkv":
            return pqkv.at[a, pl.ds(off, r)]
        return po.at[pl.ds(off, r)]

    def view(i, k, q, zz):
        name, a, off, r = chunks[i]
        if name == "skip":
            return lskip.at[pl.ds(q * rs + off, r), pl.ds(pl.multiple_of(zz * loc, loc), loc)]
        if name == "qkv":
            return lqkv.at[k - 1, a, pl.ds(q * rq + off, r)]
        return lo_.at[k - 1, pl.ds(q * ro + off, r)]

    net = Spread(nz, len(chunks), src, view, sems, (1, 2, 3, 4))
    z, p = net.z, net.p
    pskip[...] = wskip_ref[pl.ds(pl.multiple_of(p * rs, rs), rs), :].astype(F32)
    net.barrier()

    def vec(k, zz):
        return remote(vec_ref, small_ref.at[zz], vs.at[k - 1], vr.at[k - 1], net.far[k])

    for k in range(1, nz):
        vec(k, z).start()
    net.tick()
    for a, w in enumerate((wq_ref, wk_ref, wv_ref)):
        pqkv[a] = w[pl.ds(pl.multiple_of(p * rq, rq), rq), :].astype(F32)
    po[...] = wo_ref[pl.ds(pl.multiple_of(p * ro, ro), ro), :].astype(F32)
    net.tick()
    small_ref[z] = vec_ref[...]
    fskip[...] = wskip_ref[...].astype(F32)

    def cols(zz):
        return pl.ds(pl.multiple_of(zz * loc, loc), loc)

    keep = lambda: pltpu.make_async_copy(fskip, lskip.at[:, cols(z)], loc_sem.at[0])
    keep().start()
    for k in range(1, nz):
        vec(k, lax.rem(z + k, nz)).wait_recv()
    nm = 6 * d // nz

    def flat(lo, hi):
        parts = []
        while lo < hi:
            zz = lo // nm
            end = min(hi, (zz + 1) * nm)
            parts.append(small_ref[zz, :, lo - zz * nm : end - zz * nm])
            lo = end
        return jnp.concatenate(parts, axis=1)

    def hidden_cols(w, zz):
        bias = small_ref[zz, :, nm : nm + loc]

        @pl.loop(0, t // TB)
        def _(b):
            rows = pl.ds(pl.multiple_of(b * TB, TB), TB)
            acc = dot(x_ref[rows, :], w[:d, :]) + dot(y_ref[rows, :], w[d:, :])
            hid_ref[rows, cols(zz)] = acc + bias

    hidden_cols(wskip_ref, z)
    nskip = sum(c[0] == "skip" for c in chunks)
    net.until(nskip - 1)
    stage = lambda k: pltpu.make_async_copy(
        lskip.at[:, cols(lax.rem(z + k, nz))], sskip.at[k - 1], st_sem.at[k - 1]
    )
    for k in range(1, nz):
        stage(k).start()
    for k in range(1, nz):
        stage(k).wait()
        wb[...] = sskip[k - 1].astype(BF16)
        hidden_cols(wb, lax.rem(z + k, nz))
        net.tick()
    shift1, scale1 = flat(0, d), flat(d, 2 * d)

    @pl.loop(0, t // LB)
    def _(b):
        rows = pl.ds(pl.multiple_of(b * LB, LB), LB)
        xn, _ = layer_norm(hid_ref[rows, :])
        norm_ref[rows, :] = (xn * (1.0 + scale1) + shift1).astype(BF16)

    net.tick()

    def project(a, k, w):
        out = (q_ref, k_ref, v_ref)[a]

        @pl.loop(0, t // TB)
        def _(b):
            rows = pl.ds(pl.multiple_of(b * TB, TB), TB)
            u = dot(norm_ref[rows, :], w[...])
            if a < 2:
                u = u * cos_ref[rows, :] + swap_halves(u) * sin_ref[rows, :]
            if a == 0:
                u = u.astype(BF16).astype(F32) * (HEAD_DIM**-0.5)
            out[rows, k * loc : (k + 1) * loc] = u.astype(BF16)

    for a in range(3):
        project(a, 0, (wq_ref, wk_ref, wv_ref)[a])
    nq = sum(c[0] == "qkv" for c in chunks) // 3
    bring = lambda a: pltpu.make_async_copy(lqkv.at[:, a], sqkv.at[a % 2], st_sem.at[a % 2])
    for a in range(3):
        net.until(nskip + nq * (a + 1) - 1)
        bring(a).start()
        bring(a).wait()
        for k in range(1, nz):
            wb[:d, :] = sqkv[a % 2, k - 1].astype(BF16)
            project(a, k, wb.at[:d, :])
            if a < 2:
                net.tick()
    net.until(len(chunks) - 1)
    net.drain()
    for k in range(1, nz):
        vec(k, z).wait_send()
    keep().wait()


def first(x, y, wskip, wq, wk, wv, wo, vec, cos, sin, nz):
    t, d = x.shape
    loc = wq.shape[1]
    chunks = []
    rs, rq, ro = 2 * d // GROUP, d // GROUP, loc // GROUP
    for j in range(4):
        chunks.append(("skip", 0, j * rs // 4, rs // 4))
    for a in range(3):
        for j in range(2):
            chunks.append(("qkv", a, j * rq // 2, rq // 2))
    for j in range(2):
        chunks.append(("o", 0, j * ro // 2, ro // 2))
    sd = jax.ShapeDtypeStruct
    kk = nz - 1
    dma = pltpu.SemaphoreType.DMA
    outs = [
        sd((t, d), F32),
        sd((t, d), BF16),
        sd((t, nz * loc), BF16),
        sd((t, nz * loc), BF16),
        sd((t, nz * loc), BF16),
        sd((2 * d, nz * loc), F32),
        sd((kk, 3, d, loc), F32),
        sd((kk, loc, d), F32),
        sd((nz,) + vec.shape, F32),
    ]
    scratch = [
        pltpu.VMEM((rs, loc), F32),
        pltpu.VMEM((3, rq, loc), F32),
        pltpu.VMEM((ro, d), F32),
        pltpu.VMEM((2 * d, loc), F32),
        pltpu.VMEM((kk, 2 * d, loc), F32),
        pltpu.VMEM((2, kk, d, loc), F32),
        pltpu.VMEM((2 * d, loc), BF16),
        dma((1,)),
        dma((max(kk, 2),)),
        dma((kk,)),
        dma((kk,)),
    ] + spread_sems(nz, len(chunks))
    return pl.pallas_call(
        functools.partial(first_kernel, nz, chunks),
        out_shape=outs,
        in_specs=[VMEM] * 10,
        out_specs=[VMEM] * 5 + [ANY] * 3 + [VMEM],
        scratch_shapes=scratch,
        compiler_params=pltpu.CompilerParams(
            collective_id=0, has_side_effects=True, vmem_limit_bytes=60 << 20
        ),
    )(x, y, wskip, wq, wk, wv, wo, vec, cos, sin)


def gelu_parts(v):
    c = math.sqrt(2.0 / math.pi)
    v2 = v * v
    th = jnp.tanh(c * v * (1.0 + 0.044715 * v2))
    half = 0.5 * (1.0 + th)
    act = v * half
    slope = half + (0.5 * c) * v * (1.0 - th * th) * (1.0 + 3.0 * 0.044715 * v2)
    return act, slope


TN = (((0,), (0,)), ((), ()))


def second_kernel(nz, n, r, per, *refs):
    (att_ref, hid_ref, go_ref, woo_ref, wo_ref, up_ref, dn_ref, mod_ref, bup_ref, bupr_ref, bdn_ref) = refs[:11]
    (out_ref, gm_ref, gb_ref, ga_ref, gw_ref, sums_ref, gbu_ref, gg2_ref, land) = refs[11:20]
    (pc, wob, br_ref, n2_ref, gf_ref, stg, ub, db, act_s, gp_s, gws, st_sem, gw_sem) = refs[20:33]
    sems = refs[33:37]
    t, d = hid_ref.shape
    loc = woo_ref.shape[0]
    fl = up_ref.shape[1]
    kk = nz - 1
    pr = fl // GROUP
    net = Spread(
        nz,
        n,
        lambda i: pc.at[:, pl.ds(i * r, r)],
        lambda i, k, q, zz: land.at[i, :, k - 1, q],
        sems,
        (1, 2, 3, 4),
    )
    z, p = net.z, net.p
    own = pl.ds(pl.multiple_of(z * loc, loc), loc)
    pc[0] = up_ref[:, pl.ds(pl.multiple_of(p * pr, pr), pr)].astype(F32).T
    pc[1] = dn_ref[pl.ds(pl.multiple_of(p * pr, pr), pr), :].astype(F32)
    net.barrier()
    net.tick()
    row = lambda i: mod_ref[i : i + 1, :]
    gate1, shift2, scale2, gate2 = row(2), row(3), row(4), row(5)
    for k in range(1, nz):
        wob[k] = wo_ref[k - 1].astype(BF16)
    wob[0] = woo_ref[...]
    net.tick()

    @pl.loop(0, t // TB)
    def _(b):
        rows = pl.ds(pl.multiple_of(b * TB, TB), TB)
        br_ref[rows, :] = dot(att_ref[rows, :], wob[...].reshape(nz * loc, d))

    net.tick()
    sums_ref[...] = jnp.zeros_like(sums_ref)

    @pl.loop(0, t // LB)
    def _(b):
        rows = pl.ds(pl.multiple_of(b * LB, LB), LB)
        x2, _ = layer_norm(hid_ref[rows, :] + gate1 * br_ref[rows, :])
        n2_ref[rows, :] = (x2 * (1.0 + scale2) + shift2).astype(BF16)
        go = go_ref[rows, :].astype(F32)
        sums_ref[3:4, :] += jnp.sum(go, axis=0, keepdims=True)
        gf_ref[rows, :] = (gate2 * go).astype(BF16)

    def units(first_time, rows, pre, dnv, uv_g):
        act, slope = gelu_parts(pre)
        actl = act.astype(BF16)
        ffn = dot(actl, dnv[:, own])
        g_pre = (dot(gf_ref[rows, :], dnv[...], NT) * slope).astype(BF16)
        gn = uv_g(g_pre)
        if first_time:
            out_ref[rows, :] = ffn
            gm_ref[rows, :] = gn
        else:
            out_ref[rows, :] += ffn
            gm_ref[rows, :] += gn
        return actl, g_pre

    sub = fl // 4
    gwc = lambda j, s: pltpu.make_async_copy(
        gws.at[s], gw_ref.at[pl.ds(s * fl + j * sub, sub)], gw_sem.at[s]
    )
    for j in range(4):
        net.tick()
        cs = slice(j * sub, (j + 1) * sub)

        @pl.loop(0, t // TB)
        def _(b):
            rows = pl.ds(pl.multiple_of(b * TB, TB), TB)
            pre = dot(n2_ref[rows, :], up_ref[:, cs]) + bup_ref[:, cs]
            a, g = units(
                j == 0, rows, pre, dn_ref.at[cs, :], lambda gp: dot(gp, up_ref[:, cs], NT)
            )
            act_s[rows, :] = a
            gp_s[rows, :] = g

        if j > 0:
            for s in range(2):
                gwc(j - 1, s).wait()
        gbu_ref[:, cs] = jnp.sum(gp_s[...].astype(F32), axis=0, keepdims=True)
        gws[0] = dot(gp_s[...], n2_ref[...], TN)
        gws[1] = dot(act_s[...], gf_ref[...], TN)
        for s in range(2):
            gwc(j, s).start()
    for s in range(2):
        gwc(3, s).wait()

    nu = per * kk * GROUP * r
    steps = n // per

    def fetch(m):
        return pltpu.make_async_copy(
            land.at[pl.ds(m * per, per)], stg.at[m % 2], st_sem.at[m % 2]
        )

    for m in range(steps):
        net.until(m * per + per - 1)
        fetch(m).start()
        if m + 1 < steps:
            net.tick()
        fetch(m).wait()
        for c in range(per):
            w = nu // per
            ub[c * w : (c + 1) * w, :] = stg[m % 2, c, 0].reshape(w, d).astype(BF16)
            db[c * w : (c + 1) * w, :] = stg[m % 2, c, 1].reshape(w, d).astype(BF16)

        @pl.loop(0, t // TB)
        def _(b):
            rows = pl.ds(pl.multiple_of(b * TB, TB), TB)
            pre = dot(n2_ref[rows, :], ub[...], NT) + bupr_ref[m]
            units(False, rows, pre, db, lambda gp: dot(gp, ub[...]))

    net.drain()
    bdn = bdn_ref[:, own]
    gate2_own = mod_ref[5:6, own]
    gate1_own = mod_ref[2:3, own]

    @pl.loop(0, t // LB)
    def _(b):
        rows = pl.ds(pl.multiple_of(b * LB, LB), LB)
        ffn = out_ref[rows, :] + bdn
        go_own = go_ref[rows, own].astype(F32)
        gg2 = jnp.sum(go_own * ffn, axis=0, keepdims=True)

        @pl.when(b == 0)
        def _():
            gg2_ref[...] = gg2

        @pl.when(b > 0)
        def _():
            gg2_ref[...] += gg2

        out_ref[rows, :] = hid_ref[rows, own] + gate1_own * br_ref[rows, own] + gate2_own * ffn
        br = br_ref[rows, :]
        x2, r2 = layer_norm(hid_ref[rows, :] + gate1 * br)
        gn = gm_ref[rows, :]
        sums_ref[0:1, :] += jnp.sum(gn, axis=0, keepdims=True)
        sums_ref[1:2, :] += jnp.sum(gn * x2, axis=0, keepdims=True)
        gp = gn * (1.0 + scale2)
        gm = go_ref[rows, :].astype(F32) + r2 * (
            gp
            - jnp.mean(gp, axis=-1, keepdims=True)
            - x2 * jnp.mean(gp * x2, axis=-1, keepdims=True)
        )
        gm_ref[rows, :] = gm
        sums_ref[2:3, :] += jnp.sum(gm * br, axis=0, keepdims=True)
        gb_ref[rows, :] = (gate1 * gm).astype(BF16)

    @pl.loop(0, t // TB)
    def _(b):
        rows = pl.ds(pl.multiple_of(b * TB, TB), TB)
        ga_ref[rows, :] = dot(gb_ref[rows, :], wob[...].reshape(nz * loc, d), NT).astype(BF16)

    gws[0, :loc, :] = dot(att_ref[:, :loc], gb_ref[...], TN)
    last = pltpu.make_async_copy(gws.at[0, :loc], gw_ref.at[pl.ds(2 * fl, loc)], gw_sem.at[0])
    last.start()
    last.wait()


def second(att, hid, go, wo_own, wo, up, dn, mod, bup_own, bup_rest, bdn, nz, r=8, per=2):
    t, d = hid.shape
    loc = wo_own.shape[0]
    fl = up.shape[1]
    kk = nz - 1
    n = fl // GROUP // r
    nu = per * kk * GROUP * r
    sd = jax.ShapeDtypeStruct
    dma = pltpu.SemaphoreType.DMA
    outs = [
        sd((t, loc), F32),
        sd((t, d), F32),
        sd((t, d), BF16),
        sd((t, nz * loc), BF16),
        sd((2 * fl + loc, d), F32),
        sd((8, d), F32),
        sd((1, fl), F32),
        sd((1, loc), F32),
        sd((n, 2, kk, GROUP, r, d), F32),
    ]
    scratch = [
        pltpu.VMEM((2, fl // GROUP, d), F32),
        pltpu.VMEM((nz, loc, d), BF16),
        pltpu.VMEM((t, d), F32),
        pltpu.VMEM((t, d), BF16),
        pltpu.VMEM((t, d), BF16),
        pltpu.VMEM((2, per, 2, kk, GROUP, r, d), F32),
        pltpu.VMEM((nu, d), BF16),
        pltpu.VMEM((nu, d), BF16),
        pltpu.VMEM((t, fl // 4), BF16),
        pltpu.VMEM((t, fl // 4), BF16),
        pltpu.VMEM((2, max(fl // 4, loc), d), F32),
        dma((2,)),
        dma((2,)),
    ] + spread_sems(nz, n)
    b = bup_rest.reshape(kk, GROUP, n // per, per, r).transpose(2, 3, 0, 1, 4)
    b = b.reshape(n // per, 1, nu)
    return pl.pallas_call(
        functools.partial(second_kernel, nz, n, r, per),
        out_shape=outs,
        in_specs=[VMEM] * 11,
        out_specs=[VMEM] * 4 + [ANY] + [VMEM] * 3 + [ANY],
        scratch_shapes=scratch,
        compiler_params=pltpu.CompilerParams(
            collective_id=2, has_side_effects=True, vmem_limit_bytes=62 << 20
        ),
    )(att, hid, go, wo_own, wo, up, dn, mod, bup_own, b, bdn)


def reduce_kernel(ndp, nz, na, *refs):
    bits = ndp.bit_length() - 1
    ins = refs[:na]
    small, part = refs[na : na + 2]
    outs = refs[na + 2 : 2 * na + 2]
    all_small, all_part = refs[2 * na + 2 : 2 * na + 4]
    rest = refs[2 * na + 4 :]
    recv0, lev0 = rest[:na], rest[na : 2 * na]
    half_refs = rest[2 * na : -8]
    gz, s_send, s_recv, q_send, q_recv, z_send, z_recv, l_sem = rest[-8:]
    dp = lax.axis_index("dp")
    z = lax.axis_index("tensor")
    mine = [lax.rem(dp // (1 << b), 2) for b in range(bits)]
    partner = [(dp + (1 << b) * (1 - 2 * mine[b]), z) for b in range(bits)]
    bar = pltpu.get_barrier_semaphore()

    def others(j):
        return lax.rem(dp + j, ndp)

    for j in range(1, ndp):
        pl.semaphore_signal(bar, inc=1, device_id=(others(j), z), device_id_type=MESH)
    for k in range(1, nz):
        pl.semaphore_signal(bar, inc=1, device_id=(dp, lax.rem(z + k, nz)), device_id_type=MESH)
    pl.semaphore_wait(bar, ndp - 1 + nz - 1)

    def gzc(k, zz):
        return remote(part, gz.at[zz], z_send.at[k - 1], z_recv.at[k - 1], (dp, lax.rem(z + nz - k, nz)))

    for k in range(1, nz):
        gzc(k, z).start()

    def first(a, i):
        s = 2 * i + 1 - mine[0]
        return remote(ins[a].at[s], recv0[a].at[i], s_send.at[a, i], s_recv.at[a, i], partner[0])

    for a in range(na):
        for i in range(ndp // 2):
            first(a, i).start()
    gz[z] = part[...]

    def sml(j, row):
        return remote(small, all_small.at[row], q_send.at[0, j - 1], q_recv.at[0, j - 1], (others(j), z))

    def prt(j, row):
        return remote(gz, all_part.at[row], q_send.at[1, j - 1], q_recv.at[1, j - 1], (others(j), z))

    own = [
        lambda: pltpu.make_async_copy(small, all_small.at[dp], l_sem.at[0]),
        lambda: pltpu.make_async_copy(gz, all_part.at[dp], l_sem.at[1]),
    ]
    for j in range(1, ndp):
        sml(j, dp).start()
    own[0]().start()
    for k in range(1, nz):
        gzc(k, lax.rem(z + k, nz)).wait_recv()
    for j in range(1, ndp):
        prt(j, dp).start()
    own[1]().start()
    for a in range(na):
        for i in range(ndp // 2):
            first(a, i).wait_recv()
            lev0[a][i] = ins[a][2 * i + mine[0]] + recv0[a][i]
    orders = [list(range(1, bits)), list(range(bits - 1, 0, -1))]
    state = {}
    pos = 0
    for a in range(na):
        for h in range(2):
            cw = ins[a].shape[2] // 2
            state[a, h] = (lev0[a].at[:, :, pl.ds(h * cw, cw)], list(range(1, bits)))
    pending = []
    for step in range(bits - 1):
        todo = []
        for a in range(na):
            for h in range(2):
                src, free = state[a, h]
                b = orders[h][step]
                at = free.index(b)
                lo = 1 << at
                left = [f for f in free if f != b]
                cnt = 1 << len(left)
                recv, out = half_refs[pos], half_refs[pos + 1]
                sem_s, sem_r = half_refs[pos + 2], half_refs[pos + 3]
                pos += 4
                items = []
                for i in range(cnt):
                    base = (i // lo) * 2 * lo + i % lo
                    keep = base + lo * mine[b]
                    give = base + lo * (1 - mine[b])
                    c = functools.partial(
                        remote, src.at[give], recv.at[i], sem_s.at[i], sem_r.at[i], partner[b]
                    )
                    c().start()
                    items.append((c, keep, i))
                todo.append((a, h, src, recv, out, items))
                state[a, h] = (out, left)
        for a, h, src, recv, out, items in todo:
            cw = ins[a].shape[2] // 2
            for c, keep, i in items:
                c().wait_recv()
                if step == bits - 2:
                    outs[a][:, pl.ds(h * cw, cw)] = src[keep] + recv[i]
                else:
                    out[i] = src[keep] + recv[i]
                pending.append(c)
    for c in pending:
        c().wait_send()
    for a in range(na):
        for i in range(ndp // 2):
            first(a, i).wait_send()
    for k in range(1, nz):
        gzc(k, z).wait_send()
    for j in range(1, ndp):
        sml(j, dp).wait_send()
        prt(j, dp).wait_send()
        row = lax.rem(dp + ndp - j, ndp)
        sml(j, row).wait_recv()
        prt(j, row).wait_recv()
    for c in own:
        c().wait()


def reduce_over_dp(arrays, small, part, ndp, nz, cid):
    na = len(arrays)
    bits = ndp.bit_length() - 1
    sd = jax.ShapeDtypeStruct
    dma = pltpu.SemaphoreType.DMA
    scratch = [pltpu.VMEM((ndp // 2,) + a.shape[1:], F32) for a in arrays] * 2
    for step in range(bits - 1):
        cnt = ndp >> (step + 2)
        for a in arrays:
            for h in range(2):
                shape = (cnt, a.shape[1], a.shape[2] // 2)
                scratch += [pltpu.VMEM(shape, F32), pltpu.VMEM(shape, F32), dma((cnt,)), dma((cnt,))]
    scratch += [
        pltpu.VMEM((nz,) + part.shape, F32),
        dma((na, ndp // 2)),
        dma((na, ndp // 2)),
        dma((2, ndp - 1)),
        dma((2, ndp - 1)),
        dma((nz - 1,)),
        dma((nz - 1,)),
        dma((2,)),
    ]
    return pl.pallas_call(
        functools.partial(reduce_kernel, ndp, nz, na),
        out_shape=[sd(a.shape[1:], F32) for a in arrays]
        + [sd((ndp,) + small.shape, F32), sd((ndp, nz) + part.shape, F32)],
        in_specs=[VMEM] * (na + 2),
        out_specs=[VMEM] * (na + 2),
        scratch_shapes=scratch,
        compiler_params=pltpu.CompilerParams(
            collective_id=cid, has_side_effects=True, vmem_limit_bytes=56 << 20
        ),
    )(*arrays, small, part)


def swap_halves(u):
    n = u.shape[1]
    lane = lax.broadcasted_iota(jnp.int32, u.shape, 1)
    half = HEAD_DIM // 2
    return jnp.where(
        lane % HEAD_DIM < half, pltpu.roll(u, n - half, 1), pltpu.roll(u, half, 1)
    )


QB = 256
KB = 256
NEG = -1e30


def stack_heads(dst, src, heads):
    lane = lax.broadcasted_iota(jnp.int32, src.shape, 1) // HEAD_DIM
    for h in range(heads):
        dst[:, h] = jnp.where(lane == h, src, jnp.zeros_like(src)).reshape(dst.shape[0], dst.shape[2], dst.shape[3])

def fwd_kernel(heads, QB, KB, lo_ref, hi_ref, q_ref, k_ref, v_ref, segq_ref, segk_ref, o_ref, lse_ref, vt_ref, ks_ref, s_ref):
    i = pl.program_id(1)
    @pl.when(i == 0)
    def _():
        vt_ref[...] = v_ref[...].T
        stack_heads(ks_ref, k_ref[...], heads)
    q = q_ref[...]
    segq = segq_ref[0, pl.ds(0, 1)]
    e = q.shape[1]
    lo, hi = lo_ref[i], hi_ref[i]
    def first(j, mx):
        start = pl.multiple_of(j*KB, KB)
        s = dot(ks_ref[j].reshape(heads*KB, e), q, NT)
        segk = segk_ref[pl.ds(start, KB), :]
        same = jnp.concatenate([segk]*(QB//128), axis=1) == segq
        out = []
        for h in range(heads):
            sh = jnp.where(same, s[h*KB:(h+1)*KB], NEG)
            s_ref[j, h] = sh
            out.append(jnp.maximum(mx[h], jnp.max(sh.reshape(KB//8, 8, QB), axis=0)))
        return out
    mx = lax.fori_loop(lo, hi, first, [jnp.full((8, QB), NEG, F32)]*heads)
    ms = [jnp.max(m, axis=0, keepdims=True) for m in mx]
    def second(j, carry):
        ls, os_ = carry
        start = pl.multiple_of(j*KB, KB)
        nl, no = [], []
        for h in range(heads):
            p = jnp.exp(s_ref[j, h] - ms[h])
            nl.append(ls[h] + jnp.sum(p.reshape(KB//8, 8, QB), axis=0))
            vt = vt_ref[pl.ds(h*HEAD_DIM, HEAD_DIM), pl.ds(start, KB)]
            no.append(os_[h] + dot(vt, p.astype(BF16)))
        return nl, no
    ls, os_ = lax.fori_loop(lo, hi, second, ([jnp.zeros((8, QB), F32)]*heads, [jnp.zeros((HEAD_DIM, QB), F32)]*heads))
    l1 = [jnp.sum(l, axis=0, keepdims=True) for l in ls]
    out = jnp.concatenate([os_[h] / l1[h] for h in range(heads)], axis=0)
    o_ref[...] = out.T.astype(BF16)
    lse = [ms[h] + jnp.log(l1[h]) for h in range(heads)]
    lse_ref[0] = jnp.concatenate(lse + [jnp.zeros((8 - heads, QB), F32)], axis=0)

def attn_fwd(q, k, v, seg_row, seg_col, lo, hi, groups, QB=QB, KB=KB):
    t = q.shape[0]; e = q.shape[1]//groups; heads = e//HEAD_DIM
    return pl.pallas_call(functools.partial(fwd_kernel, heads, QB, KB),
        out_shape=[jax.ShapeDtypeStruct(q.shape, BF16), jax.ShapeDtypeStruct((groups, 8, t), F32)],
        grid_spec=pltpu.PrefetchScalarGridSpec(num_scalar_prefetch=2, grid=(groups, t//QB),
            in_specs=[pl.BlockSpec((QB, e), lambda g,i,*_: (i, g)), pl.BlockSpec((t, e), lambda g,i,*_: (0, g)), pl.BlockSpec((t, e), lambda g,i,*_: (0, g)),
                      pl.BlockSpec((1, 8, QB), lambda g,i,*_: (0,0,i)), pl.BlockSpec((t,128), lambda g,i,*_: (0,0))],
            out_specs=[pl.BlockSpec((QB, e), lambda g,i,*_: (i, g)), pl.BlockSpec((1,8,QB), lambda g,i,*_: (g,0,i))],
            scratch_shapes=[pltpu.VMEM((e,t),BF16), pltpu.VMEM((t//KB, heads, KB, e), BF16), pltpu.VMEM((t//KB, heads, KB, QB), F32)]),
        compiler_params=pltpu.CompilerParams(vmem_limit_bytes=56<<20))(lo, hi, q, k, v, seg_row, seg_col)

def bwd_kernel(heads, QB, KB, lo_ref, hi_ref, q_ref, k_ref, v_ref, att_ref, g_ref, lse_ref, segq_ref, segk_ref, cos_ref, sin_ref, gq_ref, gk_ref, gv_ref,
               kt_ref, ks_ref, vs_ref, dk_ref, dv_ref):
    t, e = k_ref.shape
    kt_ref[...] = k_ref[...].T
    stack_heads(ks_ref, k_ref[...], heads)
    stack_heads(vs_ref, v_ref[...], heads)
    dk_ref[...] = jnp.zeros_like(dk_ref); dv_ref[...] = jnp.zeros_like(dv_ref)
    row = lax.broadcasted_iota(jnp.int32, (8, e), 0); lane = lax.broadcasted_iota(jnp.int32, (8, e), 1)
    ind = jnp.where(lane//HEAD_DIM == row, 1.0, 0.0).astype(F32)
    lanek = lax.broadcasted_iota(jnp.int32, (KB, e), 1)//HEAD_DIM
    @pl.loop(0, t//QB)
    def _(i):
        qs = pl.multiple_of(i*QB, QB)
        q = q_ref[pl.ds(qs, QB), :]; g = g_ref[pl.ds(qs, QB), :]
        segq = segq_ref[0, pl.ds(0,1), pl.ds(qs, QB)]
        prod = g.astype(F32)*att_ref[pl.ds(qs, QB), :].astype(F32)
        delta = dot(ind, prod, NT, lax.Precision.HIGHEST)
        lse = lse_ref[0, :, pl.ds(qs, QB)]
        def body(j, dq):
            start = pl.multiple_of(j*KB, KB)
            s = dot(ks_ref[j].reshape(heads*KB, e), q, NT)
            dpt = dot(vs_ref[j].reshape(heads*KB, e), g, NT)
            segk = segk_ref[pl.ds(start, KB), :]
            same = jnp.concatenate([segk]*(QB//128), axis=1) == segq
            ps, dss, ndq = [], [], []
            for h in range(heads):
                p = jnp.exp(jnp.where(same, s[h*KB:(h+1)*KB], NEG) - lse[h:h+1])
                ds = (p*(dpt[h*KB:(h+1)*KB] - delta[h:h+1])).astype(BF16)
                ps.append(p.astype(BF16)); dss.append(ds)
                kt = kt_ref[pl.ds(h*HEAD_DIM, HEAD_DIM), pl.ds(start, KB)]
                ndq.append(dq[h] + dot(kt, ds))
            dvs = dot(jnp.concatenate(ps, axis=0), g)
            dks = dot(jnp.concatenate(dss, axis=0), q)
            dv, dk = dvs[:KB], dks[:KB]
            for h in range(1, heads):
                dv = jnp.where(lanek == h, dvs[h*KB:(h+1)*KB], dv)
                dk = jnp.where(lanek == h, dks[h*KB:(h+1)*KB], dk)
            dk_ref[pl.ds(start, KB), :] += dk
            dv_ref[pl.ds(start, KB), :] += dv
            return ndq
        dq = lax.fori_loop(lo_ref[i], hi_ref[i], body, [jnp.zeros((HEAD_DIM, QB), F32)]*heads)
        dqf = jnp.concatenate(dq, axis=0).T * (HEAD_DIM**-0.5)
        cos = cos_ref[pl.ds(qs, QB), :]; sin = sin_ref[pl.ds(qs, QB), :]
        gq_ref[pl.ds(qs, QB), :] = (dqf*cos - swap_halves(dqf)*sin).astype(BF16)
    dk = dk_ref[...]
    gk_ref[...] = (dk*cos_ref[...] - swap_halves(dk)*sin_ref[...]).astype(BF16)
    gv_ref[...] = dv_ref[...].astype(BF16)

def attn_bwd(q,k,v,att,g,lse,seg_row,seg_col,lo,hi,cos,sin,groups,QB=QB,KB=KB):
    t = q.shape[0]; e = q.shape[1]//groups; heads = e//HEAD_DIM
    col = pl.BlockSpec((t,e), lambda g,*_: (0,g)); full = lambda s: pl.BlockSpec(s, lambda g,*_: (0,0))
    return pl.pallas_call(functools.partial(bwd_kernel, heads, QB, KB), out_shape=[jax.ShapeDtypeStruct(q.shape,BF16)]*3,
        grid_spec=pltpu.PrefetchScalarGridSpec(num_scalar_prefetch=2, grid=(groups,),
            in_specs=[col]*5+[pl.BlockSpec((1,8,t), lambda g,*_: (g,0,0)), pl.BlockSpec((1,8,t), lambda g,*_: (0,0,0)), full((t,128)), full((t,e)), full((t,e))],
            out_specs=[col]*3,
            scratch_shapes=[pltpu.VMEM((e,t),BF16), pltpu.VMEM((t//KB,heads,KB,e),BF16), pltpu.VMEM((t//KB,heads,KB,e),BF16), pltpu.VMEM((t,e),F32), pltpu.VMEM((t,e),F32)]),
        compiler_params=pltpu.CompilerParams(vmem_limit_bytes=58<<20))(lo,hi,q,k,v,att,g,lse,seg_row,seg_col,cos,sin)


def gnormed_kernel(gq_ref, gk_ref, gv_ref, wq_ref, wk_ref, wv_ref, w_ref, o_ref):
    g = pl.program_id(0)
    grads = (gq_ref, gk_ref, gv_ref)
    own = (wq_ref, wk_ref, wv_ref)

    @pl.when(g == 0)
    def _():
        o_ref[...] = dot(gq_ref[...], wq_ref[...], NT)
        for a in (1, 2):
            o_ref[...] += dot(grads[a][...], own[a][...], NT)

    @pl.when(g > 0)
    def _():
        for a in range(3):
            o_ref[...] += dot(grads[a][...], w_ref[0, a].astype(BF16), NT)


def gnormed(gq, gk, gv, wq, wk, wv, w):
    t = gq.shape[0]
    d, e = wq.shape
    groups = w.shape[0] + 1
    full = lambda s: pl.BlockSpec(s, lambda g: (0, 0))
    return pl.pallas_call(
        gnormed_kernel,
        grid=(groups,),
        out_shape=jax.ShapeDtypeStruct((t, d), F32),
        in_specs=[pl.BlockSpec((t, e), lambda g: (0, g))] * 3
        + [full((d, e))] * 3
        + [pl.BlockSpec((1, 3, d, e), lambda g: (jnp.maximum(g - 1, 0), 0, 0, 0))],
        out_specs=full((t, d)),
        compiler_params=pltpu.CompilerParams(vmem_limit_bytes=56 << 20),
    )(gq, gk, gv, wq, wk, wv, w)


def stats(values):
    mean_val = jnp.mean(values, axis=-1, keepdims=True)
    centred = values - mean_val
    r = lax.rsqrt(jnp.mean(centred * centred, axis=-1, keepdims=True) + EPS)
    return centred * r, r


def norm_pull(x, r, scale, grad):
    gp = grad * (1.0 + scale)
    return r * (
        gp - jnp.mean(gp, axis=-1, keepdims=True) - x * jnp.mean(gp * x, axis=-1, keepdims=True)
    )


def time_freqs(width):
    half = width // 2
    return jnp.exp(-math.log(10000.0) * jnp.arange(half, dtype=F32) / half)


def time_embed(flow_time, width):
    angles = 1000.0 * flow_time[:, None] * time_freqs(width)[None, :]
    both = jnp.concatenate([jnp.cos(angles), jnp.sin(angles)], axis=1)
    return jax.nn.silu(both).astype(BF16)


def per_device(ndp, nz, *args):
    (
        frames,
        skip_in,
        flow_time,
        segment_ids,
        w_skip,
        b_skip,
        w_mod,
        b_mod,
        w_q,
        w_k,
        w_v,
        w_o,
        w_up,
        b_up,
        w_dn,
        b_dn,
        out_grad,
    ) = args
    t, d = frames.shape
    loc = w_q.shape[1]
    fl = w_up.shape[1]
    dp = lax.axis_index("dp")
    z = lax.axis_index("tensor")
    embed = time_embed(flow_time, d)
    mod_part = dot(embed, w_mod)[0] + b_mod
    own_small = jnp.concatenate([mod_part, b_skip, b_up])[None, :]

    seg = segment_ids[0]
    idx = jnp.arange(t, dtype=jnp.int32)
    nseg = 4
    starts = jnp.stack([jnp.sum((seg < s).astype(jnp.int32)) for s in range(nseg + 1)])
    first_at = jnp.zeros_like(seg)
    for s in range(1, nseg):
        first_at = jnp.where(seg >= s, starts[s], first_at)
    pos = (idx - first_at).astype(F32)
    half = HEAD_DIM // 2
    inv = jnp.exp(-math.log(10000.0) * 2.0 * jnp.arange(half, dtype=F32) / HEAD_DIM)
    ang = pos[:, None] * inv[None, :]
    cos_h, sin_h = jnp.cos(ang), jnp.sin(ang)
    cos = jnp.tile(cos_h, (1, loc // half))
    sin = jnp.tile(jnp.concatenate([-sin_h, sin_h], axis=1), (1, loc // HEAD_DIM))
    qb_first, qb_last = seg[::QB], seg[QB - 1 :: QB]
    lo = jnp.take(starts, qb_first) // KB
    hi = (jnp.take(starts, qb_last + 1) + KB - 1) // KB
    seg_row = jnp.broadcast_to(seg[None, None, :], (1, 8, t))
    seg_col = jnp.broadcast_to(seg[:, None], (t, 128))

    hidden, normed, q, k, v, wskip, wqkv, wo, small = first(
        frames, skip_in, w_skip, w_q, w_k, w_v, w_o, own_small, cos, sin, nz
    )
    small = small[:, 0]
    nm = mod_part.shape[0]
    mod = small[:, :nm].reshape(6, d)
    shift1, scale1, gate1, shift2, scale2, gate2 = [mod[i][None, :] for i in range(6)]
    bup = jnp.concatenate(
        [
            lax.dynamic_index_in_dim(small[:, nm + loc :], (z + k) % nz, 0, keepdims=True)
            for k in range(1, nz)
        ]
    )

    def own_cols(a):
        return lax.dynamic_slice_in_dim(a, z * loc, loc, a.ndim - 1)

    att, lse = attn_fwd(q, k, v, seg_row, seg_col, lo, hi, nz)
    output, g_mid, g_branch, g_att, gw, sums, g_b_up, g_gate2_own, _ = second(
        att,
        hidden,
        out_grad,
        w_o,
        wo,
        w_up,
        w_dn,
        jnp.concatenate([mod, jnp.zeros((2, d), F32)]),
        b_up[None, :],
        bup,
        b_dn[None, :],
        nz,
    )
    g_shift2, g_scale2, g_gate1 = sums[0], sums[1], sums[2]
    g_b_dn = gate2[0] * sums[3]
    first_sum = lax.psum_scatter(gw, "dp", scatter_dimension=1, tiled=True)
    gq, gk, gv = attn_bwd(q, k, v, att, g_att, lse, seg_row, seg_col, lo, hi, cos, sin, nz)
    x1, r1 = stats(hidden)
    g_normed = gnormed(gq, gk, gv, w_q, w_k, w_v, wqkv)
    g_qkv = jnp.concatenate([gq[:, :loc], gk[:, :loc], gv[:, :loc]], axis=1)
    g_w_qkv = dot(normed, g_qkv, TN)
    g_shift1 = jnp.sum(g_normed, axis=0)
    g_scale1 = jnp.sum(g_normed * x1, axis=0)
    g_hidden = g_mid + norm_pull(x1, r1, scale1, g_normed)
    g_low = g_hidden.astype(BF16)
    own_low = own_cols(g_low)
    g_b_skip = jnp.sum(own_cols(g_hidden), axis=0)
    g_w_skip = jnp.concatenate([dot(frames, own_low, TN), dot(skip_in, own_low, TN)], axis=0)

    def rows_of(base):
        return lax.dynamic_slice_in_dim(wskip, base + z * loc, loc, 0).astype(BF16)

    grad_frames = dot(g_low, rows_of(0), NT)
    grad_skip = dot(g_low, rows_of(d), NT)

    g_mod = jnp.concatenate(
        [g_shift1, g_scale1, g_gate1, g_shift2, g_scale2, jnp.zeros((d,), F32)]
    )
    own_mod = lax.dynamic_slice_in_dim(g_mod, z * nm, nm, 0)
    sizes = [nm, loc, fl, d, 128]
    offs = [sum(sizes[:i]) for i in range(len(sizes) + 1)]
    vec = jnp.concatenate(
        [own_mod, g_b_skip, g_b_up[0], g_b_dn, jnp.broadcast_to(flow_time, (128,))]
    )[None, :]
    s_qkv, s_w_skip, vecs, gates = reduce_over_dp(
        [g_w_qkv.reshape(ndp, d // ndp, 3 * loc), g_w_skip.reshape(ndp, 2 * d // ndp, loc)],
        vec,
        g_gate2_own,
        ndp,
        nz,
        1,
    )
    vecs = vecs[:, 0]
    gate_all = gates.reshape(ndp, d)
    pad = jnp.concatenate([jnp.zeros((ndp, 5 * d), F32), gate_all], axis=1)
    mod_rows = vecs[:, :nm] + lax.dynamic_slice_in_dim(pad, z * nm, nm, 1)

    def share(i, of):
        n = sizes[i] // ndp
        cols = lax.dynamic_slice_in_dim(of, offs[i] + dp * n, n, 1)
        return jnp.sum(cols, axis=0)

    def mine(v):
        n = v.shape[1] // ndp
        return jnp.sum(lax.dynamic_slice_in_dim(v, dp * n, n, 1), axis=0)

    s_b_mod = mine(mod_rows)
    embeds = time_embed(vecs[:, offs[4]], d)
    rows = d // ndp
    s_w_mod = dot(lax.dynamic_slice_in_dim(embeds, dp * rows, rows, 1), mod_rows.astype(BF16), TN)
    s_up = first_sum[:fl].T
    s_dn = first_sum[fl : 2 * fl]
    s_o = first_sum[2 * fl :]
    return (
        output,
        grad_frames,
        grad_skip,
        s_w_skip,
        share(1, vecs),
        s_w_mod,
        s_b_mod,
        s_qkv[:, :loc],
        s_qkv[:, loc : 2 * loc],
        s_qkv[:, 2 * loc :],
        s_o,
        s_up,
        share(2, vecs),
        s_dn,
        share(3, vecs),
    )


def solution(mesh):
    in_specs = (
        P("dp", None),
        P("dp", None),
        P("dp"),
        P("dp", None),
        P(None, "tensor"),
        P("tensor"),
        P(None, "tensor"),
        P("tensor"),
        P(None, "tensor"),
        P(None, "tensor"),
        P(None, "tensor"),
        P("tensor", None),
        P(None, "tensor"),
        P("tensor"),
        P("tensor", None),
        P(),
        P("dp", None),
    )
    out_specs = (
        P("dp", "tensor"),
        P("dp", "tensor"),
        P("dp", "tensor"),
        P("dp", "tensor"),
        P(("tensor", "dp")),
        P("dp", "tensor"),
        P(("tensor", "dp")),
        P("dp", "tensor"),
        P("dp", "tensor"),
        P("dp", "tensor"),
        P("tensor", "dp"),
        P("dp", "tensor"),
        P(("tensor", "dp")),
        P("tensor", "dp"),
        P("dp"),
    )
    return jax.shard_map(
        functools.partial(per_device, mesh.shape["dp"], mesh.shape["tensor"]),
        mesh=mesh,
        in_specs=in_specs,
        out_specs=out_specs,
        check_vma=False,
    )
```

```python
import functools
import math

import jax
import jax.numpy as jnp
from jax import lax
from jax.experimental import pallas as pl
from jax.experimental.pallas import tpu as pltpu
from jax.sharding import PartitionSpec as P

HEAD_DIM = 64
EPS = 1e-06
F32 = jnp.float32
BF16 = jnp.bfloat16
MESH = pl.DeviceIdType.MESH
ANY = pl.BlockSpec(memory_space=pl.ANY)
VMEM = pl.BlockSpec(memory_space=pltpu.VMEM)
GROUP = 8
NT = (((1,), (1,)), ((), ()))
NN = (((1,), (0,)), ((), ()))


def dot(a, b, dims=NN, precision=None):
    return lax.dot_general(a, b, dims, precision=precision, preferred_element_type=F32)


def remote(src, dst, send, recv, device):
    return pltpu.make_async_remote_copy(
        src_ref=src,
        dst_ref=dst,
        send_sem=send,
        recv_sem=recv,
        device_id=device,
        device_id_type=MESH,
    )


class Spread:
    def __init__(self, nz, n, src, land, plane, sems, lags):
        self.nz, self.n, self.src, self.land, self.plane = nz, n, src, land, plane
        self.lags = lags
        self.zs, self.zr, self.ps, self.pr, self.rs = sems
        dp = lax.axis_index("dp")
        z = lax.axis_index("tensor")
        self.z = z
        core = lax.rem(dp, 2)
        x = lax.rem(dp // 2, 2)
        y = lax.rem(dp // 4, 2)
        dx = 2 - 4 * x
        dy = 4 - 8 * y
        b1 = y + core * (x - y)
        b2 = x + core * (y - x)
        d1 = dy + core * (dx - dy)
        d2 = dx + core * (dy - dx)
        self.slot = core * 4 + 2 * b2 + b1
        self.near = {1: (dp + d1, z), 2: (dp + d2, z), 3: (dp + 1 - 2 * core, z)}
        self.far = {k: (dp, lax.rem(z + nz - k, nz)) for k in range(1, nz)}
        base = core * 4
        self.out = {1: (self.slot, 1), 2: (base + 2 * b2, 2), 3: (base, 4)}
        self.come = {
            1: (self.slot + 1 - 2 * b1, 1),
            2: (base + 2 - 2 * b2, 2),
            3: (4 - base, 4),
        }
        self.t = 0
        self.ready = -1

    def barrier(self):
        bar = pltpu.get_barrier_semaphore()
        devices = list(self.near.values()) + list(self.far.values())
        for device in devices:
            pl.semaphore_signal(bar, inc=1, device_id=device, device_id_type=MESH)
        pl.semaphore_wait(bar, len(devices))

    def _far(self, i, k):
        return remote(
            self.src(i),
            self.plane(i, self.slot, k - 1),
            self.zs.at[i, k - 1],
            self.zr.at[i, k - 1],
            self.far[k],
        )

    def _relay(self, i):
        at = 2 * (2 - self.z)
        return remote(
            self.plane(i, self.slot, 1),
            self.plane(i, self.slot, at),
            self.rs.at[i],
            self.zr.at[i, at],
            (lax.axis_index("dp"), 3 * (self.z - 1)),
        )

    def _near(self, i, stage, inward):
        at, size = (self.come if inward else self.out)[stage]
        ref = self.land(i).at[pl.ds(at, size)]
        return remote(
            ref, ref, self.ps.at[i, stage - 1], self.pr.at[i, stage - 1], self.near[stage]
        )

    def tick(self):
        t, n, z = self.t, self.n, self.z
        l1, l2, l3, l4 = self.lags
        if t < n:
            self._far(t, 2).start()
            pl.when(z != 0)(lambda: self._far(t, 1).start())
            pl.when(z != 3)(lambda: self._far(t, 3).start())
        if 0 <= t - l4 < n:
            self._near(t - l4, 3, True).wait_recv()
            self.ready = t - l4
        for stage, lag in ((3, l3), (2, l2)):
            if 0 <= t - lag < n:
                self._near(t - lag, stage - 1, True).wait_recv()
                self._near(t - lag, stage, False).start()
        i = t - l1
        if 0 <= i < n:
            self._far(i, 1).wait_recv()
            self._far(i, 3).wait_recv()
            pl.when((z == 0) | (z == 3))(lambda: self._far(i, 2).wait_recv())
            self._near(i, 1, False).start()
        j = t - l1 + 1
        if 0 <= j < n:

            @pl.when((z == 1) | (z == 2))
            def _():
                self._far(j, 2).wait_recv()
                self._relay(j).start()

        self.t += 1

    def until(self, i):
        while self.ready < i:
            self.tick()

    def drain(self):
        z = self.z
        for i in range(self.n):
            self._far(i, 2).wait_send()
            pl.when(z != 0)(lambda: self._far(i, 1).wait_send())
            pl.when(z != 3)(lambda: self._far(i, 3).wait_send())
            pl.when((z == 1) | (z == 2))(lambda: self._relay(i).wait_send())
            for stage in (1, 2, 3):
                self._near(i, stage, False).wait_send()


def spread_sems(nz, n):
    dma = pltpu.SemaphoreType.DMA
    kk = nz - 1
    return [dma((n, kk)), dma((n, kk)), dma((n, 3)), dma((n, 3)), dma((n,))]


def flat(small_ref, nm, lo, hi):
    parts = []
    while lo < hi:
        zz = lo // nm
        end = min(hi, (zz + 1) * nm)
        parts.append(small_ref[zz, :, lo - zz * nm : end - zz * nm])
        lo = end
    return parts[0] if len(parts) == 1 else jnp.concatenate(parts, axis=1)


def layer_norm(v):
    centred = v - jnp.mean(v, axis=-1, keepdims=True)
    r = lax.rsqrt(jnp.mean(centred * centred, axis=-1, keepdims=True) + EPS)
    return centred * r, r


TB = 512
LB = 128
LAGS_A = (2, 4, 6, 7)
LAGS_B = (2, 4, 6, 7)


def aligned(at, size):
    return pl.ds(pl.multiple_of(at, size), size)


def first_kernel(nz, chunks, *refs):
    ins, vec_ref = refs[:9], refs[9]
    hbm = refs[10:18]
    small_ref = refs[18]
    vmem_in = refs[19:28]
    (hid_ref, norm_ref, q_ref, k_ref, v_ref, w16_ref, o16_ref, row_ref) = refs[28:36]
    (pskip, pqkv, po, wb, lskip, lqkv, lo_, in_sem, out_sem, vs, vr) = refs[36:47]
    sems = refs[47:52]
    (wskip_ref, wq_ref, wk_ref, wv_ref, wo_ref, x_ref, y_ref, cos_ref, sin_ref) = vmem_in
    t, d = x_ref.shape
    loc = wq_ref.shape[1]
    nm = 6 * d // nz
    rs, rq, ro = pskip.shape[0], pqkv.shape[1], po.shape[0]

    def fetch(i):
        return pltpu.make_async_copy(ins[i], vmem_in[i], in_sem.at[i])

    for i in range(9):
        fetch(i).start()

    def src(i):
        name, a, c, r = chunks[i]
        if name == "skip":
            return pskip.at[pl.ds(c * r, r)]
        if name == "qkv":
            return pqkv.at[a, pl.ds(c * r, r)]
        return po.at[pl.ds(c * r, r)]

    def land(i):
        name, a, c, r = chunks[i]
        return {"skip": lskip, "qkv": lqkv.at[a], "o": lo_}[name].at[c]

    net = Spread(nz, len(chunks), src, land, lambda i, s, k: land(i).at[s, k], sems, LAGS_A)
    z, slot = net.z, net.slot
    small_ref[z] = vec_ref[...]
    fetch(0).wait()
    pskip[...] = wskip_ref[aligned(slot * rs, rs), :].astype(F32)
    net.barrier()
    net.tick()

    def vec(k, zz):
        return remote(vec_ref, small_ref.at[zz], vs.at[k - 1], vr.at[k - 1], net.far[k])

    for k in range(1, nz):
        vec(k, z).start()
    for i in (1, 2, 3, 4):
        fetch(i).wait()
    for a, w in enumerate((wq_ref, wk_ref, wv_ref)):
        pqkv[a] = w[aligned(slot * rq, rq), :].astype(F32)
    po[...] = wo_ref[aligned(slot * ro, ro), :].astype(F32)
    net.tick()
    for k in range(1, nz):
        vec(k, lax.rem(z + k, nz)).wait_recv()
    net.tick()
    for i in (5, 6, 7, 8):
        fetch(i).wait()

    def hidden_cols(w, zz):
        bias = small_ref[zz, :, nm : nm + loc]
        cols = aligned(zz * loc, loc)

        @pl.loop(0, t // TB)
        def _(b):
            rows = aligned(b * TB, TB)
            acc = dot(x_ref[rows, :], w[:d, :]) + dot(y_ref[rows, :], w[d:, :])
            hid_ref[rows, cols] = acc + bias

        row_ref[:loc, cols] = w[aligned(z * loc, loc), :]
        row_ref[loc:, cols] = w[aligned(d + z * loc, loc), :]

    net.tick()
    hidden_cols(wskip_ref, z)
    ns = sum(c[0] == "skip" for c in chunks)
    r = rs // ns
    for c in range(ns):
        net.until(c)
        for k in range(nz - 1):
            for s in range(GROUP):
                wb[k, s * rs + c * r : s * rs + (c + 1) * r, :] = lskip[c, s, k].astype(BF16)
    for k in range(1, nz):
        hidden_cols(wb.at[k - 1], lax.rem(z + k, nz))
        net.tick()
    shift1, scale1 = flat(small_ref, nm, 0, d), flat(small_ref, nm, d, 2 * d)

    @pl.loop(0, t // LB)
    def _(b):
        rows = aligned(b * LB, LB)
        xn, _ = layer_norm(hid_ref[rows, :])
        norm_ref[rows, :] = (xn * (1.0 + scale1) + shift1).astype(BF16)

    results = (hid_ref, norm_ref, q_ref, k_ref, v_ref, w16_ref, o16_ref, row_ref)

    def put(i):
        return pltpu.make_async_copy(results[i], hbm[i], out_sem.at[i])

    for i in (0, 1, 7):
        put(i).start()
    net.tick()

    def project(a, k, w):
        out = (q_ref, k_ref, v_ref)[a]

        @pl.loop(0, t // TB)
        def _(b):
            rows = aligned(b * TB, TB)
            u = dot(norm_ref[rows, :], w[...])
            if a < 2:
                u = u * wide(cos_ref[rows, :], loc) + swap_halves(u) * wide(sin_ref[rows, :], loc)
            if a == 0:
                u = u.astype(BF16).astype(F32) * (HEAD_DIM**-0.5)
            out[rows, k * loc : (k + 1) * loc] = u.astype(BF16)

    for a in range(3):
        project(a, 0, (wq_ref, wk_ref, wv_ref)[a])
        net.tick()
    nq = sum(c[0] == "qkv" for c in chunks) // 3
    r = rq // nq
    for a in range(3):
        net.until(ns + nq * (a + 1) - 1)
        for k in range(1, nz):
            for s in range(GROUP):
                for c in range(nq):
                    w16_ref[k - 1, a, s * rq + c * r : s * rq + (c + 1) * r, :] = lqkv[
                        a, c, s, k - 1
                    ].astype(BF16)
            project(a, k, w16_ref.at[k - 1, a])
            if a < 2:
                net.tick()
        put(2 + a).start()
    put(5).start()
    net.until(len(chunks) - 1)
    no = sum(c[0] == "o" for c in chunks)
    r = ro // no
    for k in range(nz - 1):
        for s in range(GROUP):
            for c in range(no):
                o16_ref[k, s * ro + c * r : s * ro + (c + 1) * r, :] = lo_[c, s, k].astype(BF16)
    put(6).start()
    net.drain()
    for k in range(1, nz):
        vec(k, z).wait_send()
    for i in range(8):
        put(i).wait()


def first(x, y, wskip, wq, wk, wv, wo, vec, cos, sin, nz):
    t, d = x.shape
    loc = wq.shape[1]
    kk = nz - 1
    rs, rq, ro = 2 * d // GROUP, d // GROUP, loc // GROUP
    ns, nq, no = 4, 2, 2
    chunks = [("skip", 0, c, rs // ns) for c in range(ns)]
    chunks += [("qkv", a, c, rq // nq) for a in range(3) for c in range(nq)]
    chunks += [("o", 0, c, ro // no) for c in range(no)]
    sd = jax.ShapeDtypeStruct
    dma = pltpu.SemaphoreType.DMA
    ins = [wskip, wq, wk, wv, wo, x, y, cos, sin]
    outs = [
        sd((t, d), F32),
        sd((t, d), BF16),
        sd((t, nz * loc), BF16),
        sd((t, nz * loc), BF16),
        sd((t, nz * loc), BF16),
        sd((kk, 3, d, loc), BF16),
        sd((kk, loc, d), BF16),
        sd((2 * loc, d), BF16),
    ]
    scratch = [pltpu.VMEM(v.shape, v.dtype) for v in ins]
    scratch += [pltpu.VMEM(o.shape, o.dtype) for o in outs]
    scratch += [
        pltpu.VMEM((rs, loc), F32),
        pltpu.VMEM((3, rq, loc), F32),
        pltpu.VMEM((ro, d), F32),
        pltpu.VMEM((kk, 2 * d, loc), BF16),
        pltpu.VMEM((ns, GROUP, kk, rs // ns, loc), F32),
        pltpu.VMEM((3, nq, GROUP, kk, rq // nq, loc), F32),
        pltpu.VMEM((no, GROUP, kk, ro // no, d), F32),
        dma((9,)),
        dma((8,)),
        dma((kk,)),
        dma((kk,)),
    ] + spread_sems(nz, len(chunks))
    return pl.pallas_call(
        functools.partial(first_kernel, nz, chunks),
        out_shape=outs + [sd((nz,) + vec.shape, F32)],
        in_specs=[ANY] * 9 + [VMEM],
        out_specs=[ANY] * 8 + [VMEM],
        scratch_shapes=scratch,
        compiler_params=pltpu.CompilerParams(
            collective_id=0, has_side_effects=True, vmem_limit_bytes=62 << 20
        ),
    )(*ins, vec)


def gelu_parts(v):
    c = math.sqrt(2.0 / math.pi)
    v2 = v * v
    th = jnp.tanh(c * v * (1.0 + 0.044715 * v2))
    half = 0.5 * (1.0 + th)
    act = v * half
    slope = half + (0.5 * c) * v * (1.0 - th * th) * (1.0 + 3.0 * 0.044715 * v2)
    return act, slope


TN = (((0,), (0,)), ((), ()))


def second_kernel(nz, n, r, steps, *refs):
    ins = refs[:7]
    small_ref, bup_ref, bdn_ref = refs[7:10]
    hbm = refs[10:14]
    gw_ref, land, sums_ref, gbu_ref, gg2_ref = refs[14:19]
    vmem_in = refs[19:26]
    (up_ref, dn_ref, woo_ref, wo_ref, att_ref, hid_ref, go_ref) = vmem_in
    (gm_ref, gb_ref, ga_ref, out_ref) = refs[26:30]
    (pc, br_ref, n2_ref, gf_ref, stg, ub, db, act_s, gp_s, gws) = refs[30:40]
    in_sem, out_sem, st_sem, gw_sem = refs[40:44]
    sems = refs[44:49]
    t, d = hid_ref.shape
    loc = woo_ref.shape[0]
    fl = up_ref.shape[1]
    pr = fl // GROUP
    nm = 6 * d // nz

    def fetch(i):
        return pltpu.make_async_copy(ins[i], vmem_in[i], in_sem.at[i])

    for i in range(7):
        fetch(i).start()
    net = Spread(
        nz,
        n,
        lambda i: pc.at[:, pl.ds(i * r, r)],
        lambda i: land.at[i],
        lambda i, s, k: land.at[i, s, :, k],
        sems,
        LAGS_B,
    )
    z, slot = net.z, net.slot
    own = aligned(z * loc, loc)
    fetch(0).wait()
    pc[0] = up_ref[:, aligned(slot * pr, pr)].astype(F32).T
    fetch(1).wait()
    pc[1] = dn_ref[aligned(slot * pr, pr), :].astype(F32)
    net.barrier()
    net.tick()
    row = lambda i: flat(small_ref, nm, i * d, (i + 1) * d)
    gate1, shift2, scale2, gate2 = row(2), row(3), row(4), row(5)
    for i in (2, 3, 4):
        fetch(i).wait()

    @pl.loop(0, t // TB)
    def _(b):
        rows = aligned(b * TB, TB)
        br_ref[rows, :] = dot(att_ref[rows, :loc], woo_ref[...]) + dot(
            att_ref[rows, loc:], wo_ref[...].reshape((nz - 1) * loc, d)
        )

    net.tick()
    sums_ref[...] = jnp.zeros_like(sums_ref)
    for i in (5, 6):
        fetch(i).wait()

    @pl.loop(0, t // LB)
    def _(b):
        rows = aligned(b * LB, LB)
        x2, _ = layer_norm(hid_ref[rows, :] + gate1 * br_ref[rows, :])
        n2_ref[rows, :] = (x2 * (1.0 + scale2) + shift2).astype(BF16)
        go = go_ref[rows, :].astype(F32)
        sums_ref[3:4, :] += jnp.sum(go, axis=0, keepdims=True)
        gf_ref[rows, :] = (gate2 * go).astype(BF16)

    net.tick()

    def units(first_time, rows, pre, dnv, back):
        act, slope = gelu_parts(pre)
        act = act.astype(BF16)
        ffn = dot(act, dnv[:, own])
        g_pre = (dot(gf_ref[rows, :], dnv[...], NT) * slope).astype(BF16)
        gn = back(g_pre)
        if first_time:
            out_ref[rows, :] = ffn
            gm_ref[rows, :] = gn
        else:
            out_ref[rows, :] += ffn
            gm_ref[rows, :] += gn
        return act, g_pre

    parts = 4
    sub = fl // parts
    gwc = lambda j, s: pltpu.make_async_copy(
        gws.at[s], gw_ref.at[pl.ds(s * fl + j * sub, sub)], gw_sem.at[s]
    )
    for j in range(parts):
        cs = slice(j * sub, (j + 1) * sub)

        @pl.loop(0, t // TB)
        def _(b):
            rows = aligned(b * TB, TB)
            pre = dot(n2_ref[rows, :], up_ref[:, cs]) + bup_ref[:, cs]
            a, g = units(
                j == 0, rows, pre, dn_ref.at[cs, :], lambda gp: dot(gp, up_ref[:, cs], NT)
            )
            act_s[rows, :] = a
            gp_s[rows, :] = g

        net.tick()
        if j > 0:
            for s in range(2):
                gwc(j - 1, s).wait()
        gbu_ref[:, cs] = jnp.sum(gp_s[...].astype(F32), axis=0, keepdims=True)
        gws[0] = dot(gp_s[...], n2_ref[...], TN)
        gws[1] = dot(act_s[...], gf_ref[...], TN)
        for s in range(2):
            gwc(j, s).start()
        net.tick()
    at = 0
    for per in steps:
        net.until(at + per - 1)
        stage = lambda: pltpu.make_async_copy(
            land.at[pl.ds(at, per)], stg.at[pl.ds(0, per)], st_sem.at[0]
        )
        stage().start()
        stage().wait()
        w = per * GROUP * r
        bias = []
        for k in range(nz - 1):
            for half, dst in ((0, ub), (1, db)):
                dst[k * w : (k + 1) * w, :] = jnp.concatenate(
                    [stg[c, s, half, k] for c in range(per) for s in range(GROUP)], axis=0
                ).astype(BF16)
            lo = nm + loc + at * GROUP * r
            bias.append(small_ref[lax.rem(z + k + 1, nz), :, lo : lo + w])
        bias = jnp.concatenate(bias, axis=1)
        w = w * (nz - 1)
        for b in range(t // TB):
            rows = pl.ds(b * TB, TB)
            pre = dot(n2_ref[rows, :], ub[:w, :], NT) + bias
            units(False, rows, pre, db.at[:w, :], lambda gp: dot(gp, ub[:w, :]))
            if net.t < n + net.lags[3]:
                net.tick()
        at += per
    net.drain()
    bdn = bdn_ref[:, own]
    results = (gm_ref, gb_ref, ga_ref, out_ref)

    def put(i, rows):
        return pltpu.make_async_copy(results[i].at[rows], hbm[i].at[rows], out_sem.at[i])

    br_own = br_ref.at[:, own]
    g1s, g2s = stg.at[0, 0, 0, 0, 0:1], stg.at[0, 0, 0, 1, 0:1]
    g1s[...] = gate1
    g2s[...] = gate2
    gate1_own = stg[0, 0, 0, 0, 0:1, own]
    gate2_own = stg[0, 0, 0, 1, 0:1, own]
    gg2_ref[...] = jnp.zeros_like(gg2_ref)

    @pl.loop(0, t // LB)
    def _(b):
        rows = aligned(b * LB, LB)
        ffn = out_ref[rows, :] + bdn
        gg2_ref[...] += jnp.sum(go_ref[rows, own].astype(F32) * ffn, axis=0, keepdims=True)
        out_ref[rows, :] = hid_ref[rows, own] + gate1_own * br_own[rows, :] + gate2_own * ffn
        br = br_ref[rows, :]
        x2, r2 = layer_norm(hid_ref[rows, :] + gate1 * br)
        gn = gm_ref[rows, :]
        sums_ref[0:1, :] += jnp.sum(gn, axis=0, keepdims=True)
        sums_ref[1:2, :] += jnp.sum(gn * x2, axis=0, keepdims=True)
        gp = gn * (1.0 + scale2)
        gm = go_ref[rows, :].astype(F32) + r2 * (
            gp
            - jnp.mean(gp, axis=-1, keepdims=True)
            - x2 * jnp.mean(gp * x2, axis=-1, keepdims=True)
        )
        gm_ref[rows, :] = gm
        sums_ref[2:3, :] += jnp.sum(gm * br, axis=0, keepdims=True)
        gb_ref[rows, :] = (gate1 * gm).astype(BF16)

    everything = pl.ds(0, t)
    for i in (0, 1, 3):
        put(i, everything).start()

    @pl.loop(0, t // TB)
    def _(b):
        rows = aligned(b * TB, TB)
        ga_ref[rows, :loc] = dot(gb_ref[rows, :], woo_ref[...], NT).astype(BF16)
        ga_ref[rows, loc:] = dot(
            gb_ref[rows, :], wo_ref[...].reshape((nz - 1) * loc, d), NT
        ).astype(BF16)

    put(2, everything).start()
    for s in range(2):
        gwc(parts - 1, s).wait()
    gws[0, :loc, :] = dot(att_ref[:, :loc], gb_ref[...], TN)
    last = lambda: pltpu.make_async_copy(
        gws.at[0, pl.ds(0, loc)], gw_ref.at[pl.ds(2 * fl, loc)], gw_sem.at[0]
    )
    last().start()
    last().wait()
    for i in range(4):
        put(i, everything).wait()


R_B = 8
STEPS_B = (4, 4, 4, 2, 2)


def second(att, hid, go, wo_own, wo, up, dn, small, bup_own, bdn, nz, r=R_B, steps=STEPS_B):
    t, d = hid.shape
    loc = wo_own.shape[0]
    fl = up.shape[1]
    kk = nz - 1
    n = fl // GROUP // r
    sd = jax.ShapeDtypeStruct
    dma = pltpu.SemaphoreType.DMA
    per = max(steps)
    nu = per * kk * GROUP * r
    ins = [up, dn, wo_own, wo, att, hid, go]
    outs = [sd((t, d), F32), sd((t, d), BF16), sd((t, nz * loc), BF16), sd((t, loc), F32)]
    rest = [
        sd((2 * fl + loc, d), F32),
        sd((n, GROUP, 2, kk, r, d), F32),
        sd((8, d), F32),
        sd((1, fl), F32),
        sd((1, loc), F32),
    ]
    scratch = [pltpu.VMEM(v.shape, v.dtype) for v in ins]
    scratch += [pltpu.VMEM(o.shape, o.dtype) for o in outs]
    scratch += [
        pltpu.VMEM((2, fl // GROUP, d), F32),
        pltpu.VMEM((t, d), F32),
        pltpu.VMEM((t, d), BF16),
        pltpu.VMEM((t, d), BF16),
        pltpu.VMEM((per, GROUP, 2, kk, r, d), F32),
        pltpu.VMEM((nu, d), BF16),
        pltpu.VMEM((nu, d), BF16),
        pltpu.VMEM((t, fl // 4), BF16),
        pltpu.VMEM((t, fl // 4), BF16),
        pltpu.VMEM((2, max(fl // 4, loc), d), F32),
        dma((7,)),
        dma((4,)),
        dma((1,)),
        dma((2,)),
    ] + spread_sems(nz, n)
    return pl.pallas_call(
        functools.partial(second_kernel, nz, n, r, steps),
        out_shape=outs + rest,
        in_specs=[ANY] * 7 + [VMEM] * 3,
        out_specs=[ANY] * 4 + [ANY] * 2 + [VMEM] * 3,
        scratch_shapes=scratch,
        compiler_params=pltpu.CompilerParams(
            collective_id=2, has_side_effects=True, vmem_limit_bytes=62 << 20
        ),
    )(*ins, small, bup_own, bdn)


class Halving:
    def __init__(self, ndp, src, out, refs, mine, partner):
        self.bits = ndp.bit_length() - 1
        self.ndp, self.src, self.out, self.mine, self.partner = ndp, src, out, mine, partner
        self.recv0, self.lev0, self.s0, self.r0 = refs[:4]
        self.rest = refs[4:]
        self.cw = src.shape[2] // 2
        self.orders = [list(range(1, self.bits)), list(range(self.bits - 1, 0, -1))]
        self.step = -1
        self.sent = []

    def _first(self, i):
        give = 2 * i + 1 - self.mine[0]
        return remote(
            self.src.at[give], self.recv0.at[i], self.s0.at[i], self.r0.at[i], self.partner[0]
        )

    def start(self):
        for i in range(self.ndp // 2):
            self._first(i).start()

    def _items(self, h):
        src, free = self.state[h]
        b = self.orders[h][self.step]
        at = free.index(b)
        lo = 1 << at
        left = [f for f in free if f != b]
        recv, out, ss, rr = self.rest[4 * (2 * self.step + h) : 4 * (2 * self.step + h) + 4]
        items = []
        for i in range(1 << len(left)):
            base = (i // lo) * 2 * lo + i % lo
            give = base + lo * (1 - self.mine[b])
            keep = base + lo * self.mine[b]
            c = functools.partial(
                remote, src.at[give], recv.at[i], ss.at[i], rr.at[i], self.partner[b]
            )
            items.append((c, keep, i))
        return items, src, recv, out, left

    def advance(self):
        if self.step < 0:
            for i in range(self.ndp // 2):
                self._first(i).wait_recv()
                self.lev0[i] = self.src[2 * i + self.mine[0]] + self.recv0[i]
            free = list(range(1, self.bits))
            self.state = [(self.lev0.at[:, :, pl.ds(h * self.cw, self.cw)], free) for h in (0, 1)]
        else:
            for h in (0, 1):
                items, src, recv, out, left = self.now[h]
                for c, keep, i in items:
                    c().wait_recv()
                    total = src[keep] + recv[i]
                    if self.step == self.bits - 2:
                        self.out[:, pl.ds(h * self.cw, self.cw)] = total
                    else:
                        out[i] = total
                    self.sent.append(c)
                self.state[h] = (out, left)
        self.step += 1
        if self.step < self.bits - 1:
            self.now = [self._items(h) for h in (0, 1)]
            for h in (0, 1):
                for c, _, _ in self.now[h][0]:
                    c().start()

    def finish(self):
        while self.step < self.bits - 1:
            self.advance()

    def drain(self):
        for c in self.sent:
            c().wait_send()
        for i in range(self.ndp // 2):
            self._first(i).wait_send()


def halving_refs(ndp, r, c):
    dma = pltpu.SemaphoreType.DMA
    bits = ndp.bit_length() - 1
    half = ndp // 2
    out = [pltpu.VMEM((half, r, c), F32), pltpu.VMEM((half, r, c), F32), dma((half,)), dma((half,))]
    for step in range(bits - 1):
        n = ndp >> (step + 2)
        for _ in range(2):
            out += [pltpu.VMEM((n, r, c // 2), F32), pltpu.VMEM((n, r, c // 2), F32), dma((n,)), dma((n,))]
    return out


def third_kernel(ndp, nz, nh, *refs):
    ni = 13
    ins = refs[:ni]
    small_ref, sums_ref, gbu_ref, gg2_ref, emb_ref = refs[ni : ni + 5]
    sqkv_ref, sskip_ref, all_ref, tot_ref = refs[ni + 5 : ni + 9]
    hbm = refs[ni + 9 : ni + 11]
    rest = refs[ni + 11 :]
    vmem_in = rest[:ni]
    (norm_ref, gq_ref, gk_ref, gv_ref, wq_ref, wk_ref, wv_ref, w_ref) = vmem_in[:8]
    (hid_ref, gm_ref, x_ref, y_ref, row_ref) = vmem_in[8:]
    gf_ref, gs_ref, gn_ref, low_ref, gwq, gws, vec, gz, mod_s = rest[ni : ni + 9]
    in_sem, out_sem, z_send, z_recv, q_send, q_recv = rest[ni + 9 : ni + 15]
    h1 = rest[ni + 15 : ni + 15 + nh]
    h2 = rest[ni + 15 + nh :]
    t, d = hid_ref.shape
    loc = wq_ref.shape[1]
    fl = gbu_ref.shape[1]
    nm = 6 * d // nz
    dp = lax.axis_index("dp")
    z = lax.axis_index("tensor")

    def fetch(i):
        return pltpu.make_async_copy(ins[i], vmem_in[i], in_sem.at[i])

    for i in range(ni):
        fetch(i).start()
    bits = ndp.bit_length() - 1
    mine = [lax.rem(dp // (1 << b), 2) for b in range(bits)]
    partner = [(dp + (1 << b) * (1 - 2 * mine[b]), z) for b in range(bits)]
    others = lambda j: (lax.rem(dp + j, ndp), z)
    bar = pltpu.get_barrier_semaphore()
    for j in range(1, ndp):
        pl.semaphore_signal(bar, inc=1, device_id=others(j), device_id_type=MESH)
    for k in range(1, nz):
        pl.semaphore_signal(
            bar, inc=1, device_id=(dp, lax.rem(z + k, nz)), device_id_type=MESH
        )
    grads = (gq_ref, gk_ref, gv_ref)
    for i in range(4):
        fetch(i).wait()
    for a in range(3):
        gwq[:, :, a * loc : (a + 1) * loc] = dot(
            norm_ref[...], grads[a][:, :loc], TN
        ).reshape(ndp, d // ndp, loc)
    pl.semaphore_wait(bar, ndp - 1 + nz - 1)
    one = Halving(ndp, gwq, sqkv_ref, h1, mine, partner)
    one.start()

    def part(k, zz):
        return remote(
            gg2_ref, gz.at[zz], z_send.at[k - 1], z_recv.at[k - 1], (dp, lax.rem(z + nz - k, nz))
        )

    for k in range(1, nz):
        part(k, z).start()
    gz[z] = gg2_ref[...]
    for i in range(4, 8):
        fetch(i).wait()
    own = (wq_ref, wk_ref, wv_ref)

    def product(b):
        rows = pl.ds(b * TB, TB)
        acc = dot(gq_ref[rows, :loc], wq_ref[...], NT)
        for k in range(nz):
            for a in range(3):
                if k == 0 and a == 0:
                    continue
                w = own[a][...] if k == 0 else w_ref[k - 1, a]
                acc = acc + dot(grads[a][rows, k * loc : (k + 1) * loc], w, NT)
        gn_ref[rows, :] = acc

    for b in range(t // TB):
        product(b)
        if b == 0:
            one.advance()
    one.advance()
    scale1 = flat(small_ref, nm, d, 2 * d)
    mod_s[...] = jnp.zeros_like(mod_s)
    for i in (8, 9):
        fetch(i).wait()

    @pl.loop(0, t // LB)
    def _(b):
        rows = aligned(b * LB, LB)
        x1, r1 = layer_norm(hid_ref[rows, :])
        gn = gn_ref[rows, :]
        mod_s[:, :d] += jnp.sum(gn, axis=0, keepdims=True)
        mod_s[:, d : 2 * d] += jnp.sum(gn * x1, axis=0, keepdims=True)
        gp = gn * (1.0 + scale1)
        gh = gm_ref[rows, :] + r1 * (
            gp
            - jnp.mean(gp, axis=-1, keepdims=True)
            - x1 * jnp.mean(gp * x1, axis=-1, keepdims=True)
        )
        mod_s[:, 6 * d :] += jnp.sum(gh, axis=0, keepdims=True)
        low_ref[rows, :] = gh.astype(BF16)

    one.advance()
    for i in (10, 11, 12):
        fetch(i).wait()
    cols = aligned(z * loc, loc)
    low_own = low_ref[:, cols]
    half = ndp // 2
    gws[:half] = dot(x_ref[...], low_own, TN).reshape(half, 2 * d // ndp, loc)
    gws[half:] = dot(y_ref[...], low_own, TN).reshape(half, 2 * d // ndp, loc)
    two = Halving(ndp, gws, sskip_ref, h2, mine, partner)
    two.start()
    for k in range(1, nz):
        part(k, lax.rem(z + k, nz)).wait_recv()
    gate2 = flat(small_ref, nm, 5 * d, 6 * d)
    mod_s[:, 2 * d : 3 * d] = sums_ref[2:3, :]
    mod_s[:, 3 * d : 4 * d] = sums_ref[0:1, :]
    mod_s[:, 4 * d : 5 * d] = sums_ref[1:2, :]
    for zz in range(nz):
        mod_s[:, 5 * d + zz * loc : 5 * d + (zz + 1) * loc] = gz[zz]
    o = nm
    vec[:, :o] = mod_s[:, aligned(z * nm, nm)]
    vec[:, o : o + loc] = mod_s[:, pl.ds(pl.multiple_of(6 * d + z * loc, loc), loc)]
    o += loc
    vec[:, o : o + fl] = gbu_ref[...]
    o += fl
    vec[:, o : o + d] = gate2 * sums_ref[3:4, :]
    o += d
    vec[:, o : o + d] = emb_ref[...]
    all_ref[dp] = vec[...]

    def give(j, row):
        return remote(vec, all_ref.at[row], q_send.at[j - 1], q_recv.at[j - 1], others(j))

    for j in range(1, ndp):
        give(j, dp).start()

    outs = (gf_ref, gs_ref)

    def put(i):
        return pltpu.make_async_copy(outs[i], hbm[i], out_sem.at[i])

    def back(i):
        w = row_ref[i * loc : (i + 1) * loc, :]
        for b in range(t // TB):
            rows = pl.ds(b * TB, TB)
            outs[i][rows, :] = dot(low_ref[rows, :], w, NT)
        put(i).start()

    two.advance()
    back(0)
    two.advance()
    one.finish()
    back(1)
    two.finish()
    for j in range(1, ndp):
        give(j, lax.rem(dp + ndp - j, ndp)).wait_recv()
    tot_ref[...] = jnp.sum(all_ref[...], axis=0)
    one.drain()
    two.drain()
    for k in range(1, nz):
        part(k, z).wait_send()
    for j in range(1, ndp):
        give(j, dp).wait_send()
    for i in range(2):
        put(i).wait()


def third(norm, gq, gk, gv, wq, wk, wv, w, hid, gm, x, y, row, small, sums, gbu, gg2, emb, ndp, nz):
    t, d = hid.shape
    loc = wq.shape[1]
    fl = gbu.shape[1]
    n = 6 * d // nz + loc + fl + 2 * d
    sd = jax.ShapeDtypeStruct
    dma = pltpu.SemaphoreType.DMA
    ins = [norm, gq, gk, gv, wq, wk, wv, w, hid, gm, x, y, row]
    scratch = [pltpu.VMEM(v.shape, v.dtype) for v in ins]
    scratch += [
        pltpu.VMEM((t, loc), F32),
        pltpu.VMEM((t, loc), F32),
        pltpu.VMEM((t, d), F32),
        pltpu.VMEM((t, d), BF16),
        pltpu.VMEM((ndp, d // ndp, 3 * loc), F32),
        pltpu.VMEM((ndp, 2 * d // ndp, loc), F32),
        pltpu.VMEM((1, n), F32),
        pltpu.VMEM((nz, 1, loc), F32),
        pltpu.VMEM((1, 7 * d), F32),
        dma((len(ins),)),
        dma((2,)),
        dma((nz - 1,)),
        dma((nz - 1,)),
        dma((ndp - 1,)),
        dma((ndp - 1,)),
    ]
    h1 = halving_refs(ndp, d // ndp, 3 * loc)
    h2 = halving_refs(ndp, 2 * d // ndp, loc)
    return pl.pallas_call(
        functools.partial(third_kernel, ndp, nz, len(h1)),
        out_shape=[
            sd((d // ndp, 3 * loc), F32),
            sd((2 * d // ndp, loc), F32),
            sd((ndp, 1, n), F32),
            sd((1, n), F32),
            sd((t, loc), F32),
            sd((t, loc), F32),
        ],
        in_specs=[ANY] * len(ins) + [VMEM] * 5,
        out_specs=[VMEM] * 4 + [ANY] * 2,
        scratch_shapes=scratch + h1 + h2,
        compiler_params=pltpu.CompilerParams(
            collective_id=1, has_side_effects=True, vmem_limit_bytes=62 << 20
        ),
    )(*ins, small, sums, gbu, gg2, emb)


def wide(table, lanes):
    return jnp.concatenate([table] * (lanes // 128), axis=1)


def swap_halves(u):
    n = u.shape[1]
    lane = lax.broadcasted_iota(jnp.int32, u.shape, 1)
    half = HEAD_DIM // 2
    return jnp.where(
        lane % HEAD_DIM < half, pltpu.roll(u, n - half, 1), pltpu.roll(u, half, 1)
    )


QB = 256
KB = 256
NEG = -1e30


def stack_heads(dst, src, heads):
    lane = lax.broadcasted_iota(jnp.int32, src.shape, 1) // HEAD_DIM
    for h in range(heads):
        dst[:, h] = jnp.where(lane == h, src, jnp.zeros_like(src)).reshape(dst.shape[0], dst.shape[2], dst.shape[3])

def fwd_kernel(heads, QB, KB, lo_ref, hi_ref, q_ref, k_ref, v_ref, segq_ref, segk_ref, o_ref, lse_ref, vt_ref, ks_ref, s_ref):
    i = pl.program_id(1)
    @pl.when(i == 0)
    def _():
        vt_ref[...] = v_ref[...].T
        stack_heads(ks_ref, k_ref[...], heads)
    q = q_ref[...]
    segq = segq_ref[0, pl.ds(0, 1)]
    e = q.shape[1]
    lo, hi = lo_ref[i], hi_ref[i]
    def first(j, mx):
        start = pl.multiple_of(j*KB, KB)
        s = dot(ks_ref[j].reshape(heads*KB, e), q, NT)
        segk = segk_ref[pl.ds(start, KB), :]
        same = jnp.concatenate([segk]*(QB//128), axis=1) == segq
        out = []
        for h in range(heads):
            sh = jnp.where(same, s[h*KB:(h+1)*KB], NEG)
            s_ref[j, h] = sh
            out.append(jnp.maximum(mx[h], jnp.max(sh.reshape(KB//8, 8, QB), axis=0)))
        return out
    mx = lax.fori_loop(lo, hi, first, [jnp.full((8, QB), NEG, F32)]*heads)
    ms = [jnp.max(m, axis=0, keepdims=True) for m in mx]
    def second(j, carry):
        ls, os_ = carry
        start = pl.multiple_of(j*KB, KB)
        nl, no = [], []
        for h in range(heads):
            p = jnp.exp(s_ref[j, h] - ms[h])
            nl.append(ls[h] + jnp.sum(p.reshape(KB//8, 8, QB), axis=0))
            vt = vt_ref[pl.ds(h*HEAD_DIM, HEAD_DIM), pl.ds(start, KB)]
            no.append(os_[h] + dot(vt, p.astype(BF16)))
        return nl, no
    ls, os_ = lax.fori_loop(lo, hi, second, ([jnp.zeros((8, QB), F32)]*heads, [jnp.zeros((HEAD_DIM, QB), F32)]*heads))
    l1 = [jnp.sum(l, axis=0, keepdims=True) for l in ls]
    out = jnp.concatenate([os_[h] / l1[h] for h in range(heads)], axis=0)
    o_ref[...] = out.T.astype(BF16)
    lse = [ms[h] + jnp.log(l1[h]) for h in range(heads)]
    lse_ref[0] = jnp.concatenate(lse + [jnp.zeros((8 - heads, QB), F32)], axis=0)

def attn_fwd(q, k, v, seg_row, seg_col, lo, hi, groups, QB=QB, KB=KB):
    t = q.shape[0]; e = q.shape[1]//groups; heads = e//HEAD_DIM
    return pl.pallas_call(functools.partial(fwd_kernel, heads, QB, KB),
        out_shape=[jax.ShapeDtypeStruct(q.shape, BF16), jax.ShapeDtypeStruct((groups, 8, t), F32)],
        grid_spec=pltpu.PrefetchScalarGridSpec(num_scalar_prefetch=2, grid=(groups, t//QB),
            in_specs=[pl.BlockSpec((QB, e), lambda g,i,*_: (i, g)), pl.BlockSpec((t, e), lambda g,i,*_: (0, g)), pl.BlockSpec((t, e), lambda g,i,*_: (0, g)),
                      pl.BlockSpec((1, 8, QB), lambda g,i,*_: (0,0,i)), pl.BlockSpec((t,128), lambda g,i,*_: (0,0))],
            out_specs=[pl.BlockSpec((QB, e), lambda g,i,*_: (i, g)), pl.BlockSpec((1,8,QB), lambda g,i,*_: (g,0,i))],
            scratch_shapes=[pltpu.VMEM((e,t),BF16), pltpu.VMEM((t//KB, heads, KB, e), BF16), pltpu.VMEM((t//KB, heads, KB, QB), F32)]),
        compiler_params=pltpu.CompilerParams(vmem_limit_bytes=56<<20))(lo, hi, q, k, v, seg_row, seg_col)

def bwd_kernel(heads, QB, KB, lo_ref, hi_ref, q_ref, k_ref, v_ref, att_ref, g_ref, lse_ref, segq_ref, segk_ref, cos_ref, sin_ref, gq_ref, gk_ref, gv_ref,
               kt_ref, ks_ref, vs_ref, dk_ref, dv_ref):
    t, e = k_ref.shape
    kt_ref[...] = k_ref[...].T
    stack_heads(ks_ref, k_ref[...], heads)
    stack_heads(vs_ref, v_ref[...], heads)
    dk_ref[...] = jnp.zeros_like(dk_ref); dv_ref[...] = jnp.zeros_like(dv_ref)
    row = lax.broadcasted_iota(jnp.int32, (8, e), 0); lane = lax.broadcasted_iota(jnp.int32, (8, e), 1)
    ind = jnp.where(lane//HEAD_DIM == row, 1.0, 0.0).astype(F32)
    lanek = lax.broadcasted_iota(jnp.int32, (KB, e), 1)//HEAD_DIM
    @pl.loop(0, t//QB)
    def _(i):
        qs = pl.multiple_of(i*QB, QB)
        q = q_ref[pl.ds(qs, QB), :]; g = g_ref[pl.ds(qs, QB), :]
        segq = segq_ref[0, pl.ds(0,1), pl.ds(qs, QB)]
        prod = g.astype(F32)*att_ref[pl.ds(qs, QB), :].astype(F32)
        delta = dot(ind, prod, NT, lax.Precision.HIGHEST)
        lse = lse_ref[0, :, pl.ds(qs, QB)]
        def body(j, dq):
            start = pl.multiple_of(j*KB, KB)
            s = dot(ks_ref[j].reshape(heads*KB, e), q, NT)
            dpt = dot(vs_ref[j].reshape(heads*KB, e), g, NT)
            segk = segk_ref[pl.ds(start, KB), :]
            same = jnp.concatenate([segk]*(QB//128), axis=1) == segq
            ps, dss, ndq = [], [], []
            for h in range(heads):
                p = jnp.exp(jnp.where(same, s[h*KB:(h+1)*KB], NEG) - lse[h:h+1])
                ds = (p*(dpt[h*KB:(h+1)*KB] - delta[h:h+1])).astype(BF16)
                ps.append(p.astype(BF16)); dss.append(ds)
                kt = kt_ref[pl.ds(h*HEAD_DIM, HEAD_DIM), pl.ds(start, KB)]
                ndq.append(dq[h] + dot(kt, ds))
            dvs = dot(jnp.concatenate(ps, axis=0), g)
            dks = dot(jnp.concatenate(dss, axis=0), q)
            dv, dk = dvs[:KB], dks[:KB]
            for h in range(1, heads):
                dv = jnp.where(lanek == h, dvs[h*KB:(h+1)*KB], dv)
                dk = jnp.where(lanek == h, dks[h*KB:(h+1)*KB], dk)
            dk_ref[pl.ds(start, KB), :] += dk
            dv_ref[pl.ds(start, KB), :] += dv
            return ndq
        dq = lax.fori_loop(lo_ref[i], hi_ref[i], body, [jnp.zeros((HEAD_DIM, QB), F32)]*heads)
        dqf = jnp.concatenate(dq, axis=0).T * (HEAD_DIM**-0.5)
        cos = wide(cos_ref[pl.ds(qs, QB), :], e)
        sin = wide(sin_ref[pl.ds(qs, QB), :], e)
        gq_ref[pl.ds(qs, QB), :] = (dqf*cos - swap_halves(dqf)*sin).astype(BF16)
    dk = dk_ref[...]
    gk_ref[...] = (dk * wide(cos_ref[...], e) - swap_halves(dk) * wide(sin_ref[...], e)).astype(BF16)
    gv_ref[...] = dv_ref[...].astype(BF16)

def attn_bwd(q,k,v,att,g,lse,seg_row,seg_col,lo,hi,cos,sin,groups,QB=QB,KB=KB):
    t = q.shape[0]; e = q.shape[1]//groups; heads = e//HEAD_DIM
    col = pl.BlockSpec((t,e), lambda g,*_: (0,g)); full = lambda s: pl.BlockSpec(s, lambda g,*_: (0,0))
    return pl.pallas_call(functools.partial(bwd_kernel, heads, QB, KB), out_shape=[jax.ShapeDtypeStruct(q.shape,BF16)]*3,
        grid_spec=pltpu.PrefetchScalarGridSpec(num_scalar_prefetch=2, grid=(groups,),
            in_specs=[col]*5+[pl.BlockSpec((1,8,t), lambda g,*_: (g,0,0)), pl.BlockSpec((1,8,t), lambda g,*_: (0,0,0)), full((t,128)), full((t,128)), full((t,128))],
            out_specs=[col]*3,
            scratch_shapes=[pltpu.VMEM((e,t),BF16), pltpu.VMEM((t//KB,heads,KB,e),BF16), pltpu.VMEM((t//KB,heads,KB,e),BF16), pltpu.VMEM((t,e),F32), pltpu.VMEM((t,e),F32)]),
        compiler_params=pltpu.CompilerParams(vmem_limit_bytes=58<<20))(lo,hi,q,k,v,att,g,lse,seg_row,seg_col,cos,sin)


def time_freqs(width):
    half = width // 2
    return jnp.exp(-math.log(10000.0) * jnp.arange(half, dtype=F32) / half)


def time_embed(flow_time, width):
    angles = 1000.0 * flow_time[:, None] * time_freqs(width)[None, :]
    both = jnp.concatenate([jnp.cos(angles), jnp.sin(angles)], axis=1)
    return jax.nn.silu(both).astype(BF16)


def per_device(ndp, nz, *args):
    (
        frames,
        skip_in,
        flow_time,
        segment_ids,
        w_skip,
        b_skip,
        w_mod,
        b_mod,
        w_q,
        w_k,
        w_v,
        w_o,
        w_up,
        b_up,
        w_dn,
        b_dn,
        out_grad,
    ) = args
    t, d = frames.shape
    loc = w_q.shape[1]
    fl = w_up.shape[1]
    dp = lax.axis_index("dp")
    z = lax.axis_index("tensor")
    embed = time_embed(flow_time, d)
    mod_part = dot(embed, w_mod)[0] + b_mod
    bup_order = b_up.reshape(GROUP, fl // GROUP // R_B, R_B).transpose(1, 0, 2).reshape(-1)
    own_small = jnp.concatenate([mod_part, b_skip, bup_order])[None, :]

    seg = segment_ids[0]
    idx = jnp.arange(t, dtype=jnp.int32)
    nseg = 4
    starts = [jnp.sum((seg < s).astype(jnp.int32)) for s in range(1, nseg)]
    first_at = jnp.zeros_like(seg)
    for s in range(1, nseg):
        first_at = jnp.where(seg >= s, starts[s - 1], first_at)
    pos = (idx - first_at).astype(F32)
    half = HEAD_DIM // 2
    inv = jnp.exp(-math.log(10000.0) * 2.0 * jnp.arange(half, dtype=F32) / HEAD_DIM)
    ang = pos[:, None] * jnp.tile(inv, 128 // half)[None, :]
    sign = jnp.where(jnp.arange(128) % HEAD_DIM < half, -1.0, 1.0)
    cos = jnp.cos(ang)
    sin = jnp.sin(ang) * sign
    below = jnp.sum((seg[None, :] < seg[::QB][:, None]).astype(jnp.int32), axis=1)
    upto = jnp.sum((seg[None, :] <= seg[QB - 1 :: QB][:, None]).astype(jnp.int32), axis=1)
    lo = below // KB
    hi = (upto + KB - 1) // KB
    seg_row = jnp.broadcast_to(seg[None, None, :], (1, 8, t))
    seg_col = jnp.broadcast_to(seg[:, None], (t, 128))

    hidden, normed, q, k, v, wqkv, wo, wrows, small = first(
        frames, skip_in, w_skip, w_q, w_k, w_v, w_o, own_small, cos, sin, nz
    )
    att, lse = attn_fwd(q, k, v, seg_row, seg_col, lo, hi, nz)
    g_mid, g_branch, g_att, output, gw, _, sums, g_b_up, g_gate2_own = second(
        att, hidden, out_grad, w_o, wo, w_up, w_dn, small, b_up[None, :], b_dn[None, :], nz
    )
    first_sum = lax.psum_scatter(gw, "dp", scatter_dimension=1, tiled=True)
    gq, gk, gv = attn_bwd(q, k, v, att, g_att, lse, seg_row, seg_col, lo, hi, cos, sin, nz)
    s_qkv, s_w_skip, vecs, total, grad_frames, grad_skip = third(
        normed,
        gq,
        gk,
        gv,
        w_q,
        w_k,
        w_v,
        wqkv,
        hidden,
        g_mid,
        frames,
        skip_in,
        wrows,
        small,
        sums,
        g_b_up,
        g_gate2_own,
        embed.astype(F32),
        ndp,
        nz,
    )
    nm = mod_part.shape[0]
    sizes = [nm, loc, fl, d]
    offs = [sum(sizes[:i]) for i in range(len(sizes) + 1)]

    def share(i):
        n = sizes[i] // ndp
        return lax.dynamic_slice_in_dim(total[0], offs[i] + dp * n, n, 0)

    rows = d // ndp
    embeds = lax.dynamic_slice_in_dim(vecs[:, 0], offs[4] + dp * rows, rows, 1)
    s_w_mod = dot(embeds.astype(BF16), vecs[:, 0, :nm].astype(BF16), TN)
    s_up = first_sum[:fl].T
    s_dn = first_sum[fl : 2 * fl]
    s_o = first_sum[2 * fl :]
    return (
        output,
        grad_frames,
        grad_skip,
        s_w_skip,
        share(1),
        s_w_mod,
        share(0),
        s_qkv[:, :loc],
        s_qkv[:, loc : 2 * loc],
        s_qkv[:, 2 * loc :],
        s_o,
        s_up,
        share(2),
        s_dn,
        share(3),
    )


def solution(mesh):
    in_specs = (
        P("dp", None),
        P("dp", None),
        P("dp"),
        P("dp", None),
        P(None, "tensor"),
        P("tensor"),
        P(None, "tensor"),
        P("tensor"),
        P(None, "tensor"),
        P(None, "tensor"),
        P(None, "tensor"),
        P("tensor", None),
        P(None, "tensor"),
        P("tensor"),
        P("tensor", None),
        P(),
        P("dp", None),
    )
    out_specs = (
        P("dp", "tensor"),
        P("dp", "tensor"),
        P("dp", "tensor"),
        P("dp", "tensor"),
        P(("tensor", "dp")),
        P("dp", "tensor"),
        P(("tensor", "dp")),
        P("dp", "tensor"),
        P("dp", "tensor"),
        P("dp", "tensor"),
        P("tensor", "dp"),
        P("dp", "tensor"),
        P(("tensor", "dp")),
        P("tensor", "dp"),
        P("dp"),
    )
    return jax.shard_map(
        functools.partial(per_device, mesh.shape["dp"], mesh.shape["tensor"]),
        mesh=mesh,
        in_specs=in_specs,
        out_specs=out_specs,
        check_vma=False,
    )
```

```python
import functools
import math

import jax
import jax.numpy as jnp
from jax import lax
from jax.experimental import pallas as pl
from jax.experimental.pallas import tpu as pltpu
from jax.sharding import PartitionSpec as P

HEAD_DIM = 64
EPS = 1e-06
F32 = jnp.float32
BF16 = jnp.bfloat16
MESH = pl.DeviceIdType.MESH
ANY = pl.BlockSpec(memory_space=pl.ANY)
VMEM = pl.BlockSpec(memory_space=pltpu.VMEM)
GROUP = 8
NT = (((1,), (1,)), ((), ()))
NN = (((1,), (0,)), ((), ()))


def dot(a, b, dims=NN, precision=None):
    return lax.dot_general(a, b, dims, precision=precision, preferred_element_type=F32)


def remote(src, dst, send, recv, device):
    return pltpu.make_async_remote_copy(
        src_ref=src,
        dst_ref=dst,
        send_sem=send,
        recv_sem=recv,
        device_id=device,
        device_id_type=MESH,
    )


class Spread:
    def __init__(self, nz, n, src, land, plane, sems, lags):
        self.nz, self.n, self.src, self.land, self.plane = nz, n, src, land, plane
        self.lags = lags
        self.zs, self.zr, self.ps, self.pr, self.rs = sems
        dp = lax.axis_index("dp")
        z = lax.axis_index("tensor")
        self.z = z
        core = lax.rem(dp, 2)
        x = lax.rem(dp // 2, 2)
        y = lax.rem(dp // 4, 2)
        dx = 2 - 4 * x
        dy = 4 - 8 * y
        b1 = y + core * (x - y)
        b2 = x + core * (y - x)
        d1 = dy + core * (dx - dy)
        d2 = dx + core * (dy - dx)
        self.slot = core * 4 + 2 * b2 + b1
        self.near = {1: (dp + d1, z), 2: (dp + d2, z), 3: (dp + 1 - 2 * core, z)}
        self.far = {k: (dp, lax.rem(z + nz - k, nz)) for k in range(1, nz)}
        base = core * 4
        self.out = {1: (self.slot, 1), 2: (base + 2 * b2, 2), 3: (base, 4)}
        self.come = {
            1: (self.slot + 1 - 2 * b1, 1),
            2: (base + 2 - 2 * b2, 2),
            3: (4 - base, 4),
        }
        self.t = 0
        self.ready = -1

    def barrier(self):
        bar = pltpu.get_barrier_semaphore()
        devices = list(self.near.values()) + list(self.far.values())
        for device in devices:
            pl.semaphore_signal(bar, inc=1, device_id=device, device_id_type=MESH)
        pl.semaphore_wait(bar, len(devices))

    def _far(self, i, k):
        return remote(
            self.src(i),
            self.plane(i, self.slot, k - 1),
            self.zs.at[i, k - 1],
            self.zr.at[i, k - 1],
            self.far[k],
        )

    def _relay(self, i):
        at = 2 * (2 - self.z)
        return remote(
            self.plane(i, self.slot, 1),
            self.plane(i, self.slot, at),
            self.rs.at[i],
            self.zr.at[i, at],
            (lax.axis_index("dp"), 3 * (self.z - 1)),
        )

    def _near(self, i, stage, inward):
        at, size = (self.come if inward else self.out)[stage]
        ref = self.land(i).at[pl.ds(at, size)]
        return remote(
            ref, ref, self.ps.at[i, stage - 1], self.pr.at[i, stage - 1], self.near[stage]
        )

    def tick(self):
        t, n, z = self.t, self.n, self.z
        l1, l2, l3, l4 = self.lags
        if t < n:
            self._far(t, 2).start()
            pl.when(z != 0)(lambda: self._far(t, 1).start())
            pl.when(z != 3)(lambda: self._far(t, 3).start())
        if 0 <= t - l4 < n:
            self._near(t - l4, 3, True).wait_recv()
            self.ready = t - l4
        for stage, lag in ((3, l3), (2, l2)):
            if 0 <= t - lag < n:
                self._near(t - lag, stage - 1, True).wait_recv()
                self._near(t - lag, stage, False).start()
        i = t - l1
        if 0 <= i < n:
            self._far(i, 1).wait_recv()
            self._far(i, 3).wait_recv()
            pl.when((z == 0) | (z == 3))(lambda: self._far(i, 2).wait_recv())
            self._near(i, 1, False).start()
        j = t - l1 + 1
        if 0 <= j < n:

            @pl.when((z == 1) | (z == 2))
            def _():
                self._far(j, 2).wait_recv()
                self._relay(j).start()

        self.t += 1

    def until(self, i):
        while self.ready < i:
            self.tick()

    def drain(self):
        z = self.z
        for i in range(self.n):
            self._far(i, 2).wait_send()
            pl.when(z != 0)(lambda: self._far(i, 1).wait_send())
            pl.when(z != 3)(lambda: self._far(i, 3).wait_send())
            pl.when((z == 1) | (z == 2))(lambda: self._relay(i).wait_send())
            for stage in (1, 2, 3):
                self._near(i, stage, False).wait_send()


def spread_sems(nz, n):
    dma = pltpu.SemaphoreType.DMA
    kk = nz - 1
    return [dma((n, kk)), dma((n, kk)), dma((n, 3)), dma((n, 3)), dma((n,))]


def flat(small_ref, nm, lo, hi):
    parts = []
    while lo < hi:
        zz = lo // nm
        end = min(hi, (zz + 1) * nm)
        parts.append(small_ref[zz, :, lo - zz * nm : end - zz * nm])
        lo = end
    return parts[0] if len(parts) == 1 else jnp.concatenate(parts, axis=1)


def layer_norm(v):
    centred = v - jnp.mean(v, axis=-1, keepdims=True)
    r = lax.rsqrt(jnp.mean(centred * centred, axis=-1, keepdims=True) + EPS)
    return centred * r, r


TB = 512
LB = 128
LAGS = (2, 4, 6, 7)
R_B = 8
STEPS = (4, 4, 4, 2, 2)
NEG = -1e30


def aligned(at, size):
    return pl.ds(pl.multiple_of(at, size), size)


def gelu_parts(v):
    c = math.sqrt(2.0 / math.pi)
    v2 = v * v
    th = jnp.tanh(c * v * (1.0 + 0.044715 * v2))
    half = 0.5 * (1.0 + th)
    act = v * half
    slope = half + (0.5 * c) * v * (1.0 - th * th) * (1.0 + 3.0 * 0.044715 * v2)
    return act, slope


TN = (((0,), (0,)), ((), ()))


def forward_kernel(nz, chunks, *refs):
    ni, no = 12, 11
    ins = refs[:ni]
    vec_ref, bup_ref, bdn_ref, segq_ref, segk_ref = refs[ni : ni + 5]
    outs = refs[ni + 5 : ni + 5 + no]
    (h_hid, h_norm, h_q, h_k, h_v, h_w16, h_row, h_att, h_gm, h_ga, h_out) = outs
    rest = refs[ni + 5 + no :]
    gw_ref, lskip, lqkv, lo_, land = rest[:5]
    small_ref, lse_ref, sums_ref, gbu_ref, gg2_ref = rest[5:10]
    vmem_in = rest[10 : 10 + ni]
    (wskip_ref, wq_ref, wk_ref, wv_ref, wo_ref, x_ref, y_ref) = vmem_in[:7]
    (cos_ref, sin_ref, up_ref, dn_ref, go_ref) = vmem_in[7:]
    rest = rest[10 + ni :]
    (hid_ref, norm_ref, q_ref, k_ref, v_ref, f1_ref, gm_ref, out_ref) = rest[:8]
    (wb, o16_ref, row_ref, sta, stb, pskip, pqkv, po, pc) = rest[8:17]
    (ub, db, act_s, gp_s, gws, vt_ref) = rest[17:23]
    in_sem, out_sem, w_sem, sa_sem, sb_sem, gw_sem, vs, vr = rest[23:31]
    sems = rest[31:36]
    t, d = x_ref.shape
    loc = wq_ref.shape[1]
    fl = up_ref.shape[1]
    kk = nz - 1
    nm = 6 * d // nz
    rs, rq, pr = pskip.shape[0], pqkv.shape[1], fl // GROUP
    heads = loc // HEAD_DIM

    def fetch(i):
        return pltpu.make_async_copy(ins[i], vmem_in[i], in_sem.at[i])

    for i in range(ni):
        fetch(i).start()

    def src(i):
        name, a, c, r = chunks[i]
        if name == "skip":
            return pskip.at[pl.ds(c * r, r)]
        if name == "qkv":
            return pqkv.at[a, pl.ds(c * r, r)]
        if name == "o":
            return po.at[c]
        return pc.at[:, pl.ds(c * r, r)]

    def place(i):
        name, a, c, r = chunks[i]
        return {"skip": lskip, "qkv": lqkv.at[a], "o": lo_, "ff": land}[name].at[c]

    def plane(i, s, k):
        if chunks[i][0] in ("skip", "qkv"):
            return place(i).at[s, k]
        return place(i).at[s, :, k]

    net = Spread(nz, len(chunks), src, place, plane, sems, LAGS)
    z, slot = net.z, net.slot
    count = lambda name: sum(c[0] == name for c in chunks)
    ns, nq, no_, nf = count("skip"), count("qkv") // 3, count("o"), count("ff")
    results = {
        "hid": (hid_ref, h_hid),
        "norm": (norm_ref, h_norm),
        "q": (q_ref, h_q),
        "k": (k_ref, h_k),
        "v": (v_ref, h_v),
        "row": (row_ref, h_row),
        "att": (norm_ref, h_att),
        "gm": (gm_ref, h_gm),
        "ga": (k_ref, h_ga),
        "out": (out_ref, h_out),
    }
    order = list(results)

    def put(name):
        return pltpu.make_async_copy(*results[name], out_sem.at[order.index(name)])

    small_ref[z] = vec_ref[...]
    fetch(0).wait()
    pskip[...] = wskip_ref[aligned(slot * rs, rs), :].astype(F32)
    net.barrier()
    net.tick()

    def vec(k, zz):
        return remote(vec_ref, small_ref.at[zz], vs.at[k - 1], vr.at[k - 1], net.far[k])

    for k in range(1, nz):
        vec(k, z).start()
    net.tick()
    for i in (1, 2, 3, 4):
        fetch(i).wait()
    for a, w in enumerate((wq_ref, wk_ref, wv_ref)):
        pqkv[a] = w[aligned(slot * rq, rq), :].astype(F32)
    ro = loc // GROUP
    po[...] = wo_ref[aligned(slot * ro, ro), :].astype(F32).reshape(po.shape)
    net.tick()
    for k in range(1, nz):
        vec(k, lax.rem(z + k, nz)).wait_recv()
    for i in (5, 6):
        fetch(i).wait()

    def hidden_cols(w, zz):
        bias = small_ref[zz, :, nm : nm + loc]
        cols = aligned(zz * loc, loc)

        @pl.loop(0, t // TB)
        def _(b):
            rows = aligned(b * TB, TB)
            acc = dot(x_ref[rows, :], w[:d, :]) + dot(y_ref[rows, :], w[d:, :])
            hid_ref[rows, cols] = acc + bias

        row_ref[:loc, cols] = w[aligned(z * loc, loc), :]
        row_ref[loc:, cols] = w[aligned(d + z * loc, loc), :]

    net.tick()
    hidden_cols(wskip_ref, z)
    for i in (9, 10):
        fetch(i).wait()
    pc[0] = up_ref[:, aligned(slot * pr, pr)].astype(F32).T
    pc[1] = dn_ref[aligned(slot * pr, pr), :].astype(F32)
    na = 0

    def stage_a(ref):
        nonlocal na
        c = pltpu.make_async_copy(ref, sta.at[na % 2], sa_sem.at[na % 2])
        c.start()
        c.wait()
        na += 1
        return sta.at[(na - 1) % 2]

    r = rs // ns
    for c in range(ns):
        net.until(c)
        st = stage_a(lskip.at[c])
        for k in range(kk):
            for s in range(GROUP):
                wb[k, s * rs + c * r : s * rs + (c + 1) * r, :] = st[s, k].astype(BF16)
    for k in range(1, nz):
        hidden_cols(wb.at[k - 1], lax.rem(z + k, nz))
        net.tick()
    put("row").start()

    shift1, scale1 = flat(small_ref, nm, 0, d), flat(small_ref, nm, d, 2 * d)

    @pl.loop(0, t // LB)
    def _(b):
        rows = aligned(b * LB, LB)
        xn, _ = layer_norm(hid_ref[rows, :])
        norm_ref[rows, :] = (xn * (1.0 + scale1) + shift1).astype(BF16)

    put("hid").start()
    put("norm").start()
    net.tick()
    for i in (7, 8):
        fetch(i).wait()

    def project(a, k, w):
        out = (q_ref, k_ref, v_ref)[a]

        @pl.loop(0, t // TB)
        def _(b):
            rows = aligned(b * TB, TB)
            u = dot(norm_ref[rows, :], w[...])
            if a < 2:
                u = u * wide(cos_ref[rows, :], loc) + swap_halves(u) * wide(sin_ref[rows, :], loc)
            if a == 0:
                u = u.astype(BF16).astype(F32) * (HEAD_DIM**-0.5)
            out[rows, k * loc : (k + 1) * loc] = u.astype(BF16)

    for a in range(3):
        project(a, 0, (wq_ref, wk_ref, wv_ref)[a])
        net.tick()
    r = rq // nq

    def w_out(a):
        return pltpu.make_async_copy(
            wb.at[:, pl.ds((a % 2) * d, d)], h_w16.at[:, a], w_sem.at[a % 2]
        )

    for a in range(3):
        if a == 2:
            w_out(0).wait()
        base = (a % 2) * d
        for c in range(nq):
            net.until(ns + nq * a + c)
            st = stage_a(lqkv.at[a, c])
            for k in range(kk):
                for s in range(GROUP):
                    at = base + s * rq + c * r
                    wb[k, at : at + r, :] = st[s, k].astype(BF16)
        for k in range(1, nz):
            project(a, k, wb.at[k - 1, pl.ds(base, d)])
        net.tick()
        w_out(a).start()
        put("qkv"[a]).start()

    put("norm").wait()
    qb = 256
    nb = t // qb
    lane = lax.broadcasted_iota(jnp.int32, (qb, loc), 1) // HEAD_DIM
    for g in range(nz):
        gc = slice(g * loc, (g + 1) * loc)
        vt_ref[...] = v_ref[:, gc].T
        for j in range(nb):
            kj = k_ref[j * qb : (j + 1) * qb, gc]
            for h in range(heads):
                x_ref[h * qb : (h + 1) * qb, j * qb : (j + 1) * qb] = jnp.where(
                    lane == h, kj, jnp.zeros_like(kj)
                )

        @pl.loop(0, nb)
        def _(i):
            rows = aligned(i * qb, qb)
            qi = q_ref[rows, gc]
            segq = segq_ref[0, pl.ds(0, 1), rows]

            def first(j, mx):
                at = aligned(j * qb, qb)
                s = dot(x_ref[:, at], qi, NT)
                same = wide(segk_ref[at, :], qb) == segq
                out = []
                for h in range(heads):
                    sh = jnp.where(same, s[h * qb : (h + 1) * qb], NEG)
                    f1_ref[at, h * qb : (h + 1) * qb] = sh
                    out.append(
                        jnp.maximum(mx[h], jnp.max(sh.reshape(qb // 8, 8, qb), axis=0))
                    )
                return out

            mx = lax.fori_loop(0, nb, first, [jnp.full((8, qb), NEG, F32)] * heads)
            ms = [jnp.max(m, axis=0, keepdims=True) for m in mx]

            def second(j, carry):
                ls, os_ = carry
                at = aligned(j * qb, qb)
                nl, nx = [], []
                for h in range(heads):
                    p = jnp.exp(f1_ref[at, h * qb : (h + 1) * qb] - ms[h])
                    nl.append(ls[h] + jnp.sum(p.reshape(qb // 8, 8, qb), axis=0))
                    vt = vt_ref[pl.ds(h * HEAD_DIM, HEAD_DIM), at]
                    nx.append(os_[h] + dot(vt, p.astype(BF16)))
                return nl, nx

            ls, os_ = lax.fori_loop(
                0,
                nb,
                second,
                ([jnp.zeros((8, qb), F32)] * heads, [jnp.zeros((HEAD_DIM, qb), F32)] * heads),
            )
            l1 = [jnp.sum(v, axis=0, keepdims=True) for v in ls]
            o = jnp.concatenate([os_[h] / l1[h] for h in range(heads)], axis=0)
            norm_ref[rows, gc] = o.astype(BF16).T
            lse = [ms[h] + jnp.log(l1[h]) for h in range(heads)]
            lse_ref[g, :, rows] = jnp.concatenate(lse + [jnp.zeros((8 - heads, qb), F32)], axis=0)

        net.tick()
    att_ref, br_ref, gf_ref, n2_ref, gb_ref, ga_ref = norm_ref, f1_ref, x_ref, y_ref, q_ref, k_ref
    put("att").start()

    net.until(ns + 3 * nq + no_ - 1)
    nbuf = 0

    def stage_b(ref):
        nonlocal nbuf
        c = pltpu.make_async_copy(ref, stb.at[nbuf % 2], sb_sem.at[nbuf % 2])
        c.start()
        c.wait()
        nbuf += 1
        return stb.at[(nbuf - 1) % 2]

    for c in range(no_):
        st = stage_b(lo_.at[c])
        for k in range(kk):
            for s in range(GROUP):
                at = s * ro + c * 2 * R_B
                o16_ref[k, at : at + 2 * R_B, :] = jnp.concatenate(
                    [st[s, 0, k], st[s, 1, k]], axis=0
                ).astype(BF16)
    row = lambda i: flat(small_ref, nm, i * d, (i + 1) * d)
    gate1, shift2, scale2, gate2 = row(2), row(3), row(4), row(5)

    @pl.loop(0, t // TB)
    def _(b):
        rows = aligned(b * TB, TB)
        br_ref[rows, :] = dot(att_ref[rows, :loc], wo_ref[...]) + dot(
            att_ref[rows, loc:], o16_ref[...].reshape(kk * loc, d)
        )

    sums_ref[...] = jnp.zeros_like(sums_ref)
    fetch(11).wait()

    @pl.loop(0, t // LB)
    def _(b):
        rows = aligned(b * LB, LB)
        x2, _ = layer_norm(hid_ref[rows, :] + gate1 * br_ref[rows, :])
        n2_ref[rows, :] = (x2 * (1.0 + scale2) + shift2).astype(BF16)
        go = go_ref[rows, :].astype(F32)
        sums_ref[3:4, :] += jnp.sum(go, axis=0, keepdims=True)
        gf_ref[rows, :] = (gate2 * go).astype(BF16)

    net.tick()

    own = aligned(z * loc, loc)

    def units(first_time, rows, pre, dnv, back):
        act, slope = gelu_parts(pre)
        act = act.astype(BF16)
        ffn = dot(act, dnv[:, own])
        g_pre = (dot(gf_ref[rows, :], dnv[...], NT) * slope).astype(BF16)
        gn = back(g_pre)
        if first_time:
            out_ref[rows, :] = ffn
            gm_ref[rows, :] = gn
        else:
            out_ref[rows, :] += ffn
            gm_ref[rows, :] += gn
        return act, g_pre

    parts = 4
    sub = fl // parts
    gwc = lambda j, s: pltpu.make_async_copy(
        gws.at[s], gw_ref.at[pl.ds(s * fl + j * sub, sub)], gw_sem.at[s]
    )
    for j in range(parts):
        cs = slice(j * sub, (j + 1) * sub)

        @pl.loop(0, t // TB)
        def _(b):
            rows = aligned(b * TB, TB)
            pre = dot(n2_ref[rows, :], up_ref[:, cs]) + bup_ref[:, cs]
            a, g = units(
                j == 0, rows, pre, dn_ref.at[cs, :], lambda gp: dot(gp, up_ref[:, cs], NT)
            )
            act_s[rows, :] = a
            gp_s[rows, :] = g

        if j > 0:
            for s in range(2):
                gwc(j - 1, s).wait()
        gbu_ref[:, cs] = jnp.sum(gp_s[...].astype(F32), axis=0, keepdims=True)
        gws[0] = dot(gp_s[...], n2_ref[...], TN)
        gws[1] = dot(act_s[...], gf_ref[...], TN)
        for s in range(2):
            gwc(j, s).start()
        net.tick()
    at = 0
    f0 = ns + 3 * nq + no_
    for per in STEPS:
        w = per * GROUP * R_B
        for c in range(per):
            net.until(f0 + at + c)
            st = stage_b(land.at[at + c])
            u = GROUP * R_B
            for k in range(kk):
                for half, dst in ((0, ub), (1, db)):
                    dst[k * w + c * u : k * w + (c + 1) * u, :] = jnp.concatenate(
                        [st[s, half, k] for s in range(GROUP)], axis=0
                    ).astype(BF16)
        bias = []
        for k in range(kk):
            lo = nm + loc + at * GROUP * R_B
            bias.append(small_ref[lax.rem(z + k + 1, nz), :, lo : lo + w])
        bias = jnp.concatenate(bias, axis=1)
        w = w * kk

        @pl.loop(0, t // TB)
        def _(b):
            rows = aligned(b * TB, TB)
            pre = dot(n2_ref[rows, :], ub[:w, :], NT) + bias
            units(False, rows, pre, db.at[:w, :], lambda gp: dot(gp, ub[:w, :]))

        if net.t < net.n + net.lags[3]:
            net.tick()
        at += per

    put("q").wait()
    put("k").wait()
    bdn = bdn_ref[:, own]
    stb[0, 0, 0, 0, 0:1] = gate1
    stb[0, 0, 0, 1, 0:1] = gate2
    gate1_own = stb[0, 0, 0, 0, 0:1, own]
    gate2_own = stb[0, 0, 0, 1, 0:1, own]
    gg2_ref[...] = jnp.zeros_like(gg2_ref)

    @pl.loop(0, t // LB)
    def _(b):
        rows = aligned(b * LB, LB)
        ffn = out_ref[rows, :] + bdn
        gg2_ref[...] += jnp.sum(go_ref[rows, own].astype(F32) * ffn, axis=0, keepdims=True)
        out_ref[rows, :] = hid_ref[rows, own] + gate1_own * br_ref[rows, own] + gate2_own * ffn
        br = br_ref[rows, :]
        x2, r2 = layer_norm(hid_ref[rows, :] + gate1 * br)
        gn = gm_ref[rows, :]
        sums_ref[0:1, :] += jnp.sum(gn, axis=0, keepdims=True)
        sums_ref[1:2, :] += jnp.sum(gn * x2, axis=0, keepdims=True)
        gp = gn * (1.0 + scale2)
        gm = go_ref[rows, :].astype(F32) + r2 * (
            gp
            - jnp.mean(gp, axis=-1, keepdims=True)
            - x2 * jnp.mean(gp * x2, axis=-1, keepdims=True)
        )
        gm_ref[rows, :] = gm
        sums_ref[2:3, :] += jnp.sum(gm * br, axis=0, keepdims=True)
        gb_ref[rows, :] = (gate1 * gm).astype(BF16)

    put("gm").start()
    put("out").start()

    @pl.loop(0, t // TB)
    def _(b):
        rows = aligned(b * TB, TB)
        ga_ref[rows, :loc] = dot(gb_ref[rows, :], wo_ref[...], NT).astype(BF16)
        ga_ref[rows, loc:] = dot(
            gb_ref[rows, :], o16_ref[...].reshape(kk * loc, d), NT
        ).astype(BF16)

    put("ga").start()
    for s in range(2):
        gwc(parts - 1, s).wait()
    gws[0, :loc, :] = dot(att_ref[:, :loc], gb_ref[...], TN)
    last = lambda: pltpu.make_async_copy(
        gws.at[0, pl.ds(0, loc)], gw_ref.at[pl.ds(2 * fl, loc)], gw_sem.at[0]
    )
    last().start()
    net.drain()
    for k in range(1, nz):
        vec(k, z).wait_send()
    w_out(1).wait()
    w_out(2).wait()
    last().wait()
    for name in ("hid", "v", "row", "att", "gm", "ga", "out"):
        put(name).wait()


def forward(x, y, go, wskip, wq, wk, wv, wo, up, dn, vec, bup, bdn, cos, sin, segq, segk, nz):
    t, d = x.shape
    loc = wq.shape[1]
    fl = up.shape[1]
    kk = nz - 1
    rs, rq, ro = 2 * d // GROUP, d // GROUP, loc // GROUP
    ns, nq, no = 4, 2, ro // (2 * R_B)
    nf = fl // GROUP // R_B
    chunks = [("skip", 0, c, rs // ns) for c in range(ns)]
    chunks += [("qkv", a, c, rq // nq) for a in range(3) for c in range(nq)]
    chunks += [("o", 0, c, 2 * R_B) for c in range(no)]
    chunks += [("ff", 0, c, R_B) for c in range(nf)]
    sd = jax.ShapeDtypeStruct
    dma = pltpu.SemaphoreType.DMA
    ins = [wskip, wq, wk, wv, wo, x, y, cos, sin, up, dn, go]
    e = nz * loc
    per = max(STEPS)
    nu = per * kk * GROUP * R_B
    outs = [
        sd((t, d), F32),
        sd((t, d), BF16),
        sd((t, e), BF16),
        sd((t, e), BF16),
        sd((t, e), BF16),
        sd((kk, 3, d, loc), BF16),
        sd((2 * loc, d), BF16),
        sd((t, e), BF16),
        sd((t, d), F32),
        sd((t, e), BF16),
        sd((t, loc), F32),
    ]
    more = [
        sd((2 * fl + loc, d), F32),
        sd((ns, GROUP, kk, rs // ns, loc), F32),
        sd((3, nq, GROUP, kk, rq // nq, loc), F32),
        sd((no, GROUP, 2, kk, R_B, d), F32),
        sd((nf, GROUP, 2, kk, R_B, d), F32),
    ]
    small = [
        sd((nz,) + vec.shape, F32),
        sd((nz, 8, t), F32),
        sd((8, d), F32),
        sd((1, fl), F32),
        sd((1, loc), F32),
    ]
    scratch = [pltpu.VMEM(v.shape, v.dtype) for v in ins]
    scratch += [
        pltpu.VMEM((t, d), F32),
        pltpu.VMEM((t, d), BF16),
        pltpu.VMEM((t, e), BF16),
        pltpu.VMEM((t, e), BF16),
        pltpu.VMEM((t, e), BF16),
        pltpu.VMEM((t, d), F32),
        pltpu.VMEM((t, d), F32),
        pltpu.VMEM((t, loc), F32),
        pltpu.VMEM((kk, 2 * d, loc), BF16),
        pltpu.VMEM((kk, loc, d), BF16),
        pltpu.VMEM((2 * loc, d), BF16),
        pltpu.VMEM((2, GROUP, kk, rs // ns, loc), F32),
        pltpu.VMEM((2, GROUP, 2, kk, R_B, d), F32),
        pltpu.VMEM((rs, loc), F32),
        pltpu.VMEM((3, rq, loc), F32),
        pltpu.VMEM((no, 2, R_B, d), F32),
        pltpu.VMEM((2, fl // GROUP, d), F32),
        pltpu.VMEM((nu, d), BF16),
        pltpu.VMEM((nu, d), BF16),
        pltpu.VMEM((t, fl // 4), BF16),
        pltpu.VMEM((t, fl // 4), BF16),
        pltpu.VMEM((2, max(fl // 4, loc), d), F32),
        pltpu.VMEM((loc, t), BF16),
        dma((len(ins),)),
        dma((10,)),
        dma((2,)),
        dma((2,)),
        dma((2,)),
        dma((2,)),
        dma((kk,)),
        dma((kk,)),
    ] + spread_sems(nz, len(chunks))
    return pl.pallas_call(
        functools.partial(forward_kernel, nz, chunks),
        out_shape=outs + more + small,
        in_specs=[ANY] * len(ins) + [VMEM] * 5,
        out_specs=[ANY] * (len(outs) + len(more)) + [VMEM] * 5,
        scratch_shapes=scratch,
        compiler_params=pltpu.CompilerParams(
            collective_id=0, has_side_effects=True, vmem_limit_bytes=63 << 20
        ),
    )(*ins, vec, bup, bdn, segq, segk)


class Halving:
    def __init__(self, ndp, src, out, refs, mine, partner):
        self.bits = ndp.bit_length() - 1
        self.ndp, self.src, self.out, self.mine, self.partner = ndp, src, out, mine, partner
        self.recv0, self.lev0, self.s0, self.r0 = refs[:4]
        self.rest = refs[4:]
        self.cw = src.shape[2] // 2
        self.orders = [list(range(1, self.bits)), list(range(self.bits - 1, 0, -1))]
        self.step = -1
        self.sent = []

    def _first(self, i):
        give = 2 * i + 1 - self.mine[0]
        return remote(
            self.src.at[give], self.recv0.at[i], self.s0.at[i], self.r0.at[i], self.partner[0]
        )

    def start(self):
        for i in range(self.ndp // 2):
            self._first(i).start()

    def _items(self, h):
        src, free = self.state[h]
        b = self.orders[h][self.step]
        at = free.index(b)
        lo = 1 << at
        left = [f for f in free if f != b]
        recv, out, ss, rr = self.rest[4 * (2 * self.step + h) : 4 * (2 * self.step + h) + 4]
        items = []
        for i in range(1 << len(left)):
            base = (i // lo) * 2 * lo + i % lo
            give = base + lo * (1 - self.mine[b])
            keep = base + lo * self.mine[b]
            c = functools.partial(
                remote, src.at[give], recv.at[i], ss.at[i], rr.at[i], self.partner[b]
            )
            items.append((c, keep, i))
        return items, src, recv, out, left

    def advance(self):
        if self.step < 0:
            for i in range(self.ndp // 2):
                self._first(i).wait_recv()
                self.lev0[i] = self.src[2 * i + self.mine[0]] + self.recv0[i]
            free = list(range(1, self.bits))
            self.state = [(self.lev0.at[:, :, pl.ds(h * self.cw, self.cw)], free) for h in (0, 1)]
        else:
            for h in (0, 1):
                items, src, recv, out, left = self.now[h]
                for c, keep, i in items:
                    c().wait_recv()
                    total = src[keep] + recv[i]
                    if self.step == self.bits - 2:
                        self.out[:, pl.ds(h * self.cw, self.cw)] = total
                    else:
                        out[i] = total
                    self.sent.append(c)
                self.state[h] = (out, left)
        self.step += 1
        if self.step < self.bits - 1:
            self.now = [self._items(h) for h in (0, 1)]
            for h in (0, 1):
                for c, _, _ in self.now[h][0]:
                    c().start()

    def finish(self):
        while self.step < self.bits - 1:
            self.advance()

    def drain(self):
        for c in self.sent:
            c().wait_send()
        for i in range(self.ndp // 2):
            self._first(i).wait_send()


def halving_refs(ndp, r, c):
    dma = pltpu.SemaphoreType.DMA
    bits = ndp.bit_length() - 1
    half = ndp // 2
    out = [pltpu.VMEM((half, r, c), F32), pltpu.VMEM((half, r, c), F32), dma((half,)), dma((half,))]
    for step in range(bits - 1):
        n = ndp >> (step + 2)
        for _ in range(2):
            out += [pltpu.VMEM((n, r, c // 2), F32), pltpu.VMEM((n, r, c // 2), F32), dma((n,)), dma((n,))]
    return out


def third_kernel(ndp, nz, nh, *refs):
    ni = 13
    ins = refs[:ni]
    small_ref, sums_ref, gbu_ref, gg2_ref, emb_ref = refs[ni : ni + 5]
    sqkv_ref, sskip_ref, all_ref, tot_ref = refs[ni + 5 : ni + 9]
    hbm = refs[ni + 9 : ni + 11]
    rest = refs[ni + 11 :]
    vmem_in = rest[:ni]
    (norm_ref, gq_ref, gk_ref, gv_ref, wq_ref, wk_ref, wv_ref, w_ref) = vmem_in[:8]
    (hid_ref, gm_ref, x_ref, y_ref, row_ref) = vmem_in[8:]
    gf_ref, gs_ref, gn_ref, low_ref, gwq, gws, vec, gz, mod_s = rest[ni : ni + 9]
    in_sem, out_sem, z_send, z_recv, q_send, q_recv = rest[ni + 9 : ni + 15]
    h1 = rest[ni + 15 : ni + 15 + nh]
    h2 = rest[ni + 15 + nh :]
    t, d = hid_ref.shape
    loc = wq_ref.shape[1]
    fl = gbu_ref.shape[1]
    nm = 6 * d // nz
    dp = lax.axis_index("dp")
    z = lax.axis_index("tensor")

    def fetch(i):
        return pltpu.make_async_copy(ins[i], vmem_in[i], in_sem.at[i])

    for i in range(ni):
        fetch(i).start()
    bits = ndp.bit_length() - 1
    mine = [lax.rem(dp // (1 << b), 2) for b in range(bits)]
    partner = [(dp + (1 << b) * (1 - 2 * mine[b]), z) for b in range(bits)]
    others = lambda j: (lax.rem(dp + j, ndp), z)
    bar = pltpu.get_barrier_semaphore()
    for j in range(1, ndp):
        pl.semaphore_signal(bar, inc=1, device_id=others(j), device_id_type=MESH)
    for k in range(1, nz):
        pl.semaphore_signal(
            bar, inc=1, device_id=(dp, lax.rem(z + k, nz)), device_id_type=MESH
        )
    grads = (gq_ref, gk_ref, gv_ref)
    for i in range(4):
        fetch(i).wait()
    for a in range(3):
        gwq[:, :, a * loc : (a + 1) * loc] = dot(
            norm_ref[...], grads[a][:, :loc], TN
        ).reshape(ndp, d // ndp, loc)
    pl.semaphore_wait(bar, ndp - 1 + nz - 1)
    one = Halving(ndp, gwq, sqkv_ref, h1, mine, partner)
    one.start()

    def part(k, zz):
        return remote(
            gg2_ref, gz.at[zz], z_send.at[k - 1], z_recv.at[k - 1], (dp, lax.rem(z + nz - k, nz))
        )

    for k in range(1, nz):
        part(k, z).start()
    gz[z] = gg2_ref[...]
    for i in range(4, 8):
        fetch(i).wait()
    own = (wq_ref, wk_ref, wv_ref)

    def product(b):
        rows = pl.ds(b * TB, TB)
        acc = dot(gq_ref[rows, :loc], wq_ref[...], NT)
        for k in range(nz):
            for a in range(3):
                if k == 0 and a == 0:
                    continue
                w = own[a][...] if k == 0 else w_ref[k - 1, a]
                acc = acc + dot(grads[a][rows, k * loc : (k + 1) * loc], w, NT)
        gn_ref[rows, :] = acc

    for b in range(t // TB):
        product(b)
        if b == 0:
            one.advance()
    one.advance()
    scale1 = flat(small_ref, nm, d, 2 * d)
    mod_s[...] = jnp.zeros_like(mod_s)
    for i in (8, 9):
        fetch(i).wait()

    @pl.loop(0, t // LB)
    def _(b):
        rows = aligned(b * LB, LB)
        x1, r1 = layer_norm(hid_ref[rows, :])
        gn = gn_ref[rows, :]
        mod_s[:, :d] += jnp.sum(gn, axis=0, keepdims=True)
        mod_s[:, d : 2 * d] += jnp.sum(gn * x1, axis=0, keepdims=True)
        gp = gn * (1.0 + scale1)
        gh = gm_ref[rows, :] + r1 * (
            gp
            - jnp.mean(gp, axis=-1, keepdims=True)
            - x1 * jnp.mean(gp * x1, axis=-1, keepdims=True)
        )
        mod_s[:, 6 * d :] += jnp.sum(gh, axis=0, keepdims=True)
        low_ref[rows, :] = gh.astype(BF16)

    one.advance()
    for i in (10, 11, 12):
        fetch(i).wait()
    cols = aligned(z * loc, loc)
    low_own = low_ref[:, cols]
    half = ndp // 2
    gws[:half] = dot(x_ref[...], low_own, TN).reshape(half, 2 * d // ndp, loc)
    gws[half:] = dot(y_ref[...], low_own, TN).reshape(half, 2 * d // ndp, loc)
    two = Halving(ndp, gws, sskip_ref, h2, mine, partner)
    two.start()
    for k in range(1, nz):
        part(k, lax.rem(z + k, nz)).wait_recv()
    gate2 = flat(small_ref, nm, 5 * d, 6 * d)
    mod_s[:, 2 * d : 3 * d] = sums_ref[2:3, :]
    mod_s[:, 3 * d : 4 * d] = sums_ref[0:1, :]
    mod_s[:, 4 * d : 5 * d] = sums_ref[1:2, :]
    for zz in range(nz):
        mod_s[:, 5 * d + zz * loc : 5 * d + (zz + 1) * loc] = gz[zz]
    o = nm
    vec[:, :o] = mod_s[:, aligned(z * nm, nm)]
    vec[:, o : o + loc] = mod_s[:, pl.ds(pl.multiple_of(6 * d + z * loc, loc), loc)]
    o += loc
    vec[:, o : o + fl] = gbu_ref[...]
    o += fl
    vec[:, o : o + d] = gate2 * sums_ref[3:4, :]
    o += d
    vec[:, o : o + d] = emb_ref[...]
    all_ref[dp] = vec[...]

    def give(j, row):
        return remote(vec, all_ref.at[row], q_send.at[j - 1], q_recv.at[j - 1], others(j))

    for j in range(1, ndp):
        give(j, dp).start()

    outs = (gf_ref, gs_ref)

    def put(i):
        return pltpu.make_async_copy(outs[i], hbm[i], out_sem.at[i])

    def back(i):
        w = row_ref[i * loc : (i + 1) * loc, :]
        for b in range(t // TB):
            rows = pl.ds(b * TB, TB)
            outs[i][rows, :] = dot(low_ref[rows, :], w, NT)
        put(i).start()

    two.advance()
    back(0)
    two.advance()
    one.finish()
    back(1)
    two.finish()
    for j in range(1, ndp):
        give(j, lax.rem(dp + ndp - j, ndp)).wait_recv()
    tot_ref[...] = jnp.sum(all_ref[...], axis=0)
    one.drain()
    two.drain()
    for k in range(1, nz):
        part(k, z).wait_send()
    for j in range(1, ndp):
        give(j, dp).wait_send()
    for i in range(2):
        put(i).wait()


def third(norm, gq, gk, gv, wq, wk, wv, w, hid, gm, x, y, row, small, sums, gbu, gg2, emb, ndp, nz):
    t, d = hid.shape
    loc = wq.shape[1]
    fl = gbu.shape[1]
    n = 6 * d // nz + loc + fl + 2 * d
    sd = jax.ShapeDtypeStruct
    dma = pltpu.SemaphoreType.DMA
    ins = [norm, gq, gk, gv, wq, wk, wv, w, hid, gm, x, y, row]
    scratch = [pltpu.VMEM(v.shape, v.dtype) for v in ins]
    scratch += [
        pltpu.VMEM((t, loc), F32),
        pltpu.VMEM((t, loc), F32),
        pltpu.VMEM((t, d), F32),
        pltpu.VMEM((t, d), BF16),
        pltpu.VMEM((ndp, d // ndp, 3 * loc), F32),
        pltpu.VMEM((ndp, 2 * d // ndp, loc), F32),
        pltpu.VMEM((1, n), F32),
        pltpu.VMEM((nz, 1, loc), F32),
        pltpu.VMEM((1, 7 * d), F32),
        dma((len(ins),)),
        dma((2,)),
        dma((nz - 1,)),
        dma((nz - 1,)),
        dma((ndp - 1,)),
        dma((ndp - 1,)),
    ]
    h1 = halving_refs(ndp, d // ndp, 3 * loc)
    h2 = halving_refs(ndp, 2 * d // ndp, loc)
    return pl.pallas_call(
        functools.partial(third_kernel, ndp, nz, len(h1)),
        out_shape=[
            sd((d // ndp, 3 * loc), F32),
            sd((2 * d // ndp, loc), F32),
            sd((ndp, 1, n), F32),
            sd((1, n), F32),
            sd((t, loc), F32),
            sd((t, loc), F32),
        ],
        in_specs=[ANY] * len(ins) + [VMEM] * 5,
        out_specs=[VMEM] * 4 + [ANY] * 2,
        scratch_shapes=scratch + h1 + h2,
        compiler_params=pltpu.CompilerParams(
            collective_id=1, has_side_effects=True, vmem_limit_bytes=62 << 20
        ),
    )(*ins, small, sums, gbu, gg2, emb)


def wide(table, lanes):
    return jnp.concatenate([table] * (lanes // 128), axis=1)


def swap_halves(u):
    n = u.shape[1]
    lane = lax.broadcasted_iota(jnp.int32, u.shape, 1)
    half = HEAD_DIM // 2
    return jnp.where(
        lane % HEAD_DIM < half, pltpu.roll(u, n - half, 1), pltpu.roll(u, half, 1)
    )


QB = 256
KB = 256


def stack_heads(dst, src, heads):
    lane = lax.broadcasted_iota(jnp.int32, src.shape, 1) // HEAD_DIM
    for h in range(heads):
        dst[:, h] = jnp.where(lane == h, src, jnp.zeros_like(src)).reshape(dst.shape[0], dst.shape[2], dst.shape[3])

def bwd_kernel(heads, QB, KB, lo_ref, hi_ref, q_ref, k_ref, v_ref, att_ref, g_ref, lse_ref, segq_ref, segk_ref, cos_ref, sin_ref, gq_ref, gk_ref, gv_ref,
               kt_ref, ks_ref, vs_ref, dk_ref, dv_ref):
    t, e = k_ref.shape
    kt_ref[...] = k_ref[...].T
    stack_heads(ks_ref, k_ref[...], heads)
    stack_heads(vs_ref, v_ref[...], heads)
    dk_ref[...] = jnp.zeros_like(dk_ref); dv_ref[...] = jnp.zeros_like(dv_ref)
    row = lax.broadcasted_iota(jnp.int32, (8, e), 0); lane = lax.broadcasted_iota(jnp.int32, (8, e), 1)
    ind = jnp.where(lane//HEAD_DIM == row, 1.0, 0.0).astype(F32)
    lanek = lax.broadcasted_iota(jnp.int32, (KB, e), 1)//HEAD_DIM
    @pl.loop(0, t//QB)
    def _(i):
        qs = pl.multiple_of(i*QB, QB)
        q = q_ref[pl.ds(qs, QB), :]; g = g_ref[pl.ds(qs, QB), :]
        segq = segq_ref[0, pl.ds(0,1), pl.ds(qs, QB)]
        prod = g.astype(F32)*att_ref[pl.ds(qs, QB), :].astype(F32)
        delta = dot(ind, prod, NT, lax.Precision.HIGHEST)
        lse = lse_ref[0, :, pl.ds(qs, QB)]
        def body(j, dq):
            start = pl.multiple_of(j*KB, KB)
            s = dot(ks_ref[j].reshape(heads*KB, e), q, NT)
            dpt = dot(vs_ref[j].reshape(heads*KB, e), g, NT)
            segk = segk_ref[pl.ds(start, KB), :]
            same = jnp.concatenate([segk]*(QB//128), axis=1) == segq
            ps, dss, ndq = [], [], []
            for h in range(heads):
                p = jnp.exp(jnp.where(same, s[h*KB:(h+1)*KB], NEG) - lse[h:h+1])
                ds = (p*(dpt[h*KB:(h+1)*KB] - delta[h:h+1])).astype(BF16)
                ps.append(p.astype(BF16)); dss.append(ds)
                kt = kt_ref[pl.ds(h*HEAD_DIM, HEAD_DIM), pl.ds(start, KB)]
                ndq.append(dq[h] + dot(kt, ds))
            dvs = dot(jnp.concatenate(ps, axis=0), g)
            dks = dot(jnp.concatenate(dss, axis=0), q)
            dv, dk = dvs[:KB], dks[:KB]
            for h in range(1, heads):
                dv = jnp.where(lanek == h, dvs[h*KB:(h+1)*KB], dv)
                dk = jnp.where(lanek == h, dks[h*KB:(h+1)*KB], dk)
            dk_ref[pl.ds(start, KB), :] += dk
            dv_ref[pl.ds(start, KB), :] += dv
            return ndq
        dq = lax.fori_loop(lo_ref[i], hi_ref[i], body, [jnp.zeros((HEAD_DIM, QB), F32)]*heads)
        dqf = jnp.concatenate(dq, axis=0).T * (HEAD_DIM**-0.5)
        cos = wide(cos_ref[pl.ds(qs, QB), :], e)
        sin = wide(sin_ref[pl.ds(qs, QB), :], e)
        gq_ref[pl.ds(qs, QB), :] = (dqf*cos - swap_halves(dqf)*sin).astype(BF16)
    dk = dk_ref[...]
    gk_ref[...] = (dk * wide(cos_ref[...], e) - swap_halves(dk) * wide(sin_ref[...], e)).astype(BF16)
    gv_ref[...] = dv_ref[...].astype(BF16)

def attn_bwd(q,k,v,att,g,lse,seg_row,seg_col,lo,hi,cos,sin,groups,QB=QB,KB=KB):
    t = q.shape[0]; e = q.shape[1]//groups; heads = e//HEAD_DIM
    col = pl.BlockSpec((t,e), lambda g,*_: (0,g)); full = lambda s: pl.BlockSpec(s, lambda g,*_: (0,0))
    return pl.pallas_call(functools.partial(bwd_kernel, heads, QB, KB), out_shape=[jax.ShapeDtypeStruct(q.shape,BF16)]*3,
        grid_spec=pltpu.PrefetchScalarGridSpec(num_scalar_prefetch=2, grid=(groups,),
            in_specs=[col]*5+[pl.BlockSpec((1,8,t), lambda g,*_: (g,0,0)), pl.BlockSpec((1,8,t), lambda g,*_: (0,0,0)), full((t,128)), full((t,128)), full((t,128))],
            out_specs=[col]*3,
            scratch_shapes=[pltpu.VMEM((e,t),BF16), pltpu.VMEM((t//KB,heads,KB,e),BF16), pltpu.VMEM((t//KB,heads,KB,e),BF16), pltpu.VMEM((t,e),F32), pltpu.VMEM((t,e),F32)]),
        compiler_params=pltpu.CompilerParams(vmem_limit_bytes=58<<20))(lo,hi,q,k,v,att,g,lse,seg_row,seg_col,cos,sin)


def time_freqs(width):
    half = width // 2
    return jnp.exp(-math.log(10000.0) * jnp.arange(half, dtype=F32) / half)


def time_embed(flow_time, width):
    angles = 1000.0 * flow_time[:, None] * time_freqs(width)[None, :]
    both = jnp.concatenate([jnp.cos(angles), jnp.sin(angles)], axis=1)
    return jax.nn.silu(both).astype(BF16)


def per_device(ndp, nz, *args):
    (
        frames,
        skip_in,
        flow_time,
        segment_ids,
        w_skip,
        b_skip,
        w_mod,
        b_mod,
        w_q,
        w_k,
        w_v,
        w_o,
        w_up,
        b_up,
        w_dn,
        b_dn,
        out_grad,
    ) = args
    t, d = frames.shape
    loc = w_q.shape[1]
    fl = w_up.shape[1]
    dp = lax.axis_index("dp")
    z = lax.axis_index("tensor")
    embed = time_embed(flow_time, d)
    mod_part = dot(embed, w_mod)[0] + b_mod
    bup_order = b_up.reshape(GROUP, fl // GROUP // R_B, R_B).transpose(1, 0, 2).reshape(-1)
    own_small = jnp.concatenate([mod_part, b_skip, bup_order])[None, :]

    seg = segment_ids[0]
    idx = jnp.arange(t, dtype=jnp.int32)
    nseg = 4
    starts = [jnp.sum((seg < s).astype(jnp.int32)) for s in range(1, nseg)]
    first_at = jnp.zeros_like(seg)
    for s in range(1, nseg):
        first_at = jnp.where(seg >= s, starts[s - 1], first_at)
    pos = (idx - first_at).astype(F32)
    half = HEAD_DIM // 2
    inv = jnp.exp(-math.log(10000.0) * 2.0 * jnp.arange(half, dtype=F32) / HEAD_DIM)
    ang = pos[:, None] * jnp.tile(inv, 128 // half)[None, :]
    sign = jnp.where(jnp.arange(128) % HEAD_DIM < half, -1.0, 1.0)
    cos = jnp.cos(ang)
    sin = jnp.sin(ang) * sign
    below = jnp.sum((seg[None, :] < seg[::QB][:, None]).astype(jnp.int32), axis=1)
    upto = jnp.sum((seg[None, :] <= seg[QB - 1 :: QB][:, None]).astype(jnp.int32), axis=1)
    lo = below // KB
    hi = (upto + KB - 1) // KB
    seg_row = jnp.broadcast_to(seg[None, None, :], (1, 8, t))
    seg_col = jnp.broadcast_to(seg[:, None], (t, 128))

    (hidden, normed, q, k, v, wqkv, wrows, att, g_mid, g_att, output, gw, _, _, _, _) = (
        forwarded := forward(
            frames,
            skip_in,
            out_grad,
            w_skip,
            w_q,
            w_k,
            w_v,
            w_o,
            w_up,
            w_dn,
            own_small,
            b_up[None, :],
            b_dn[None, :],
            cos,
            sin,
            seg_row,
            seg_col,
            nz,
        )
    )[:16]
    small, lse, sums, g_b_up, g_gate2_own = forwarded[16:]
    first_sum = lax.psum_scatter(gw, "dp", scatter_dimension=1, tiled=True)
    gq, gk, gv = attn_bwd(q, k, v, att, g_att, lse, seg_row, seg_col, lo, hi, cos, sin, nz)
    s_qkv, s_w_skip, vecs, total, grad_frames, grad_skip = third(
        normed,
        gq,
        gk,
        gv,
        w_q,
        w_k,
        w_v,
        wqkv,
        hidden,
        g_mid,
        frames,
        skip_in,
        wrows,
        small,
        sums,
        g_b_up,
        g_gate2_own,
        embed.astype(F32),
        ndp,
        nz,
    )
    nm = mod_part.shape[0]
    sizes = [nm, loc, fl, d]
    offs = [sum(sizes[:i]) for i in range(len(sizes) + 1)]

    def share(i):
        n = sizes[i] // ndp
        return lax.dynamic_slice_in_dim(total[0], offs[i] + dp * n, n, 0)

    rows = d // ndp
    embeds = lax.dynamic_slice_in_dim(vecs[:, 0], offs[4] + dp * rows, rows, 1)
    s_w_mod = dot(embeds.astype(BF16), vecs[:, 0, :nm].astype(BF16), TN)
    s_up = first_sum[:fl].T
    s_dn = first_sum[fl : 2 * fl]
    s_o = first_sum[2 * fl :]
    return (
        output,
        grad_frames,
        grad_skip,
        s_w_skip,
        share(1),
        s_w_mod,
        share(0),
        s_qkv[:, :loc],
        s_qkv[:, loc : 2 * loc],
        s_qkv[:, 2 * loc :],
        s_o,
        s_up,
        share(2),
        s_dn,
        share(3),
    )


def solution(mesh):
    in_specs = (
        P("dp", None),
        P("dp", None),
        P("dp"),
        P("dp", None),
        P(None, "tensor"),
        P("tensor"),
        P(None, "tensor"),
        P("tensor"),
        P(None, "tensor"),
        P(None, "tensor"),
        P(None, "tensor"),
        P("tensor", None),
        P(None, "tensor"),
        P("tensor"),
        P("tensor", None),
        P(),
        P("dp", None),
    )
    out_specs = (
        P("dp", "tensor"),
        P("dp", "tensor"),
        P("dp", "tensor"),
        P("dp", "tensor"),
        P(("tensor", "dp")),
        P("dp", "tensor"),
        P(("tensor", "dp")),
        P("dp", "tensor"),
        P("dp", "tensor"),
        P("dp", "tensor"),
        P("tensor", "dp"),
        P("dp", "tensor"),
        P(("tensor", "dp")),
        P("tensor", "dp"),
        P("dp"),
    )
    return jax.shard_map(
        functools.partial(per_device, mesh.shape["dp"], mesh.shape["tensor"]),
        mesh=mesh,
        in_specs=in_specs,
        out_specs=out_specs,
        check_vma=False,
    )
```

```python
import functools
import math

import jax
import jax.numpy as jnp
from jax import lax
from jax.experimental import pallas as pl
from jax.experimental.pallas import tpu as pltpu
from jax.sharding import PartitionSpec as P

HEAD_DIM = 64
EPS = 1e-06
F32 = jnp.float32
BF16 = jnp.bfloat16
MESH = pl.DeviceIdType.MESH
ANY = pl.BlockSpec(memory_space=pl.ANY)
VMEM = pl.BlockSpec(memory_space=pltpu.VMEM)
GROUP = 8
NT = (((1,), (1,)), ((), ()))
NN = (((1,), (0,)), ((), ()))


def dot(a, b, dims=NN, precision=None):
    return lax.dot_general(a, b, dims, precision=precision, preferred_element_type=F32)


def remote(src, dst, send, recv, device):
    return pltpu.make_async_remote_copy(
        src_ref=src,
        dst_ref=dst,
        send_sem=send,
        recv_sem=recv,
        device_id=device,
        device_id_type=MESH,
    )


class Spread:
    def __init__(self, nz, n, src, land, plane, double, sems, lags):
        self.nz, self.n, self.src, self.land, self.plane = nz, n, src, land, plane
        self.double = double
        self.lags = lags
        self.zs, self.zr, self.ps, self.pr, self.rs = sems
        dp = lax.axis_index("dp")
        z = lax.axis_index("tensor")
        self.z = z
        core = lax.rem(dp, 2)
        x = lax.rem(dp // 2, 2)
        y = lax.rem(dp // 4, 2)
        dx = 2 - 4 * x
        dy = 4 - 8 * y
        b1 = y + core * (x - y)
        b2 = x + core * (y - x)
        d1 = dy + core * (dx - dy)
        d2 = dx + core * (dy - dx)
        self.slot = core * 4 + 2 * b2 + b1
        self.b1 = b1
        self.pair = core * 4 + 2 * b2
        self.near = {1: (dp + d1, z), 2: (dp + d2, z), 3: (dp + 1 - 2 * core, z)}
        self.far = {k: (dp, lax.rem(z + nz - k, nz)) for k in range(1, nz)}
        base = core * 4
        self.out = {1: (self.slot, 1), 2: (base + 2 * b2, 2), 3: (base, 4)}
        self.come = {
            1: (self.slot + 1 - 2 * b1, 1),
            2: (base + 2 - 2 * b2, 2),
            3: (4 - base, 4),
        }
        self.t = 0
        self.ready = -1

    def barrier(self):
        bar = pltpu.get_barrier_semaphore()
        devices = list(self.near.values()) + list(self.far.values())
        for device in devices:
            pl.semaphore_signal(bar, inc=1, device_id=device, device_id_type=MESH)
        pl.semaphore_wait(bar, len(devices))

    def _plane(self, i, k):
        return self.plane(i, self.pair if self.double(i) else self.slot, k)

    def _far(self, i, k):
        return remote(
            self.src(i),
            self._plane(i, k - 1),
            self.zs.at[i, k - 1],
            self.zr.at[i, k - 1],
            self.far[k],
        )

    def _relay(self, i):
        at = 2 * (2 - self.z)
        return remote(
            self._plane(i, 1),
            self._plane(i, at),
            self.rs.at[i],
            self.zr.at[i, at],
            (lax.axis_index("dp"), 3 * (self.z - 1)),
        )

    def _near(self, i, stage, inward):
        at, size = (self.come if inward else self.out)[stage]
        ref = self.land(i).at[pl.ds(at, size)]
        return remote(
            ref, ref, self.ps.at[i, stage - 1], self.pr.at[i, stage - 1], self.near[stage]
        )

    def tick(self):
        t, n, z = self.t, self.n, self.z
        l1, l2, l3, l4 = self.lags
        if t < n:
            self._far(t, 2).start()
            pl.when(z != 0)(lambda: self._far(t, 1).start())
            pl.when(z != 3)(lambda: self._far(t, 3).start())
        if 0 <= t - l4 < n:
            self._near(t - l4, 3, True).wait_recv()
            self.ready = t - l4
        for stage, lag in ((3, l3), (2, l2)):
            if 0 <= t - lag < n:
                if not (stage == 2 and self.double(t - lag)):
                    self._near(t - lag, stage - 1, True).wait_recv()
                self._near(t - lag, stage, False).start()
        i = t - l1
        if 0 <= i < n:
            self._far(i, 1).wait_recv()
            self._far(i, 3).wait_recv()
            pl.when((z == 0) | (z == 3))(lambda: self._far(i, 2).wait_recv())
            if not self.double(i):
                self._near(i, 1, False).start()
        j = t - l1 + 1
        if 0 <= j < n:

            @pl.when((z == 1) | (z == 2))
            def _():
                self._far(j, 2).wait_recv()
                self._relay(j).start()

        self.t += 1

    def until(self, i):
        while self.ready < i:
            self.tick()

    def drain(self):
        z = self.z
        for i in range(self.n):
            self._far(i, 2).wait_send()
            pl.when(z != 0)(lambda: self._far(i, 1).wait_send())
            pl.when(z != 3)(lambda: self._far(i, 3).wait_send())
            pl.when((z == 1) | (z == 2))(lambda: self._relay(i).wait_send())
            for stage in (1, 2, 3):
                if not (stage == 1 and self.double(i)):
                    self._near(i, stage, False).wait_send()


def spread_sems(nz, n):
    dma = pltpu.SemaphoreType.DMA
    kk = nz - 1
    return [dma((n, kk)), dma((n, kk)), dma((n, 3)), dma((n, 3)), dma((n,))]


def flat(small_ref, nm, lo, hi):
    parts = []
    while lo < hi:
        zz = lo // nm
        end = min(hi, (zz + 1) * nm)
        parts.append(small_ref[zz, :, lo - zz * nm : end - zz * nm])
        lo = end
    return parts[0] if len(parts) == 1 else jnp.concatenate(parts, axis=1)


def layer_norm(v):
    centred = v - jnp.mean(v, axis=-1, keepdims=True)
    r = lax.rsqrt(jnp.mean(centred * centred, axis=-1, keepdims=True) + EPS)
    return centred * r, r


TB = 512
LB = 128
LAGS = (3, 5, 7, 8)
DOUBLE = 2
R_B = 8
STEPS = (4, 4, 4, 2, 2)
NEG = -1e30


def aligned(at, size):
    return pl.ds(pl.multiple_of(at, size), size)


def gelu_parts(v):
    c = math.sqrt(2.0 / math.pi)
    v2 = v * v
    th = jnp.tanh(c * v * (1.0 + 0.044715 * v2))
    half = 0.5 * (1.0 + th)
    act = v * half
    slope = half + (0.5 * c) * v * (1.0 - th * th) * (1.0 + 3.0 * 0.044715 * v2)
    return act, slope


TN = (((0,), (0,)), ((), ()))


def forward_kernel(nz, chunks, *refs):
    ni, no = 12, 11
    ins = refs[:ni]
    vec_ref, bup_ref, bdn_ref, segq_ref, segk_ref = refs[ni : ni + 5]
    outs = refs[ni + 5 : ni + 5 + no]
    (h_hid, h_norm, h_q, h_k, h_v, h_w16, h_row, h_att, h_gm, h_ga, h_out) = outs
    rest = refs[ni + 5 + no :]
    gw_ref, lskip, lqkv, lo_, land = rest[:5]
    small_ref, lse_ref, sums_ref, gbu_ref, gg2_ref = rest[5:10]
    vmem_in = rest[10 : 10 + ni]
    (wskip_ref, wq_ref, wk_ref, wv_ref, wo_ref, x_ref, y_ref) = vmem_in[:7]
    (cos_ref, sin_ref, up_ref, dn_ref, go_ref) = vmem_in[7:]
    rest = rest[10 + ni :]
    (hid_ref, norm_ref, q_ref, k_ref, v_ref, f1_ref, gm_ref, out_ref) = rest[:8]
    (wb, o16_ref, sta, stb, pskip, pqkv, po, pc) = rest[8:16]
    (ub, db, gws, vt_ref) = rest[16:20]
    in_sem, out_sem, w_sem, sa_sem, sb_sem, gw_sem, vs, vr = rest[20:28]
    sems = rest[28:33]
    row_ref = ub.at[pl.ds(0, h_row.shape[0])]
    t, d = x_ref.shape
    loc = wq_ref.shape[1]
    fl = up_ref.shape[1]
    kk = nz - 1
    nm = 6 * d // nz
    rs, rq, pr = pskip.shape[1], pqkv.shape[2], fl // GROUP
    heads = loc // HEAD_DIM

    def fetch(i):
        return pltpu.make_async_copy(ins[i], vmem_in[i], in_sem.at[i])

    for i in range(ni):
        fetch(i).start()

    double = lambda i: i % 3 == DOUBLE

    def src(i):
        name, a, c, r = chunks[i]
        which = slice(None) if double(i) else net.b1
        if name == "skip":
            return pskip.at[which, pl.ds(c * r, r)]
        if name == "qkv":
            return pqkv.at[which, a, pl.ds(c * r, r)]
        if name == "o":
            return po.at[which, c]
        return pc.at[which, :, pl.ds(c * r, r)]

    def place(i):
        name, a, c, r = chunks[i]
        return {"skip": lskip, "qkv": lqkv.at[a], "o": lo_, "ff": land}[name].at[c]

    def plane(i, s, k):
        if double(i):
            s = pl.ds(s, 2)
        if chunks[i][0] in ("skip", "qkv"):
            return place(i).at[s, k]
        return place(i).at[s, :, k]

    net = Spread(nz, len(chunks), src, place, plane, double, sems, LAGS)
    z = net.z
    count = lambda name: sum(c[0] == name for c in chunks)
    ns, nq, no_, nf = count("skip"), count("qkv") // 3, count("o"), count("ff")
    results = {
        "hid": (hid_ref, h_hid),
        "norm": (norm_ref, h_norm),
        "q": (q_ref, h_q),
        "k": (k_ref, h_k),
        "v": (v_ref, h_v),
        "row": (row_ref, h_row),
        "att": (y_ref, h_att),
        "gm": (gm_ref, h_gm),
        "ga": (k_ref, h_ga),
        "out": (out_ref, h_out),
    }
    order = list(results)

    def put(name):
        return pltpu.make_async_copy(*results[name], out_sem.at[order.index(name)])

    small_ref[z] = vec_ref[...]
    fetch(0).wait()
    part = lambda ref, j, r: ref[aligned((net.pair + j) * r, r), :].astype(F32)
    for j in range(2):
        pskip[j] = part(wskip_ref, j, rs)
    net.barrier()
    net.tick()

    def vec(k, zz):
        return remote(vec_ref, small_ref.at[zz], vs.at[k - 1], vr.at[k - 1], net.far[k])

    for k in range(1, nz):
        vec(k, z).start()
    net.tick()
    for i in (1, 2, 3, 4):
        fetch(i).wait()
    ro = loc // GROUP
    for j in range(2):
        for a, w in enumerate((wq_ref, wk_ref, wv_ref)):
            pqkv[j, a] = part(w, j, rq)
        po[j] = part(wo_ref, j, ro).reshape(po.shape[1:])
    net.tick()
    for k in range(1, nz):
        vec(k, lax.rem(z + k, nz)).wait_recv()
    for i in (5, 6):
        fetch(i).wait()

    def hidden_cols(w, zz):
        bias = small_ref[zz, :, nm : nm + loc]
        cols = aligned(zz * loc, loc)

        @pl.loop(0, t // TB)
        def _(b):
            rows = aligned(b * TB, TB)
            acc = dot(x_ref[rows, :], w[:d, :]) + dot(y_ref[rows, :], w[d:, :])
            hid_ref[rows, cols] = acc + bias

        row_ref[:loc, cols] = w[aligned(z * loc, loc), :]
        row_ref[loc:, cols] = w[aligned(d + z * loc, loc), :]

    net.tick()
    hidden_cols(wskip_ref, z)
    for i in (9, 10):
        fetch(i).wait()
    for j in range(2):
        pc[j, 0] = up_ref[:, aligned((net.pair + j) * pr, pr)].astype(F32).T
        pc[j, 1] = part(dn_ref, j, pr)

    def stager(buf, sem, first_chunk, end):
        started = set()

        def copy(i):
            at = (i - first_chunk) % 2
            return pltpu.make_async_copy(place(i), buf.at[at], sem.at[at])

        def take(i):
            net.until(i)
            if i not in started:
                copy(i).start()
                started.add(i)
            copy(i).wait()
            if i + 1 < end and net.ready > i:
                copy(i + 1).start()
                started.add(i + 1)
            return buf.at[(i - first_chunk) % 2]

        return take

    nsq = ns + 3 * nq
    stage_a = stager(sta, sa_sem, 0, nsq)
    stage_b = stager(stb, sb_sem, nsq, net.n)
    r = rs // ns
    for c in range(ns):
        st = stage_a(c)
        for k in range(kk):
            for s in range(GROUP):
                wb[k, s * rs + c * r : s * rs + (c + 1) * r, :] = st[s, k].astype(BF16)
    for k in range(1, nz):
        hidden_cols(wb.at[k - 1], lax.rem(z + k, nz))
        net.tick()
    put("row").start()

    shift1, scale1 = flat(small_ref, nm, 0, d), flat(small_ref, nm, d, 2 * d)

    @pl.loop(0, t // LB)
    def _(b):
        rows = aligned(b * LB, LB)
        xn, _ = layer_norm(hid_ref[rows, :])
        norm_ref[rows, :] = (xn * (1.0 + scale1) + shift1).astype(BF16)

    put("hid").start()
    put("norm").start()
    net.tick()
    for i in (7, 8):
        fetch(i).wait()

    qb = 256
    nb = t // qb

    def attend(g):
        gc = slice(g * loc, (g + 1) * loc)
        lane = lax.broadcasted_iota(jnp.int32, (qb, loc), 1) // HEAD_DIM
        vt_ref[...] = v_ref[:, gc].T
        for j in range(nb):
            kj = k_ref[j * qb : (j + 1) * qb, gc]
            for h in range(heads):
                x_ref[h * qb : (h + 1) * qb, j * qb : (j + 1) * qb] = jnp.where(
                    lane == h, kj, jnp.zeros_like(kj)
                )

        def block(i):
            rows = aligned(i * qb, qb)
            qi = q_ref[rows, gc]
            segq = segq_ref[0, pl.ds(0, 1), rows]

            def first(j, mx):
                at = aligned(j * qb, qb)
                s = dot(x_ref[:, at], qi, NT)
                same = wide(segk_ref[at, :], qb) == segq
                out = []
                for h in range(heads):
                    sh = jnp.where(same, s[h * qb : (h + 1) * qb], NEG)
                    f1_ref[at, h * qb : (h + 1) * qb] = sh
                    out.append(
                        jnp.maximum(mx[h], jnp.max(sh.reshape(qb // 8, 8, qb), axis=0))
                    )
                return out

            mx = lax.fori_loop(0, nb, first, [jnp.full((8, qb), NEG, F32)] * heads)
            ms = [jnp.max(m, axis=0, keepdims=True) for m in mx]

            def second(j, carry):
                ls, os_ = carry
                at = aligned(j * qb, qb)
                nl, nx = [], []
                for h in range(heads):
                    p = jnp.exp(f1_ref[at, h * qb : (h + 1) * qb] - ms[h])
                    nl.append(ls[h] + jnp.sum(p.reshape(qb // 8, 8, qb), axis=0))
                    vt = vt_ref[pl.ds(h * HEAD_DIM, HEAD_DIM), at]
                    nx.append(os_[h] + dot(vt, p.astype(BF16)))
                return nl, nx

            ls, os_ = lax.fori_loop(
                0,
                nb,
                second,
                ([jnp.zeros((8, qb), F32)] * heads, [jnp.zeros((HEAD_DIM, qb), F32)] * heads),
            )
            l1 = [jnp.sum(v, axis=0, keepdims=True) for v in ls]
            o = jnp.concatenate([os_[h] / l1[h] for h in range(heads)], axis=0)
            y_ref[rows, gc] = o.astype(BF16).T
            lse = [ms[h] + jnp.log(l1[h]) for h in range(heads)]
            lse_ref[g, :, rows] = jnp.concatenate(lse + [jnp.zeros((8 - heads, qb), F32)], axis=0)

        for half in range(2):
            pl.loop(half * nb // 2, (half + 1) * nb // 2)(block)
            net.tick()

    def project(a, k, w):
        out = (q_ref, k_ref, v_ref)[a]

        @pl.loop(0, t // TB)
        def _(b):
            rows = aligned(b * TB, TB)
            u = dot(norm_ref[rows, :], w[...])
            if a < 2:
                u = u * wide(cos_ref[rows, :], loc) + swap_halves(u) * wide(sin_ref[rows, :], loc)
            if a == 0:
                u = u.astype(BF16).astype(F32) * (HEAD_DIM**-0.5)
            out[rows, k * loc : (k + 1) * loc] = u.astype(BF16)

    for a in range(3):
        project(a, 0, (wq_ref, wk_ref, wv_ref)[a])
    net.tick()
    attend(0)
    r = rq // nq

    def w_out(a):
        return pltpu.make_async_copy(
            wb.at[:, pl.ds((a % 2) * d, d)], h_w16.at[:, a], w_sem.at[a % 2]
        )

    for a in range(3):
        if a == 2:
            w_out(0).wait()
        base = (a % 2) * d
        for c in range(nq):
            st = stage_a(ns + nq * a + c)
            for k in range(kk):
                for s in range(GROUP):
                    at = base + s * rq + c * r
                    wb[k, at : at + r, :] = st[s, k].astype(BF16)
        for k in range(1, nz):
            project(a, k, wb.at[k - 1, pl.ds(base, d)])
        net.tick()
        w_out(a).start()
        put("qkv"[a]).start()

    for g in range(1, nz):
        attend(g)
    put("norm").wait()
    att_ref, br_ref, gf_ref, n2_ref, gb_ref, ga_ref = y_ref, f1_ref, x_ref, norm_ref, q_ref, k_ref
    put("att").start()

    for c in range(no_):
        st = stage_b(nsq + c)
        for k in range(kk):
            for s in range(GROUP):
                at = s * ro + c * 2 * R_B
                o16_ref[k, at : at + 2 * R_B, :] = jnp.concatenate(
                    [st[s, 0, k], st[s, 1, k]], axis=0
                ).astype(BF16)
    row = lambda i: flat(small_ref, nm, i * d, (i + 1) * d)
    gate1, shift2, scale2, gate2 = row(2), row(3), row(4), row(5)

    @pl.loop(0, t // TB)
    def _(b):
        rows = aligned(b * TB, TB)
        br_ref[rows, :] = dot(att_ref[rows, :loc], wo_ref[...]) + dot(
            att_ref[rows, loc:], o16_ref[...].reshape(kk * loc, d)
        )

    net.tick()
    sums_ref[...] = jnp.zeros_like(sums_ref)
    fetch(11).wait()

    @pl.loop(0, t // LB)
    def _(b):
        rows = aligned(b * LB, LB)
        x2, _ = layer_norm(hid_ref[rows, :] + gate1 * br_ref[rows, :])
        n2_ref[rows, :] = (x2 * (1.0 + scale2) + shift2).astype(BF16)
        go = go_ref[rows, :].astype(F32)
        sums_ref[3:4, :] += jnp.sum(go, axis=0, keepdims=True)
        gf_ref[rows, :] = (gate2 * go).astype(BF16)

    net.tick()

    own = aligned(z * loc, loc)

    def units(first_time, rows, pre, dnv, back):
        act, slope = gelu_parts(pre)
        act = act.astype(BF16)
        ffn = dot(act, dnv[:, own])
        g_pre = (dot(gf_ref[rows, :], dnv[...], NT) * slope).astype(BF16)
        gn = back(g_pre)
        if first_time:
            out_ref[rows, :] = ffn
            gm_ref[rows, :] = gn
        else:
            out_ref[rows, :] += ffn
            gm_ref[rows, :] += gn
        return act, g_pre

    parts = 4
    sub = fl // parts
    w_out(1).wait()
    w_out(2).wait()
    act_s, gp_s = wb.at[0, pl.ds(0, t), pl.ds(0, sub)], wb.at[1, pl.ds(0, t), pl.ds(0, sub)]
    gwc = lambda j, s: pltpu.make_async_copy(
        gws.at[s], gw_ref.at[pl.ds(s * fl + j * sub, sub)], gw_sem.at[s]
    )
    for j in range(parts):
        cs = slice(j * sub, (j + 1) * sub)

        @pl.loop(0, t // TB)
        def _(b):
            rows = aligned(b * TB, TB)
            pre = dot(n2_ref[rows, :], up_ref[:, cs]) + bup_ref[:, cs]
            a, g = units(
                j == 0, rows, pre, dn_ref.at[cs, :], lambda gp: dot(gp, up_ref[:, cs], NT)
            )
            act_s[rows, :] = a
            gp_s[rows, :] = g

        if j > 0:
            for s in range(2):
                gwc(j - 1, s).wait()
        gbu_ref[:, cs] = jnp.sum(gp_s[...].astype(F32), axis=0, keepdims=True)
        gws[0] = dot(gp_s[...], n2_ref[...], TN)
        gws[1] = dot(act_s[...], gf_ref[...], TN)
        for s in range(2):
            gwc(j, s).start()
        net.tick()
    put("row").wait()
    at = 0
    f0 = ns + 3 * nq + no_
    for per in STEPS:
        w = per * GROUP * R_B
        for c in range(per):
            st = stage_b(f0 + at + c)
            u = GROUP * R_B
            for k in range(kk):
                for half, dst in ((0, ub), (1, db)):
                    dst[k * w + c * u : k * w + (c + 1) * u, :] = jnp.concatenate(
                        [st[s, half, k] for s in range(GROUP)], axis=0
                    ).astype(BF16)
        bias = []
        for k in range(kk):
            lo = nm + loc + at * GROUP * R_B
            bias.append(small_ref[lax.rem(z + k + 1, nz), :, lo : lo + w])
        bias = jnp.concatenate(bias, axis=1)
        w = w * kk

        @pl.loop(0, t // TB)
        def _(b):
            rows = aligned(b * TB, TB)
            pre = dot(n2_ref[rows, :], ub[:w, :], NT) + bias
            units(False, rows, pre, db.at[:w, :], lambda gp: dot(gp, ub[:w, :]))

        if net.t < net.n + net.lags[3]:
            net.tick()
        at += per

    put("q").wait()
    put("k").wait()
    bdn = bdn_ref[:, own]
    stb[0, 0, 0, 0, 0:1] = gate1
    stb[0, 0, 0, 1, 0:1] = gate2
    gate1_own = stb[0, 0, 0, 0, 0:1, own]
    gate2_own = stb[0, 0, 0, 1, 0:1, own]
    gg2_ref[...] = jnp.zeros_like(gg2_ref)

    @pl.loop(0, t // LB)
    def _(b):
        rows = aligned(b * LB, LB)
        ffn = out_ref[rows, :] + bdn
        gg2_ref[...] += jnp.sum(go_ref[rows, own].astype(F32) * ffn, axis=0, keepdims=True)
        out_ref[rows, :] = hid_ref[rows, own] + gate1_own * br_ref[rows, own] + gate2_own * ffn
        br = br_ref[rows, :]
        x2, r2 = layer_norm(hid_ref[rows, :] + gate1 * br)
        gn = gm_ref[rows, :]
        sums_ref[0:1, :] += jnp.sum(gn, axis=0, keepdims=True)
        sums_ref[1:2, :] += jnp.sum(gn * x2, axis=0, keepdims=True)
        gp = gn * (1.0 + scale2)
        gm = go_ref[rows, :].astype(F32) + r2 * (
            gp
            - jnp.mean(gp, axis=-1, keepdims=True)
            - x2 * jnp.mean(gp * x2, axis=-1, keepdims=True)
        )
        gm_ref[rows, :] = gm
        sums_ref[2:3, :] += jnp.sum(gm * br, axis=0, keepdims=True)
        gb_ref[rows, :] = (gate1 * gm).astype(BF16)

    put("gm").start()
    put("out").start()

    @pl.loop(0, t // TB)
    def _(b):
        rows = aligned(b * TB, TB)
        ga_ref[rows, :loc] = dot(gb_ref[rows, :], wo_ref[...], NT).astype(BF16)
        ga_ref[rows, loc:] = dot(
            gb_ref[rows, :], o16_ref[...].reshape(kk * loc, d), NT
        ).astype(BF16)

    put("ga").start()
    for s in range(2):
        gwc(parts - 1, s).wait()
    gws[0, :loc, :] = dot(att_ref[:, :loc], gb_ref[...], TN)
    last = lambda: pltpu.make_async_copy(
        gws.at[0, pl.ds(0, loc)], gw_ref.at[pl.ds(2 * fl, loc)], gw_sem.at[0]
    )
    last().start()
    net.drain()
    for k in range(1, nz):
        vec(k, z).wait_send()
    last().wait()
    for name in ("hid", "v", "att", "gm", "ga", "out"):
        put(name).wait()


def forward(x, y, go, wskip, wq, wk, wv, wo, up, dn, vec, bup, bdn, cos, sin, segq, segk, nz):
    t, d = x.shape
    loc = wq.shape[1]
    fl = up.shape[1]
    kk = nz - 1
    rs, rq, ro = 2 * d // GROUP, d // GROUP, loc // GROUP
    ns, nq, no = 4, 2, ro // (2 * R_B)
    nf = fl // GROUP // R_B
    chunks = [("skip", 0, c, rs // ns) for c in range(ns)]
    chunks += [("qkv", a, c, rq // nq) for a in range(3) for c in range(nq)]
    chunks += [("o", 0, c, 2 * R_B) for c in range(no)]
    chunks += [("ff", 0, c, R_B) for c in range(nf)]
    sd = jax.ShapeDtypeStruct
    dma = pltpu.SemaphoreType.DMA
    ins = [wskip, wq, wk, wv, wo, x, y, cos, sin, up, dn, go]
    e = nz * loc
    per = max(STEPS)
    nu = per * kk * GROUP * R_B
    outs = [
        sd((t, d), F32),
        sd((t, d), BF16),
        sd((t, e), BF16),
        sd((t, e), BF16),
        sd((t, e), BF16),
        sd((kk, 3, d, loc), BF16),
        sd((2 * loc, d), BF16),
        sd((t, e), BF16),
        sd((t, d), F32),
        sd((t, e), BF16),
        sd((t, loc), F32),
    ]
    more = [
        sd((2 * fl + loc, d), F32),
        sd((ns, GROUP, kk, rs // ns, loc), F32),
        sd((3, nq, GROUP, kk, rq // nq, loc), F32),
        sd((no, GROUP, 2, kk, R_B, d), F32),
        sd((nf, GROUP, 2, kk, R_B, d), F32),
    ]
    small = [
        sd((nz,) + vec.shape, F32),
        sd((nz, 8, t), F32),
        sd((8, d), F32),
        sd((1, fl), F32),
        sd((1, loc), F32),
    ]
    scratch = [pltpu.VMEM(v.shape, v.dtype) for v in ins]
    scratch += [
        pltpu.VMEM((t, d), F32),
        pltpu.VMEM((t, d), BF16),
        pltpu.VMEM((t, e), BF16),
        pltpu.VMEM((t, e), BF16),
        pltpu.VMEM((t, e), BF16),
        pltpu.VMEM((t, d), F32),
        pltpu.VMEM((t, d), F32),
        pltpu.VMEM((t, loc), F32),
        pltpu.VMEM((kk, 2 * d, loc), BF16),
        pltpu.VMEM((kk, loc, d), BF16),
        pltpu.VMEM((2, GROUP, kk, rs // ns, loc), F32),
        pltpu.VMEM((2, GROUP, 2, kk, R_B, d), F32),
        pltpu.VMEM((2, rs, loc), F32),
        pltpu.VMEM((2, 3, rq, loc), F32),
        pltpu.VMEM((2, no, 2, R_B, d), F32),
        pltpu.VMEM((2, 2, fl // GROUP, d), F32),
        pltpu.VMEM((nu, d), BF16),
        pltpu.VMEM((nu, d), BF16),
        pltpu.VMEM((2, max(fl // 4, loc), d), F32),
        pltpu.VMEM((loc, t), BF16),
        dma((len(ins),)),
        dma((10,)),
        dma((2,)),
        dma((2,)),
        dma((2,)),
        dma((2,)),
        dma((kk,)),
        dma((kk,)),
    ] + spread_sems(nz, len(chunks))
    return pl.pallas_call(
        functools.partial(forward_kernel, nz, chunks),
        out_shape=outs + more + small,
        in_specs=[ANY] * len(ins) + [VMEM] * 5,
        out_specs=[ANY] * (len(outs) + len(more)) + [VMEM] * 5,
        scratch_shapes=scratch,
        compiler_params=pltpu.CompilerParams(
            collective_id=0, has_side_effects=True, vmem_limit_bytes=63 << 20
        ),
    )(*ins, vec, bup, bdn, segq, segk)


class Halving:
    def __init__(self, ndp, src, out, refs, mine, partner):
        self.bits = ndp.bit_length() - 1
        self.ndp, self.src, self.out, self.mine, self.partner = ndp, src, out, mine, partner
        self.recv0, self.lev0, self.s0, self.r0 = refs[:4]
        self.rest = refs[4:]
        self.cw = src.shape[2] // 2
        self.orders = [list(range(1, self.bits)), list(range(self.bits - 1, 0, -1))]
        self.step = -1
        self.sent = []

    def _first(self, i):
        give = 2 * i + 1 - self.mine[0]
        return remote(
            self.src.at[give], self.recv0.at[i], self.s0.at[i], self.r0.at[i], self.partner[0]
        )

    def start(self):
        for i in range(self.ndp // 2):
            self._first(i).start()

    def _items(self, h):
        src, free = self.state[h]
        b = self.orders[h][self.step]
        at = free.index(b)
        lo = 1 << at
        left = [f for f in free if f != b]
        recv, out, ss, rr = self.rest[4 * (2 * self.step + h) : 4 * (2 * self.step + h) + 4]
        items = []
        for i in range(1 << len(left)):
            base = (i // lo) * 2 * lo + i % lo
            give = base + lo * (1 - self.mine[b])
            keep = base + lo * self.mine[b]
            c = functools.partial(
                remote, src.at[give], recv.at[i], ss.at[i], rr.at[i], self.partner[b]
            )
            items.append((c, keep, i))
        return items, src, recv, out, left

    def advance(self):
        if self.step < 0:
            for i in range(self.ndp // 2):
                self._first(i).wait_recv()
                self.lev0[i] = self.src[2 * i + self.mine[0]] + self.recv0[i]
            free = list(range(1, self.bits))
            self.state = [(self.lev0.at[:, :, pl.ds(h * self.cw, self.cw)], free) for h in (0, 1)]
        else:
            for h in (0, 1):
                items, src, recv, out, left = self.now[h]
                for c, keep, i in items:
                    c().wait_recv()
                    total = src[keep] + recv[i]
                    if self.step == self.bits - 2:
                        self.out[:, pl.ds(h * self.cw, self.cw)] = total
                    else:
                        out[i] = total
                    self.sent.append(c)
                self.state[h] = (out, left)
        self.step += 1
        if self.step < self.bits - 1:
            self.now = [self._items(h) for h in (0, 1)]
            for h in (0, 1):
                for c, _, _ in self.now[h][0]:
                    c().start()

    def finish(self):
        while self.step < self.bits - 1:
            self.advance()

    def drain(self):
        for c in self.sent:
            c().wait_send()
        for i in range(self.ndp // 2):
            self._first(i).wait_send()


def halving_refs(ndp, r, c):
    dma = pltpu.SemaphoreType.DMA
    bits = ndp.bit_length() - 1
    half = ndp // 2
    out = [pltpu.VMEM((half, r, c), F32), pltpu.VMEM((half, r, c), F32), dma((half,)), dma((half,))]
    for step in range(bits - 1):
        n = ndp >> (step + 2)
        for _ in range(2):
            out += [pltpu.VMEM((n, r, c // 2), F32), pltpu.VMEM((n, r, c // 2), F32), dma((n,)), dma((n,))]
    return out


def third_kernel(ndp, nz, nh, *refs):
    ni = 13
    ins = refs[:ni]
    small_ref, sums_ref, gbu_ref, gg2_ref, emb_ref = refs[ni : ni + 5]
    sqkv_ref, sskip_ref, all_ref, tot_ref = refs[ni + 5 : ni + 9]
    hbm = refs[ni + 9 : ni + 11]
    rest = refs[ni + 11 :]
    vmem_in = rest[:ni]
    (norm_ref, gq_ref, gk_ref, gv_ref, wq_ref, wk_ref, wv_ref, w_ref) = vmem_in[:8]
    (hid_ref, gm_ref, x_ref, y_ref, row_ref) = vmem_in[8:]
    gf_ref, gs_ref, gn_ref, low_ref, gwq, gws, vec, gz, mod_s = rest[ni : ni + 9]
    in_sem, out_sem, z_send, z_recv, q_send, q_recv = rest[ni + 9 : ni + 15]
    h1 = rest[ni + 15 : ni + 15 + nh]
    h2 = rest[ni + 15 + nh :]
    t, d = hid_ref.shape
    loc = wq_ref.shape[1]
    fl = gbu_ref.shape[1]
    nm = 6 * d // nz
    dp = lax.axis_index("dp")
    z = lax.axis_index("tensor")

    def fetch(i):
        return pltpu.make_async_copy(ins[i], vmem_in[i], in_sem.at[i])

    for i in range(ni):
        fetch(i).start()
    bits = ndp.bit_length() - 1
    mine = [lax.rem(dp // (1 << b), 2) for b in range(bits)]
    partner = [(dp + (1 << b) * (1 - 2 * mine[b]), z) for b in range(bits)]
    others = lambda j: (lax.rem(dp + j, ndp), z)
    bar = pltpu.get_barrier_semaphore()
    for j in range(1, ndp):
        pl.semaphore_signal(bar, inc=1, device_id=others(j), device_id_type=MESH)
    for k in range(1, nz):
        pl.semaphore_signal(
            bar, inc=1, device_id=(dp, lax.rem(z + k, nz)), device_id_type=MESH
        )
    grads = (gq_ref, gk_ref, gv_ref)
    for i in range(4):
        fetch(i).wait()
    for a in range(3):
        gwq[:, :, a * loc : (a + 1) * loc] = dot(
            norm_ref[...], grads[a][:, :loc], TN
        ).reshape(ndp, d // ndp, loc)
    pl.semaphore_wait(bar, ndp - 1 + nz - 1)
    one = Halving(ndp, gwq, sqkv_ref, h1, mine, partner)
    one.start()

    def part(k, zz):
        return remote(
            gg2_ref, gz.at[zz], z_send.at[k - 1], z_recv.at[k - 1], (dp, lax.rem(z + nz - k, nz))
        )

    for k in range(1, nz):
        part(k, z).start()
    gz[z] = gg2_ref[...]
    for i in range(4, 8):
        fetch(i).wait()
    own = (wq_ref, wk_ref, wv_ref)

    def product(b):
        rows = pl.ds(b * TB, TB)
        acc = dot(gq_ref[rows, :loc], wq_ref[...], NT)
        for k in range(nz):
            for a in range(3):
                if k == 0 and a == 0:
                    continue
                w = own[a][...] if k == 0 else w_ref[k - 1, a]
                acc = acc + dot(grads[a][rows, k * loc : (k + 1) * loc], w, NT)
        gn_ref[rows, :] = acc

    for b in range(t // TB):
        product(b)
        if b == 0:
            one.advance()
    one.advance()
    scale1 = flat(small_ref, nm, d, 2 * d)
    mod_s[...] = jnp.zeros_like(mod_s)
    for i in (8, 9):
        fetch(i).wait()

    @pl.loop(0, t // LB)
    def _(b):
        rows = aligned(b * LB, LB)
        x1, r1 = layer_norm(hid_ref[rows, :])
        gn = gn_ref[rows, :]
        mod_s[:, :d] += jnp.sum(gn, axis=0, keepdims=True)
        mod_s[:, d : 2 * d] += jnp.sum(gn * x1, axis=0, keepdims=True)
        gp = gn * (1.0 + scale1)
        gh = gm_ref[rows, :] + r1 * (
            gp
            - jnp.mean(gp, axis=-1, keepdims=True)
            - x1 * jnp.mean(gp * x1, axis=-1, keepdims=True)
        )
        mod_s[:, 6 * d :] += jnp.sum(gh, axis=0, keepdims=True)
        low_ref[rows, :] = gh.astype(BF16)

    one.advance()
    for i in (10, 11, 12):
        fetch(i).wait()
    cols = aligned(z * loc, loc)
    low_own = low_ref[:, cols]
    half = ndp // 2
    gws[:half] = dot(x_ref[...], low_own, TN).reshape(half, 2 * d // ndp, loc)
    gws[half:] = dot(y_ref[...], low_own, TN).reshape(half, 2 * d // ndp, loc)
    two = Halving(ndp, gws, sskip_ref, h2, mine, partner)
    two.start()
    for k in range(1, nz):
        part(k, lax.rem(z + k, nz)).wait_recv()
    gate2 = flat(small_ref, nm, 5 * d, 6 * d)
    mod_s[:, 2 * d : 3 * d] = sums_ref[2:3, :]
    mod_s[:, 3 * d : 4 * d] = sums_ref[0:1, :]
    mod_s[:, 4 * d : 5 * d] = sums_ref[1:2, :]
    for zz in range(nz):
        mod_s[:, 5 * d + zz * loc : 5 * d + (zz + 1) * loc] = gz[zz]
    o = nm
    vec[:, :o] = mod_s[:, aligned(z * nm, nm)]
    vec[:, o : o + loc] = mod_s[:, pl.ds(pl.multiple_of(6 * d + z * loc, loc), loc)]
    o += loc
    vec[:, o : o + fl] = gbu_ref[...]
    o += fl
    vec[:, o : o + d] = gate2 * sums_ref[3:4, :]
    o += d
    vec[:, o : o + d] = emb_ref[...]
    all_ref[dp] = vec[...]

    def give(j, row):
        return remote(vec, all_ref.at[row], q_send.at[j - 1], q_recv.at[j - 1], others(j))

    for j in range(1, ndp):
        give(j, dp).start()

    outs = (gf_ref, gs_ref)

    def put(i):
        return pltpu.make_async_copy(outs[i], hbm[i], out_sem.at[i])

    def back(i):
        w = row_ref[i * loc : (i + 1) * loc, :]
        for b in range(t // TB):
            rows = pl.ds(b * TB, TB)
            outs[i][rows, :] = dot(low_ref[rows, :], w, NT)
        put(i).start()

    two.advance()
    back(0)
    two.advance()
    one.finish()
    back(1)
    two.finish()
    for j in range(1, ndp):
        give(j, lax.rem(dp + ndp - j, ndp)).wait_recv()
    tot_ref[...] = jnp.sum(all_ref[...], axis=0)
    one.drain()
    two.drain()
    for k in range(1, nz):
        part(k, z).wait_send()
    for j in range(1, ndp):
        give(j, dp).wait_send()
    for i in range(2):
        put(i).wait()


def third(norm, gq, gk, gv, wq, wk, wv, w, hid, gm, x, y, row, small, sums, gbu, gg2, emb, ndp, nz):
    t, d = hid.shape
    loc = wq.shape[1]
    fl = gbu.shape[1]
    n = 6 * d // nz + loc + fl + 2 * d
    sd = jax.ShapeDtypeStruct
    dma = pltpu.SemaphoreType.DMA
    ins = [norm, gq, gk, gv, wq, wk, wv, w, hid, gm, x, y, row]
    scratch = [pltpu.VMEM(v.shape, v.dtype) for v in ins]
    scratch += [
        pltpu.VMEM((t, loc), F32),
        pltpu.VMEM((t, loc), F32),
        pltpu.VMEM((t, d), F32),
        pltpu.VMEM((t, d), BF16),
        pltpu.VMEM((ndp, d // ndp, 3 * loc), F32),
        pltpu.VMEM((ndp, 2 * d // ndp, loc), F32),
        pltpu.VMEM((1, n), F32),
        pltpu.VMEM((nz, 1, loc), F32),
        pltpu.VMEM((1, 7 * d), F32),
        dma((len(ins),)),
        dma((2,)),
        dma((nz - 1,)),
        dma((nz - 1,)),
        dma((ndp - 1,)),
        dma((ndp - 1,)),
    ]
    h1 = halving_refs(ndp, d // ndp, 3 * loc)
    h2 = halving_refs(ndp, 2 * d // ndp, loc)
    return pl.pallas_call(
        functools.partial(third_kernel, ndp, nz, len(h1)),
        out_shape=[
            sd((d // ndp, 3 * loc), F32),
            sd((2 * d // ndp, loc), F32),
            sd((ndp, 1, n), F32),
            sd((1, n), F32),
            sd((t, loc), F32),
            sd((t, loc), F32),
        ],
        in_specs=[ANY] * len(ins) + [VMEM] * 5,
        out_specs=[VMEM] * 4 + [ANY] * 2,
        scratch_shapes=scratch + h1 + h2,
        compiler_params=pltpu.CompilerParams(
            collective_id=1, has_side_effects=True, vmem_limit_bytes=62 << 20
        ),
    )(*ins, small, sums, gbu, gg2, emb)


def wide(table, lanes):
    return jnp.concatenate([table] * (lanes // 128), axis=1)


def swap_halves(u):
    n = u.shape[1]
    lane = lax.broadcasted_iota(jnp.int32, u.shape, 1)
    half = HEAD_DIM // 2
    return jnp.where(
        lane % HEAD_DIM < half, pltpu.roll(u, n - half, 1), pltpu.roll(u, half, 1)
    )


QB = 256
KB = 256


def stack_heads(dst, src, heads):
    lane = lax.broadcasted_iota(jnp.int32, src.shape, 1) // HEAD_DIM
    for h in range(heads):
        dst[:, h] = jnp.where(lane == h, src, jnp.zeros_like(src)).reshape(dst.shape[0], dst.shape[2], dst.shape[3])

def bwd_kernel(heads, QB, KB, lo_ref, hi_ref, q_ref, k_ref, v_ref, att_ref, g_ref, lse_ref, segq_ref, segk_ref, cos_ref, sin_ref, gq_ref, gk_ref, gv_ref,
               kt_ref, ks_ref, vs_ref, dk_ref, dv_ref):
    t, e = k_ref.shape
    kt_ref[...] = k_ref[...].T
    stack_heads(ks_ref, k_ref[...], heads)
    stack_heads(vs_ref, v_ref[...], heads)
    dk_ref[...] = jnp.zeros_like(dk_ref); dv_ref[...] = jnp.zeros_like(dv_ref)
    row = lax.broadcasted_iota(jnp.int32, (8, e), 0); lane = lax.broadcasted_iota(jnp.int32, (8, e), 1)
    ind = jnp.where(lane//HEAD_DIM == row, 1.0, 0.0).astype(F32)
    lanek = lax.broadcasted_iota(jnp.int32, (KB, e), 1)//HEAD_DIM
    @pl.loop(0, t//QB)
    def _(i):
        qs = pl.multiple_of(i*QB, QB)
        q = q_ref[pl.ds(qs, QB), :]; g = g_ref[pl.ds(qs, QB), :]
        segq = segq_ref[0, pl.ds(0,1), pl.ds(qs, QB)]
        prod = g.astype(F32)*att_ref[pl.ds(qs, QB), :].astype(F32)
        delta = dot(ind, prod, NT, lax.Precision.HIGHEST)
        lse = lse_ref[0, :, pl.ds(qs, QB)]
        def body(j, dq):
            start = pl.multiple_of(j*KB, KB)
            s = dot(ks_ref[j].reshape(heads*KB, e), q, NT)
            dpt = dot(vs_ref[j].reshape(heads*KB, e), g, NT)
            segk = segk_ref[pl.ds(start, KB), :]
            same = jnp.concatenate([segk]*(QB//128), axis=1) == segq
            ps, dss, ndq = [], [], []
            for h in range(heads):
                p = jnp.exp(jnp.where(same, s[h*KB:(h+1)*KB], NEG) - lse[h:h+1])
                ds = (p*(dpt[h*KB:(h+1)*KB] - delta[h:h+1])).astype(BF16)
                ps.append(p.astype(BF16)); dss.append(ds)
                kt = kt_ref[pl.ds(h*HEAD_DIM, HEAD_DIM), pl.ds(start, KB)]
                ndq.append(dq[h] + dot(kt, ds))
            dvs = dot(jnp.concatenate(ps, axis=0), g)
            dks = dot(jnp.concatenate(dss, axis=0), q)
            dv, dk = dvs[:KB], dks[:KB]
            for h in range(1, heads):
                dv = jnp.where(lanek == h, dvs[h*KB:(h+1)*KB], dv)
                dk = jnp.where(lanek == h, dks[h*KB:(h+1)*KB], dk)
            dk_ref[pl.ds(start, KB), :] += dk
            dv_ref[pl.ds(start, KB), :] += dv
            return ndq
        dq = lax.fori_loop(lo_ref[i], hi_ref[i], body, [jnp.zeros((HEAD_DIM, QB), F32)]*heads)
        dqf = jnp.concatenate(dq, axis=0).T * (HEAD_DIM**-0.5)
        cos = wide(cos_ref[pl.ds(qs, QB), :], e)
        sin = wide(sin_ref[pl.ds(qs, QB), :], e)
        gq_ref[pl.ds(qs, QB), :] = (dqf*cos - swap_halves(dqf)*sin).astype(BF16)
    dk = dk_ref[...]
    gk_ref[...] = (dk * wide(cos_ref[...], e) - swap_halves(dk) * wide(sin_ref[...], e)).astype(BF16)
    gv_ref[...] = dv_ref[...].astype(BF16)

def attn_bwd(q,k,v,att,g,lse,seg_row,seg_col,lo,hi,cos,sin,groups,QB=QB,KB=KB):
    t = q.shape[0]; e = q.shape[1]//groups; heads = e//HEAD_DIM
    col = pl.BlockSpec((t,e), lambda g,*_: (0,g)); full = lambda s: pl.BlockSpec(s, lambda g,*_: (0,0))
    return pl.pallas_call(functools.partial(bwd_kernel, heads, QB, KB), out_shape=[jax.ShapeDtypeStruct(q.shape,BF16)]*3,
        grid_spec=pltpu.PrefetchScalarGridSpec(num_scalar_prefetch=2, grid=(groups,),
            in_specs=[col]*5+[pl.BlockSpec((1,8,t), lambda g,*_: (g,0,0)), pl.BlockSpec((1,8,t), lambda g,*_: (0,0,0)), full((t,128)), full((t,128)), full((t,128))],
            out_specs=[col]*3,
            scratch_shapes=[pltpu.VMEM((e,t),BF16), pltpu.VMEM((t//KB,heads,KB,e),BF16), pltpu.VMEM((t//KB,heads,KB,e),BF16), pltpu.VMEM((t,e),F32), pltpu.VMEM((t,e),F32)]),
        compiler_params=pltpu.CompilerParams(vmem_limit_bytes=58<<20))(lo,hi,q,k,v,att,g,lse,seg_row,seg_col,cos,sin)


def time_freqs(width):
    half = width // 2
    return jnp.exp(-math.log(10000.0) * jnp.arange(half, dtype=F32) / half)


def time_embed(flow_time, width):
    angles = 1000.0 * flow_time[:, None] * time_freqs(width)[None, :]
    both = jnp.concatenate([jnp.cos(angles), jnp.sin(angles)], axis=1)
    return jax.nn.silu(both).astype(BF16)


def per_device(ndp, nz, *args):
    (
        frames,
        skip_in,
        flow_time,
        segment_ids,
        w_skip,
        b_skip,
        w_mod,
        b_mod,
        w_q,
        w_k,
        w_v,
        w_o,
        w_up,
        b_up,
        w_dn,
        b_dn,
        out_grad,
    ) = args
    t, d = frames.shape
    loc = w_q.shape[1]
    fl = w_up.shape[1]
    dp = lax.axis_index("dp")
    z = lax.axis_index("tensor")
    embed = time_embed(flow_time, d)
    mod_part = dot(embed, w_mod)[0] + b_mod
    bup_order = b_up.reshape(GROUP, fl // GROUP // R_B, R_B).transpose(1, 0, 2).reshape(-1)
    own_small = jnp.concatenate([mod_part, b_skip, bup_order])[None, :]

    seg = segment_ids[0]
    idx = jnp.arange(t, dtype=jnp.int32)
    nseg = 4
    starts = [jnp.sum((seg < s).astype(jnp.int32)) for s in range(1, nseg)]
    first_at = jnp.zeros_like(seg)
    for s in range(1, nseg):
        first_at = jnp.where(seg >= s, starts[s - 1], first_at)
    pos = (idx - first_at).astype(F32)
    half = HEAD_DIM // 2
    inv = jnp.exp(-math.log(10000.0) * 2.0 * jnp.arange(half, dtype=F32) / HEAD_DIM)
    ang = pos[:, None] * jnp.tile(inv, 128 // half)[None, :]
    sign = jnp.where(jnp.arange(128) % HEAD_DIM < half, -1.0, 1.0)
    cos = jnp.cos(ang)
    sin = jnp.sin(ang) * sign
    below = jnp.sum((seg[None, :] < seg[::QB][:, None]).astype(jnp.int32), axis=1)
    upto = jnp.sum((seg[None, :] <= seg[QB - 1 :: QB][:, None]).astype(jnp.int32), axis=1)
    lo = below // KB
    hi = (upto + KB - 1) // KB
    seg_row = jnp.broadcast_to(seg[None, None, :], (1, 8, t))
    seg_col = jnp.broadcast_to(seg[:, None], (t, 128))

    (hidden, normed, q, k, v, wqkv, wrows, att, g_mid, g_att, output, gw, _, _, _, _) = (
        forwarded := forward(
            frames,
            skip_in,
            out_grad,
            w_skip,
            w_q,
            w_k,
            w_v,
            w_o,
            w_up,
            w_dn,
            own_small,
            b_up[None, :],
            b_dn[None, :],
            cos,
            sin,
            seg_row,
            seg_col,
            nz,
        )
    )[:16]
    small, lse, sums, g_b_up, g_gate2_own = forwarded[16:]
    first_sum = lax.psum_scatter(gw, "dp", scatter_dimension=1, tiled=True)
    gq, gk, gv = attn_bwd(q, k, v, att, g_att, lse, seg_row, seg_col, lo, hi, cos, sin, nz)
    s_qkv, s_w_skip, vecs, total, grad_frames, grad_skip = third(
        normed,
        gq,
        gk,
        gv,
        w_q,
        w_k,
        w_v,
        wqkv,
        hidden,
        g_mid,
        frames,
        skip_in,
        wrows,
        small,
        sums,
        g_b_up,
        g_gate2_own,
        embed.astype(F32),
        ndp,
        nz,
    )
    nm = mod_part.shape[0]
    sizes = [nm, loc, fl, d]
    offs = [sum(sizes[:i]) for i in range(len(sizes) + 1)]

    def share(i):
        n = sizes[i] // ndp
        return lax.dynamic_slice_in_dim(total[0], offs[i] + dp * n, n, 0)

    rows = d // ndp
    embeds = lax.dynamic_slice_in_dim(vecs[:, 0], offs[4] + dp * rows, rows, 1)
    s_w_mod = dot(embeds.astype(BF16), vecs[:, 0, :nm].astype(BF16), TN)
    s_up = first_sum[:fl].T
    s_dn = first_sum[fl : 2 * fl]
    s_o = first_sum[2 * fl :]
    return (
        output,
        grad_frames,
        grad_skip,
        s_w_skip,
        share(1),
        s_w_mod,
        share(0),
        s_qkv[:, :loc],
        s_qkv[:, loc : 2 * loc],
        s_qkv[:, 2 * loc :],
        s_o,
        s_up,
        share(2),
        s_dn,
        share(3),
    )


def solution(mesh):
    in_specs = (
        P("dp", None),
        P("dp", None),
        P("dp"),
        P("dp", None),
        P(None, "tensor"),
        P("tensor"),
        P(None, "tensor"),
        P("tensor"),
        P(None, "tensor"),
        P(None, "tensor"),
        P(None, "tensor"),
        P("tensor", None),
        P(None, "tensor"),
        P("tensor"),
        P("tensor", None),
        P(),
        P("dp", None),
    )
    out_specs = (
        P("dp", "tensor"),
        P("dp", "tensor"),
        P("dp", "tensor"),
        P("dp", "tensor"),
        P(("tensor", "dp")),
        P("dp", "tensor"),
        P(("tensor", "dp")),
        P("dp", "tensor"),
        P("dp", "tensor"),
        P("dp", "tensor"),
        P("tensor", "dp"),
        P("dp", "tensor"),
        P(("tensor", "dp")),
        P("tensor", "dp"),
        P("dp"),
    )
    return jax.shard_map(
        functools.partial(per_device, mesh.shape["dp"], mesh.shape["tensor"]),
        mesh=mesh,
        in_specs=in_specs,
        out_specs=out_specs,
        check_vma=False,
    )
```

```python
import functools
import math

import jax
import jax.numpy as jnp
from jax import lax
from jax.experimental import pallas as pl
from jax.experimental.pallas import tpu as pltpu
from jax.sharding import PartitionSpec as P

HEAD_DIM = 64
EPS = 1e-06
F32 = jnp.float32
BF16 = jnp.bfloat16
MESH = pl.DeviceIdType.MESH
ANY = pl.BlockSpec(memory_space=pl.ANY)
VMEM = pl.BlockSpec(memory_space=pltpu.VMEM)
GROUP = 8
NT = (((1,), (1,)), ((), ()))
NN = (((1,), (0,)), ((), ()))


def dot(a, b, dims=NN, precision=None):
    return lax.dot_general(a, b, dims, precision=precision, preferred_element_type=F32)


def remote(src, dst, send, recv, device):
    return pltpu.make_async_remote_copy(
        src_ref=src,
        dst_ref=dst,
        send_sem=send,
        recv_sem=recv,
        device_id=device,
        device_id_type=MESH,
    )


class Spread:
    def __init__(self, nz, n, src, land, plane, double, sems, lags):
        self.nz, self.n, self.src, self.land, self.plane = nz, n, src, land, plane
        self.double = double
        self.lags = lags
        self.zs, self.zr, self.ps, self.pr, self.rs = sems
        dp = lax.axis_index("dp")
        z = lax.axis_index("tensor")
        self.z = z
        core = lax.rem(dp, 2)
        x = lax.rem(dp // 2, 2)
        y = lax.rem(dp // 4, 2)
        dx = 2 - 4 * x
        dy = 4 - 8 * y
        b1 = y + core * (x - y)
        b2 = x + core * (y - x)
        d1 = dy + core * (dx - dy)
        d2 = dx + core * (dy - dx)
        self.slot = core * 4 + 2 * b2 + b1
        self.b1 = b1
        self.pair = core * 4 + 2 * b2
        self.near = {1: (dp + d1, z), 2: (dp + d2, z), 3: (dp + 1 - 2 * core, z)}
        self.far = {k: (dp, lax.rem(z + nz - k, nz)) for k in range(1, nz)}
        base = core * 4
        self.out = {1: (self.slot, 1), 2: (base + 2 * b2, 2), 3: (base, 4)}
        self.come = {
            1: (self.slot + 1 - 2 * b1, 1),
            2: (base + 2 - 2 * b2, 2),
            3: (4 - base, 4),
        }
        self.t = 0
        self.ready = -1

    def barrier(self):
        bar = pltpu.get_barrier_semaphore()
        devices = list(self.near.values()) + list(self.far.values())
        for device in devices:
            pl.semaphore_signal(bar, inc=1, device_id=device, device_id_type=MESH)
        pl.semaphore_wait(bar, len(devices))

    def _plane(self, i, k):
        return self.plane(i, self.pair if self.double(i) else self.slot, k)

    def _far(self, i, k):
        return remote(
            self.src(i),
            self._plane(i, k - 1),
            self.zs.at[i, k - 1],
            self.zr.at[i, k - 1],
            self.far[k],
        )

    def _relay(self, i):
        at = 2 * (2 - self.z)
        return remote(
            self._plane(i, 1),
            self._plane(i, at),
            self.rs.at[i],
            self.zr.at[i, at],
            (lax.axis_index("dp"), 3 * (self.z - 1)),
        )

    def _near(self, i, stage, inward):
        at, size = (self.come if inward else self.out)[stage]
        ref = self.land(i).at[pl.ds(at, size)]
        return remote(
            ref, ref, self.ps.at[i, stage - 1], self.pr.at[i, stage - 1], self.near[stage]
        )

    def tick(self):
        t, n, z = self.t, self.n, self.z
        l1, l2, l3, l4 = self.lags
        if t < n:
            self._far(t, 2).start()
            pl.when(z != 0)(lambda: self._far(t, 1).start())
            pl.when(z != 3)(lambda: self._far(t, 3).start())
        if 0 <= t - l4 < n:
            self._near(t - l4, 3, True).wait_recv()
            self.ready = t - l4
        for stage, lag in ((3, l3), (2, l2)):
            if 0 <= t - lag < n:
                if not (stage == 2 and self.double(t - lag)):
                    self._near(t - lag, stage - 1, True).wait_recv()
                self._near(t - lag, stage, False).start()
        i = t - l1
        if 0 <= i < n:
            self._far(i, 1).wait_recv()
            self._far(i, 3).wait_recv()
            pl.when((z == 0) | (z == 3))(lambda: self._far(i, 2).wait_recv())
            if not self.double(i):
                self._near(i, 1, False).start()
        j = t - l1 + 1
        if 0 <= j < n:

            @pl.when((z == 1) | (z == 2))
            def _():
                self._far(j, 2).wait_recv()
                self._relay(j).start()

        self.t += 1

    def until(self, i):
        while self.ready < i:
            self.tick()

    def drain(self):
        z = self.z
        for i in range(self.n):
            self._far(i, 2).wait_send()
            pl.when(z != 0)(lambda: self._far(i, 1).wait_send())
            pl.when(z != 3)(lambda: self._far(i, 3).wait_send())
            pl.when((z == 1) | (z == 2))(lambda: self._relay(i).wait_send())
            for stage in (1, 2, 3):
                if not (stage == 1 and self.double(i)):
                    self._near(i, stage, False).wait_send()


def spread_sems(nz, n):
    dma = pltpu.SemaphoreType.DMA
    kk = nz - 1
    return [dma((n, kk)), dma((n, kk)), dma((n, 3)), dma((n, 3)), dma((n,))]


def flat(small_ref, nm, lo, hi):
    parts = []
    while lo < hi:
        zz = lo // nm
        end = min(hi, (zz + 1) * nm)
        parts.append(small_ref[zz, :, lo - zz * nm : end - zz * nm])
        lo = end
    return parts[0] if len(parts) == 1 else jnp.concatenate(parts, axis=1)


def layer_norm(v):
    centred = v - jnp.mean(v, axis=-1, keepdims=True)
    r = lax.rsqrt(jnp.mean(centred * centred, axis=-1, keepdims=True) + EPS)
    return centred * r, r


TB = 512
LB = 128
LAGS = (3, 5, 7, 8)
DOUBLE = 2
R_B = 8
STEPS = (4, 4, 4, 2, 2)
NEG = -1e30


def aligned(at, size):
    return pl.ds(pl.multiple_of(at, size), size)


def gelu_parts(v):
    c = math.sqrt(2.0 / math.pi)
    v2 = v * v
    th = jnp.tanh(c * v * (1.0 + 0.044715 * v2))
    half = 0.5 * (1.0 + th)
    act = v * half
    slope = half + (0.5 * c) * v * (1.0 - th * th) * (1.0 + 3.0 * 0.044715 * v2)
    return act, slope


TN = (((0,), (0,)), ((), ()))


def forward_kernel(nz, chunks, *refs):
    ni, no = 10, 13
    ins = refs[:ni]
    vec_ref, bup_ref, bdn_ref, segq_ref, segk_ref = refs[ni : ni + 5]
    outs = refs[ni + 5 : ni + 5 + no]
    (h_hid, h_norm, h_q, h_k, h_v, h_w16, h_row, h_att, h_gm, h_ga, h_out, h_cos, h_sin) = outs
    rest = refs[ni + 5 + no :]
    gw_ref, lskip, lqkv, lo_, land = rest[:5]
    small_ref, lse_ref, sums_ref, gbu_ref, gg2_ref = rest[5:10]
    vmem_in = rest[10 : 10 + ni]
    (wskip_ref, wq_ref, wk_ref, wv_ref, wo_ref, x_ref, y_ref) = vmem_in[:7]
    (up_ref, dn_ref, go_ref) = vmem_in[7:]
    rest = rest[10 + ni :]
    (hid_ref, norm_ref, q_ref, k_ref, v_ref, f1_ref, gm_ref, out_ref) = rest[:8]
    (wb, o16_ref, sta, stb, pskip, pqkv, po, pc) = rest[8:16]
    (ub, db, gws, vt_ref, cos_ref, sin_ref) = rest[16:22]
    in_sem, out_sem, w_sem, sa_sem, sb_sem, gw_sem, vs, vr = rest[22:30]
    sems = rest[30:35]
    row_ref = ub.at[pl.ds(0, h_row.shape[0])]
    t, d = x_ref.shape
    loc = wq_ref.shape[1]
    fl = up_ref.shape[1]
    kk = nz - 1
    nm = 6 * d // nz
    rs, rq, pr = pskip.shape[1], pqkv.shape[2], fl // GROUP
    heads = loc // HEAD_DIM

    def fetch(i):
        return pltpu.make_async_copy(ins[i], vmem_in[i], in_sem.at[i])

    for i in range(ni):
        fetch(i).start()

    double = lambda i: i % 3 == DOUBLE

    def src(i):
        name, a, c, r = chunks[i]
        which = slice(None) if double(i) else net.b1
        if name == "skip":
            return pskip.at[which, pl.ds(c * r, r)]
        if name == "qkv":
            return pqkv.at[which, a, pl.ds(c * r, r)]
        if name == "o":
            return po.at[which, c]
        return pc.at[which, :, pl.ds(c * r, r)]

    def place(i):
        name, a, c, r = chunks[i]
        return {"skip": lskip, "qkv": lqkv.at[a], "o": lo_, "ff": land}[name].at[c]

    def plane(i, s, k):
        if double(i):
            s = pl.ds(s, 2)
        if chunks[i][0] in ("skip", "qkv"):
            return place(i).at[s, k]
        return place(i).at[s, :, k]

    net = Spread(nz, len(chunks), src, place, plane, double, sems, LAGS)
    z = net.z
    count = lambda name: sum(c[0] == name for c in chunks)
    ns, nq, no_, nf = count("skip"), count("qkv") // 3, count("o"), count("ff")
    results = {
        "hid": (hid_ref, h_hid),
        "norm": (norm_ref, h_norm),
        "q": (q_ref, h_q),
        "k": (k_ref, h_k),
        "v": (v_ref, h_v),
        "row": (row_ref, h_row),
        "att": (y_ref, h_att),
        "gm": (gm_ref, h_gm),
        "ga": (k_ref, h_ga),
        "out": (out_ref, h_out),
        "cos": (cos_ref, h_cos),
        "sin": (sin_ref, h_sin),
    }
    order = list(results)

    def put(name):
        return pltpu.make_async_copy(*results[name], out_sem.at[order.index(name)])

    small_ref[z] = vec_ref[...]
    fetch(0).wait()
    part = lambda ref, j, r: ref[aligned((net.pair + j) * r, r), :].astype(F32)
    for j in range(2):
        pskip[j] = part(wskip_ref, j, rs)
    net.barrier()
    net.tick()

    def vec(k, zz):
        return remote(vec_ref, small_ref.at[zz], vs.at[k - 1], vr.at[k - 1], net.far[k])

    for k in range(1, nz):
        vec(k, z).start()
    net.tick()
    for i in (1, 2, 3, 4):
        fetch(i).wait()
    ro = loc // GROUP
    for j in range(2):
        for a, w in enumerate((wq_ref, wk_ref, wv_ref)):
            pqkv[j, a] = part(w, j, rq)
        po[j] = part(wo_ref, j, ro).reshape(po.shape[1:])
    net.tick()
    for k in range(1, nz):
        vec(k, lax.rem(z + k, nz)).wait_recv()
    for i in (5, 6):
        fetch(i).wait()

    def hidden_cols(w, zz):
        bias = small_ref[zz, :, nm : nm + loc]
        cols = aligned(zz * loc, loc)

        @pl.loop(0, t // TB)
        def _(b):
            rows = aligned(b * TB, TB)
            acc = dot(x_ref[rows, :], w[:d, :]) + dot(y_ref[rows, :], w[d:, :])
            hid_ref[rows, cols] = acc + bias

        row_ref[:loc, cols] = w[aligned(z * loc, loc), :]
        row_ref[loc:, cols] = w[aligned(d + z * loc, loc), :]

    net.tick()
    hidden_cols(wskip_ref, z)
    for i in (7, 8):
        fetch(i).wait()
    for j in range(2):
        pc[j, 0] = up_ref[:, aligned((net.pair + j) * pr, pr)].astype(F32).T
        pc[j, 1] = part(dn_ref, j, pr)

    segs = segq_ref[0, pl.ds(0, 1)]
    starts = [
        jnp.sum(jnp.where(segs < i, 1.0, 0.0), axis=1, keepdims=True) for i in range(1, 4)
    ]
    lane1 = lax.broadcasted_iota(jnp.int32, (1, 128), 1)
    half = HEAD_DIM // 2
    inv = jnp.exp((-math.log(10000.0) * 2.0 / HEAD_DIM) * (lane1 % half).astype(F32))
    sign = jnp.where(lane1 % HEAD_DIM < half, -1.0, 1.0)

    @pl.loop(0, t // LB)
    def _(b):
        rows = aligned(b * LB, LB)
        sk = segk_ref[rows, :]
        at = jnp.zeros(sk.shape, F32)
        for i in range(1, 4):
            at = jnp.where(sk >= i, starts[i - 1], at)
        idx = (lax.broadcasted_iota(jnp.int32, sk.shape, 0) + b * LB).astype(F32)
        ang = (idx - at) * inv
        cos_ref[rows, :] = jnp.cos(ang)
        sin_ref[rows, :] = jnp.sin(ang) * sign

    put("cos").start()
    put("sin").start()

    def stager(buf, sem, first_chunk, end):
        started = set()

        def copy(i):
            at = (i - first_chunk) % 2
            return pltpu.make_async_copy(place(i), buf.at[at], sem.at[at])

        def take(i):
            net.until(i)
            if i not in started:
                copy(i).start()
                started.add(i)
            copy(i).wait()
            if i + 1 < end and net.ready > i:
                copy(i + 1).start()
                started.add(i + 1)
            return buf.at[(i - first_chunk) % 2]

        return take

    nsq = ns + 3 * nq
    stage_a = stager(sta, sa_sem, 0, nsq)
    stage_b = stager(stb, sb_sem, nsq, net.n)
    r = rs // ns
    for c in range(ns):
        st = stage_a(c)
        for k in range(kk):
            for s in range(GROUP):
                wb[k, s * rs + c * r : s * rs + (c + 1) * r, :] = st[s, k].astype(BF16)
    for k in range(1, nz):
        hidden_cols(wb.at[k - 1], lax.rem(z + k, nz))
        net.tick()
    put("row").start()

    shift1, scale1 = flat(small_ref, nm, 0, d), flat(small_ref, nm, d, 2 * d)

    @pl.loop(0, t // LB)
    def _(b):
        rows = aligned(b * LB, LB)
        xn, _ = layer_norm(hid_ref[rows, :])
        norm_ref[rows, :] = (xn * (1.0 + scale1) + shift1).astype(BF16)

    put("hid").start()
    put("norm").start()
    net.tick()

    qb = 256
    nb = t // qb

    def attend(g):
        gc = slice(g * loc, (g + 1) * loc)
        lane = lax.broadcasted_iota(jnp.int32, (qb, loc), 1) // HEAD_DIM
        vt_ref[...] = v_ref[:, gc].T
        for j in range(nb):
            kj = k_ref[j * qb : (j + 1) * qb, gc]
            for h in range(heads):
                x_ref[h * qb : (h + 1) * qb, j * qb : (j + 1) * qb] = jnp.where(
                    lane == h, kj, jnp.zeros_like(kj)
                )

        def block(i):
            rows = aligned(i * qb, qb)
            qi = q_ref[rows, gc]
            segq = segq_ref[0, pl.ds(0, 1), rows]

            def first(j, mx):
                at = aligned(j * qb, qb)
                s = dot(x_ref[:, at], qi, NT)
                same = wide(segk_ref[at, :], qb) == segq
                out = []
                for h in range(heads):
                    sh = jnp.where(same, s[h * qb : (h + 1) * qb], NEG)
                    f1_ref[at, h * qb : (h + 1) * qb] = sh
                    out.append(
                        jnp.maximum(mx[h], jnp.max(sh.reshape(qb // 8, 8, qb), axis=0))
                    )
                return out

            mx = lax.fori_loop(0, nb, first, [jnp.full((8, qb), NEG, F32)] * heads)
            ms = [jnp.max(m, axis=0, keepdims=True) for m in mx]

            def second(j, carry):
                ls, os_ = carry
                at = aligned(j * qb, qb)
                nl, nx = [], []
                for h in range(heads):
                    p = jnp.exp(f1_ref[at, h * qb : (h + 1) * qb] - ms[h])
                    nl.append(ls[h] + jnp.sum(p.reshape(qb // 8, 8, qb), axis=0))
                    vt = vt_ref[pl.ds(h * HEAD_DIM, HEAD_DIM), at]
                    nx.append(os_[h] + dot(vt, p.astype(BF16)))
                return nl, nx

            ls, os_ = lax.fori_loop(
                0,
                nb,
                second,
                ([jnp.zeros((8, qb), F32)] * heads, [jnp.zeros((HEAD_DIM, qb), F32)] * heads),
            )
            l1 = [jnp.sum(v, axis=0, keepdims=True) for v in ls]
            o = jnp.concatenate([os_[h] / l1[h] for h in range(heads)], axis=0)
            y_ref[rows, gc] = o.astype(BF16).T
            lse = [ms[h] + jnp.log(l1[h]) for h in range(heads)]
            lse_ref[g, :, rows] = jnp.concatenate(lse + [jnp.zeros((8 - heads, qb), F32)], axis=0)

        for half in range(2):
            pl.loop(half * nb // 2, (half + 1) * nb // 2)(block)
            net.tick()

    def project(a, k, w):
        out = (q_ref, k_ref, v_ref)[a]

        @pl.loop(0, t // TB)
        def _(b):
            rows = aligned(b * TB, TB)
            u = dot(norm_ref[rows, :], w[...])
            if a < 2:
                u = u * wide(cos_ref[rows, :], loc) + swap_halves(u) * wide(sin_ref[rows, :], loc)
            if a == 0:
                u = u.astype(BF16).astype(F32) * (HEAD_DIM**-0.5)
            out[rows, k * loc : (k + 1) * loc] = u.astype(BF16)

    for a in range(3):
        project(a, 0, (wq_ref, wk_ref, wv_ref)[a])
    net.tick()
    attend(0)
    r = rq // nq

    def w_out(a):
        return pltpu.make_async_copy(
            wb.at[:, pl.ds((a % 2) * d, d)], h_w16.at[:, a], w_sem.at[a % 2]
        )

    for a in range(3):
        if a == 2:
            w_out(0).wait()
        base = (a % 2) * d
        for c in range(nq):
            st = stage_a(ns + nq * a + c)
            for k in range(kk):
                for s in range(GROUP):
                    at = base + s * rq + c * r
                    wb[k, at : at + r, :] = st[s, k].astype(BF16)
        for k in range(1, nz):
            project(a, k, wb.at[k - 1, pl.ds(base, d)])
        net.tick()
        w_out(a).start()
        put("qkv"[a]).start()

    for g in range(1, nz):
        attend(g)
    put("norm").wait()
    att_ref, br_ref, gf_ref, n2_ref, gb_ref, ga_ref = y_ref, f1_ref, x_ref, norm_ref, q_ref, k_ref
    put("att").start()

    for c in range(no_):
        st = stage_b(nsq + c)
        for k in range(kk):
            for s in range(GROUP):
                at = s * ro + c * 2 * R_B
                o16_ref[k, at : at + 2 * R_B, :] = jnp.concatenate(
                    [st[s, 0, k], st[s, 1, k]], axis=0
                ).astype(BF16)
    row = lambda i: flat(small_ref, nm, i * d, (i + 1) * d)
    gate1, shift2, scale2, gate2 = row(2), row(3), row(4), row(5)

    @pl.loop(0, t // TB)
    def _(b):
        rows = aligned(b * TB, TB)
        br_ref[rows, :] = dot(att_ref[rows, :loc], wo_ref[...]) + dot(
            att_ref[rows, loc:], o16_ref[...].reshape(kk * loc, d)
        )

    net.tick()
    sums_ref[...] = jnp.zeros_like(sums_ref)
    fetch(9).wait()

    @pl.loop(0, t // LB)
    def _(b):
        rows = aligned(b * LB, LB)
        x2, _ = layer_norm(hid_ref[rows, :] + gate1 * br_ref[rows, :])
        n2_ref[rows, :] = (x2 * (1.0 + scale2) + shift2).astype(BF16)
        go = go_ref[rows, :].astype(F32)
        sums_ref[3:4, :] += jnp.sum(go, axis=0, keepdims=True)
        gf_ref[rows, :] = (gate2 * go).astype(BF16)

    net.tick()

    own = aligned(z * loc, loc)

    def units(first_time, rows, pre, dnv, back):
        act, slope = gelu_parts(pre)
        act = act.astype(BF16)
        ffn = dot(act, dnv[:, own])
        g_pre = (dot(gf_ref[rows, :], dnv[...], NT) * slope).astype(BF16)
        gn = back(g_pre)
        if first_time:
            out_ref[rows, :] = ffn
            gm_ref[rows, :] = gn
        else:
            out_ref[rows, :] += ffn
            gm_ref[rows, :] += gn
        return act, g_pre

    parts = 4
    sub = fl // parts
    w_out(1).wait()
    w_out(2).wait()
    act_s, gp_s = wb.at[0, pl.ds(0, t), pl.ds(0, sub)], wb.at[1, pl.ds(0, t), pl.ds(0, sub)]
    gwc = lambda j, s: pltpu.make_async_copy(
        gws.at[s], gw_ref.at[pl.ds(s * fl + j * sub, sub)], gw_sem.at[s]
    )
    for j in range(parts):
        cs = slice(j * sub, (j + 1) * sub)

        @pl.loop(0, t // TB)
        def _(b):
            rows = aligned(b * TB, TB)
            pre = dot(n2_ref[rows, :], up_ref[:, cs]) + bup_ref[:, cs]
            a, g = units(
                j == 0, rows, pre, dn_ref.at[cs, :], lambda gp: dot(gp, up_ref[:, cs], NT)
            )
            act_s[rows, :] = a
            gp_s[rows, :] = g

        if j > 0:
            for s in range(2):
                gwc(j - 1, s).wait()
        gbu_ref[:, cs] = jnp.sum(gp_s[...].astype(F32), axis=0, keepdims=True)
        gws[0] = dot(gp_s[...], n2_ref[...], TN)
        gws[1] = dot(act_s[...], gf_ref[...], TN)
        for s in range(2):
            gwc(j, s).start()
        net.tick()
    put("row").wait()
    at = 0
    f0 = ns + 3 * nq + no_
    for per in STEPS:
        w = per * GROUP * R_B
        for c in range(per):
            st = stage_b(f0 + at + c)
            u = GROUP * R_B
            for k in range(kk):
                for half, dst in ((0, ub), (1, db)):
                    dst[k * w + c * u : k * w + (c + 1) * u, :] = jnp.concatenate(
                        [st[s, half, k] for s in range(GROUP)], axis=0
                    ).astype(BF16)
        bias = []
        for k in range(kk):
            lo = nm + loc + at * GROUP * R_B
            bias.append(small_ref[lax.rem(z + k + 1, nz), :, lo : lo + w])
        bias = jnp.concatenate(bias, axis=1)
        w = w * kk

        @pl.loop(0, t // TB)
        def _(b):
            rows = aligned(b * TB, TB)
            pre = dot(n2_ref[rows, :], ub[:w, :], NT) + bias
            units(False, rows, pre, db.at[:w, :], lambda gp: dot(gp, ub[:w, :]))

        if net.t < net.n + net.lags[3]:
            net.tick()
        at += per

    put("q").wait()
    put("k").wait()
    bdn = bdn_ref[:, own]
    stb[0, 0, 0, 0, 0:1] = gate1
    stb[0, 0, 0, 1, 0:1] = gate2
    gate1_own = stb[0, 0, 0, 0, 0:1, own]
    gate2_own = stb[0, 0, 0, 1, 0:1, own]
    gg2_ref[...] = jnp.zeros_like(gg2_ref)

    @pl.loop(0, t // LB)
    def _(b):
        rows = aligned(b * LB, LB)
        ffn = out_ref[rows, :] + bdn
        gg2_ref[...] += jnp.sum(go_ref[rows, own].astype(F32) * ffn, axis=0, keepdims=True)
        out_ref[rows, :] = hid_ref[rows, own] + gate1_own * br_ref[rows, own] + gate2_own * ffn
        br = br_ref[rows, :]
        x2, r2 = layer_norm(hid_ref[rows, :] + gate1 * br)
        gn = gm_ref[rows, :]
        sums_ref[0:1, :] += jnp.sum(gn, axis=0, keepdims=True)
        sums_ref[1:2, :] += jnp.sum(gn * x2, axis=0, keepdims=True)
        gp = gn * (1.0 + scale2)
        gm = go_ref[rows, :].astype(F32) + r2 * (
            gp
            - jnp.mean(gp, axis=-1, keepdims=True)
            - x2 * jnp.mean(gp * x2, axis=-1, keepdims=True)
        )
        gm_ref[rows, :] = gm
        sums_ref[2:3, :] += jnp.sum(gm * br, axis=0, keepdims=True)
        gb_ref[rows, :] = (gate1 * gm).astype(BF16)

    put("gm").start()
    put("out").start()

    @pl.loop(0, t // TB)
    def _(b):
        rows = aligned(b * TB, TB)
        ga_ref[rows, :loc] = dot(gb_ref[rows, :], wo_ref[...], NT).astype(BF16)
        ga_ref[rows, loc:] = dot(
            gb_ref[rows, :], o16_ref[...].reshape(kk * loc, d), NT
        ).astype(BF16)

    put("ga").start()
    for s in range(2):
        gwc(parts - 1, s).wait()
    gws[0, :loc, :] = dot(att_ref[:, :loc], gb_ref[...], TN)
    last = lambda: pltpu.make_async_copy(
        gws.at[0, pl.ds(0, loc)], gw_ref.at[pl.ds(2 * fl, loc)], gw_sem.at[0]
    )
    last().start()
    net.drain()
    for k in range(1, nz):
        vec(k, z).wait_send()
    last().wait()
    for name in ("hid", "v", "att", "gm", "ga", "out", "cos", "sin"):
        put(name).wait()


def forward(x, y, go, wskip, wq, wk, wv, wo, up, dn, vec, bup, bdn, segq, segk, nz):
    t, d = x.shape
    loc = wq.shape[1]
    fl = up.shape[1]
    kk = nz - 1
    rs, rq, ro = 2 * d // GROUP, d // GROUP, loc // GROUP
    ns, nq, no = 4, 2, ro // (2 * R_B)
    nf = fl // GROUP // R_B
    chunks = [("skip", 0, c, rs // ns) for c in range(ns)]
    chunks += [("qkv", a, c, rq // nq) for a in range(3) for c in range(nq)]
    chunks += [("o", 0, c, 2 * R_B) for c in range(no)]
    chunks += [("ff", 0, c, R_B) for c in range(nf)]
    sd = jax.ShapeDtypeStruct
    dma = pltpu.SemaphoreType.DMA
    ins = [wskip, wq, wk, wv, wo, x, y, up, dn, go]
    e = nz * loc
    per = max(STEPS)
    nu = per * kk * GROUP * R_B
    outs = [
        sd((t, d), F32),
        sd((t, d), BF16),
        sd((t, e), BF16),
        sd((t, e), BF16),
        sd((t, e), BF16),
        sd((kk, 3, d, loc), BF16),
        sd((2 * loc, d), BF16),
        sd((t, e), BF16),
        sd((t, d), F32),
        sd((t, e), BF16),
        sd((t, loc), F32),
        sd((t, 128), F32),
        sd((t, 128), F32),
    ]
    more = [
        sd((2 * fl + loc, d), F32),
        sd((ns, GROUP, kk, rs // ns, loc), F32),
        sd((3, nq, GROUP, kk, rq // nq, loc), F32),
        sd((no, GROUP, 2, kk, R_B, d), F32),
        sd((nf, GROUP, 2, kk, R_B, d), F32),
    ]
    small = [
        sd((nz,) + vec.shape, F32),
        sd((nz, 8, t), F32),
        sd((8, d), F32),
        sd((1, fl), F32),
        sd((1, loc), F32),
    ]
    scratch = [pltpu.VMEM(v.shape, v.dtype) for v in ins]
    scratch += [
        pltpu.VMEM((t, d), F32),
        pltpu.VMEM((t, d), BF16),
        pltpu.VMEM((t, e), BF16),
        pltpu.VMEM((t, e), BF16),
        pltpu.VMEM((t, e), BF16),
        pltpu.VMEM((t, d), F32),
        pltpu.VMEM((t, d), F32),
        pltpu.VMEM((t, loc), F32),
        pltpu.VMEM((kk, 2 * d, loc), BF16),
        pltpu.VMEM((kk, loc, d), BF16),
        pltpu.VMEM((2, GROUP, kk, rs // ns, loc), F32),
        pltpu.VMEM((2, GROUP, 2, kk, R_B, d), F32),
        pltpu.VMEM((2, rs, loc), F32),
        pltpu.VMEM((2, 3, rq, loc), F32),
        pltpu.VMEM((2, no, 2, R_B, d), F32),
        pltpu.VMEM((2, 2, fl // GROUP, d), F32),
        pltpu.VMEM((nu, d), BF16),
        pltpu.VMEM((nu, d), BF16),
        pltpu.VMEM((2, max(fl // 4, loc), d), F32),
        pltpu.VMEM((loc, t), BF16),
        pltpu.VMEM((t, 128), F32),
        pltpu.VMEM((t, 128), F32),
        dma((len(ins),)),
        dma((12,)),
        dma((2,)),
        dma((2,)),
        dma((2,)),
        dma((2,)),
        dma((kk,)),
        dma((kk,)),
    ] + spread_sems(nz, len(chunks))
    return pl.pallas_call(
        functools.partial(forward_kernel, nz, chunks),
        out_shape=outs + more + small,
        in_specs=[ANY] * len(ins) + [VMEM] * 5,
        out_specs=[ANY] * (len(outs) + len(more)) + [VMEM] * 5,
        scratch_shapes=scratch,
        compiler_params=pltpu.CompilerParams(
            collective_id=0, has_side_effects=True, vmem_limit_bytes=63 << 20
        ),
    )(*ins, vec, bup, bdn, segq, segk)


class Halving:
    def __init__(self, ndp, src, out, refs, mine, partner):
        self.bits = ndp.bit_length() - 1
        self.ndp, self.src, self.out, self.mine, self.partner = ndp, src, out, mine, partner
        self.recv0, self.lev0, self.s0, self.r0 = refs[:4]
        self.rest = refs[4:]
        self.cw = src.shape[2] // 2
        self.orders = [list(range(1, self.bits)), list(range(self.bits - 1, 0, -1))]
        self.step = -1
        self.sent = []

    def _first(self, i):
        give = 2 * i + 1 - self.mine[0]
        return remote(
            self.src.at[give], self.recv0.at[i], self.s0.at[i], self.r0.at[i], self.partner[0]
        )

    def start(self):
        for i in range(self.ndp // 2):
            self._first(i).start()

    def _items(self, h):
        src, free = self.state[h]
        b = self.orders[h][self.step]
        at = free.index(b)
        lo = 1 << at
        left = [f for f in free if f != b]
        recv, out, ss, rr = self.rest[4 * (2 * self.step + h) : 4 * (2 * self.step + h) + 4]
        items = []
        for i in range(1 << len(left)):
            base = (i // lo) * 2 * lo + i % lo
            give = base + lo * (1 - self.mine[b])
            keep = base + lo * self.mine[b]
            c = functools.partial(
                remote, src.at[give], recv.at[i], ss.at[i], rr.at[i], self.partner[b]
            )
            items.append((c, keep, i))
        return items, src, recv, out, left

    def advance(self):
        if self.step < 0:
            for i in range(self.ndp // 2):
                self._first(i).wait_recv()
                self.lev0[i] = self.src[2 * i + self.mine[0]] + self.recv0[i]
            free = list(range(1, self.bits))
            self.state = [(self.lev0.at[:, :, pl.ds(h * self.cw, self.cw)], free) for h in (0, 1)]
        else:
            for h in (0, 1):
                items, src, recv, out, left = self.now[h]
                for c, keep, i in items:
                    c().wait_recv()
                    total = src[keep] + recv[i]
                    if self.step == self.bits - 2:
                        self.out[:, pl.ds(h * self.cw, self.cw)] = total
                    else:
                        out[i] = total
                    self.sent.append(c)
                self.state[h] = (out, left)
        self.step += 1
        if self.step < self.bits - 1:
            self.now = [self._items(h) for h in (0, 1)]
            for h in (0, 1):
                for c, _, _ in self.now[h][0]:
                    c().start()

    def finish(self):
        while self.step < self.bits - 1:
            self.advance()

    def drain(self):
        for c in self.sent:
            c().wait_send()
        for i in range(self.ndp // 2):
            self._first(i).wait_send()


def halving_refs(ndp, r, c):
    dma = pltpu.SemaphoreType.DMA
    bits = ndp.bit_length() - 1
    half = ndp // 2
    out = [pltpu.VMEM((half, r, c), F32), pltpu.VMEM((half, r, c), F32), dma((half,)), dma((half,))]
    for step in range(bits - 1):
        n = ndp >> (step + 2)
        for _ in range(2):
            out += [pltpu.VMEM((n, r, c // 2), F32), pltpu.VMEM((n, r, c // 2), F32), dma((n,)), dma((n,))]
    return out


def third_kernel(ndp, nz, nh, *refs):
    ni = 13
    ins = refs[:ni]
    small_ref, sums_ref, gbu_ref, gg2_ref, emb_ref = refs[ni : ni + 5]
    sqkv_ref, sskip_ref, all_ref, tot_ref = refs[ni + 5 : ni + 9]
    hbm = refs[ni + 9 : ni + 11]
    rest = refs[ni + 11 :]
    vmem_in = rest[:ni]
    (norm_ref, gq_ref, gk_ref, gv_ref, wq_ref, wk_ref, wv_ref, w_ref) = vmem_in[:8]
    (hid_ref, gm_ref, x_ref, y_ref, row_ref) = vmem_in[8:]
    gf_ref, gs_ref, gn_ref, low_ref, gwq, gws, vec, gz, mod_s = rest[ni : ni + 9]
    in_sem, out_sem, z_send, z_recv, q_send, q_recv = rest[ni + 9 : ni + 15]
    h1 = rest[ni + 15 : ni + 15 + nh]
    h2 = rest[ni + 15 + nh :]
    t, d = hid_ref.shape
    loc = wq_ref.shape[1]
    fl = gbu_ref.shape[1]
    nm = 6 * d // nz
    dp = lax.axis_index("dp")
    z = lax.axis_index("tensor")

    def fetch(i):
        return pltpu.make_async_copy(ins[i], vmem_in[i], in_sem.at[i])

    for i in range(ni):
        fetch(i).start()
    bits = ndp.bit_length() - 1
    mine = [lax.rem(dp // (1 << b), 2) for b in range(bits)]
    partner = [(dp + (1 << b) * (1 - 2 * mine[b]), z) for b in range(bits)]
    others = lambda j: (lax.rem(dp + j, ndp), z)
    bar = pltpu.get_barrier_semaphore()
    for j in range(1, ndp):
        pl.semaphore_signal(bar, inc=1, device_id=others(j), device_id_type=MESH)
    for k in range(1, nz):
        pl.semaphore_signal(
            bar, inc=1, device_id=(dp, lax.rem(z + k, nz)), device_id_type=MESH
        )
    grads = (gq_ref, gk_ref, gv_ref)
    for i in range(4):
        fetch(i).wait()
    for a in range(3):
        gwq[:, :, a * loc : (a + 1) * loc] = dot(
            norm_ref[...], grads[a][:, :loc], TN
        ).reshape(ndp, d // ndp, loc)
    pl.semaphore_wait(bar, ndp - 1 + nz - 1)
    one = Halving(ndp, gwq, sqkv_ref, h1, mine, partner)
    one.start()

    def part(k, zz):
        return remote(
            gg2_ref, gz.at[zz], z_send.at[k - 1], z_recv.at[k - 1], (dp, lax.rem(z + nz - k, nz))
        )

    for k in range(1, nz):
        part(k, z).start()
    gz[z] = gg2_ref[...]
    for i in range(4, 8):
        fetch(i).wait()
    own = (wq_ref, wk_ref, wv_ref)

    def product(b):
        rows = pl.ds(b * TB, TB)
        acc = dot(gq_ref[rows, :loc], wq_ref[...], NT)
        for k in range(nz):
            for a in range(3):
                if k == 0 and a == 0:
                    continue
                w = own[a][...] if k == 0 else w_ref[k - 1, a]
                acc = acc + dot(grads[a][rows, k * loc : (k + 1) * loc], w, NT)
        gn_ref[rows, :] = acc

    for b in range(t // TB):
        product(b)
        if b == 0:
            one.advance()
    one.advance()
    scale1 = flat(small_ref, nm, d, 2 * d)
    mod_s[...] = jnp.zeros_like(mod_s)
    for i in (8, 9):
        fetch(i).wait()

    @pl.loop(0, t // LB)
    def _(b):
        rows = aligned(b * LB, LB)
        x1, r1 = layer_norm(hid_ref[rows, :])
        gn = gn_ref[rows, :]
        mod_s[:, :d] += jnp.sum(gn, axis=0, keepdims=True)
        mod_s[:, d : 2 * d] += jnp.sum(gn * x1, axis=0, keepdims=True)
        gp = gn * (1.0 + scale1)
        gh = gm_ref[rows, :] + r1 * (
            gp
            - jnp.mean(gp, axis=-1, keepdims=True)
            - x1 * jnp.mean(gp * x1, axis=-1, keepdims=True)
        )
        mod_s[:, 6 * d :] += jnp.sum(gh, axis=0, keepdims=True)
        low_ref[rows, :] = gh.astype(BF16)

    one.advance()
    for i in (10, 11, 12):
        fetch(i).wait()
    cols = aligned(z * loc, loc)
    low_own = low_ref[:, cols]
    half = ndp // 2
    gws[:half] = dot(x_ref[...], low_own, TN).reshape(half, 2 * d // ndp, loc)
    gws[half:] = dot(y_ref[...], low_own, TN).reshape(half, 2 * d // ndp, loc)
    two = Halving(ndp, gws, sskip_ref, h2, mine, partner)
    two.start()
    for k in range(1, nz):
        part(k, lax.rem(z + k, nz)).wait_recv()
    gate2 = flat(small_ref, nm, 5 * d, 6 * d)
    mod_s[:, 2 * d : 3 * d] = sums_ref[2:3, :]
    mod_s[:, 3 * d : 4 * d] = sums_ref[0:1, :]
    mod_s[:, 4 * d : 5 * d] = sums_ref[1:2, :]
    for zz in range(nz):
        mod_s[:, 5 * d + zz * loc : 5 * d + (zz + 1) * loc] = gz[zz]
    o = nm
    vec[:, :o] = mod_s[:, aligned(z * nm, nm)]
    vec[:, o : o + loc] = mod_s[:, pl.ds(pl.multiple_of(6 * d + z * loc, loc), loc)]
    o += loc
    vec[:, o : o + fl] = gbu_ref[...]
    o += fl
    vec[:, o : o + d] = gate2 * sums_ref[3:4, :]
    o += d
    vec[:, o : o + d] = emb_ref[...]
    all_ref[dp] = vec[...]

    def give(j, row):
        return remote(vec, all_ref.at[row], q_send.at[j - 1], q_recv.at[j - 1], others(j))

    for j in range(1, ndp):
        give(j, dp).start()

    outs = (gf_ref, gs_ref)

    def put(i):
        return pltpu.make_async_copy(outs[i], hbm[i], out_sem.at[i])

    def back(i):
        w = row_ref[i * loc : (i + 1) * loc, :]
        for b in range(t // TB):
            rows = pl.ds(b * TB, TB)
            outs[i][rows, :] = dot(low_ref[rows, :], w, NT)
        put(i).start()

    two.advance()
    back(0)
    two.advance()
    one.finish()
    back(1)
    two.finish()
    for j in range(1, ndp):
        give(j, lax.rem(dp + ndp - j, ndp)).wait_recv()
    tot_ref[...] = jnp.sum(all_ref[...], axis=0)
    one.drain()
    two.drain()
    for k in range(1, nz):
        part(k, z).wait_send()
    for j in range(1, ndp):
        give(j, dp).wait_send()
    for i in range(2):
        put(i).wait()


def third(norm, gq, gk, gv, wq, wk, wv, w, hid, gm, x, y, row, small, sums, gbu, gg2, emb, ndp, nz):
    t, d = hid.shape
    loc = wq.shape[1]
    fl = gbu.shape[1]
    n = 6 * d // nz + loc + fl + 2 * d
    sd = jax.ShapeDtypeStruct
    dma = pltpu.SemaphoreType.DMA
    ins = [norm, gq, gk, gv, wq, wk, wv, w, hid, gm, x, y, row]
    scratch = [pltpu.VMEM(v.shape, v.dtype) for v in ins]
    scratch += [
        pltpu.VMEM((t, loc), F32),
        pltpu.VMEM((t, loc), F32),
        pltpu.VMEM((t, d), F32),
        pltpu.VMEM((t, d), BF16),
        pltpu.VMEM((ndp, d // ndp, 3 * loc), F32),
        pltpu.VMEM((ndp, 2 * d // ndp, loc), F32),
        pltpu.VMEM((1, n), F32),
        pltpu.VMEM((nz, 1, loc), F32),
        pltpu.VMEM((1, 7 * d), F32),
        dma((len(ins),)),
        dma((2,)),
        dma((nz - 1,)),
        dma((nz - 1,)),
        dma((ndp - 1,)),
        dma((ndp - 1,)),
    ]
    h1 = halving_refs(ndp, d // ndp, 3 * loc)
    h2 = halving_refs(ndp, 2 * d // ndp, loc)
    return pl.pallas_call(
        functools.partial(third_kernel, ndp, nz, len(h1)),
        out_shape=[
            sd((d // ndp, 3 * loc), F32),
            sd((2 * d // ndp, loc), F32),
            sd((ndp, 1, n), F32),
            sd((1, n), F32),
            sd((t, loc), F32),
            sd((t, loc), F32),
        ],
        in_specs=[ANY] * len(ins) + [VMEM] * 5,
        out_specs=[VMEM] * 4 + [ANY] * 2,
        scratch_shapes=scratch + h1 + h2,
        compiler_params=pltpu.CompilerParams(
            collective_id=1, has_side_effects=True, vmem_limit_bytes=62 << 20
        ),
    )(*ins, small, sums, gbu, gg2, emb)


def wide(table, lanes):
    return jnp.concatenate([table] * (lanes // 128), axis=1)


def swap_halves(u):
    n = u.shape[1]
    lane = lax.broadcasted_iota(jnp.int32, u.shape, 1)
    half = HEAD_DIM // 2
    return jnp.where(
        lane % HEAD_DIM < half, pltpu.roll(u, n - half, 1), pltpu.roll(u, half, 1)
    )


QB = 256
KB = 256


def stack_heads(dst, src, heads):
    lane = lax.broadcasted_iota(jnp.int32, src.shape, 1) // HEAD_DIM
    for h in range(heads):
        dst[:, h] = jnp.where(lane == h, src, jnp.zeros_like(src)).reshape(dst.shape[0], dst.shape[2], dst.shape[3])

def bwd_kernel(heads, QB, KB, lo_ref, hi_ref, q_ref, k_ref, v_ref, att_ref, g_ref, lse_ref, segq_ref, segk_ref, cos_ref, sin_ref, gq_ref, gk_ref, gv_ref,
               ks_ref, vs_ref, dk_ref, dv_ref, qm_ref, gm_ref, dq_ref):
    t, e = k_ref.shape
    stack_heads(ks_ref, k_ref[...], heads)
    stack_heads(vs_ref, v_ref[...], heads)
    dk_ref[...] = jnp.zeros_like(dk_ref); dv_ref[...] = jnp.zeros_like(dv_ref)
    row = lax.broadcasted_iota(jnp.int32, (8, e), 0); lane = lax.broadcasted_iota(jnp.int32, (8, e), 1)
    ind = jnp.where(lane//HEAD_DIM == row, 1.0, 0.0).astype(F32)
    @pl.loop(0, t//QB)
    def _(i):
        qs = pl.multiple_of(i*QB, QB)
        q = q_ref[pl.ds(qs, QB), :]; g = g_ref[pl.ds(qs, QB), :]
        segq = segq_ref[0, pl.ds(0,1), pl.ds(qs, QB)]
        prod = g.astype(F32)*att_ref[pl.ds(qs, QB), :].astype(F32)
        delta = dot(ind, prod, NT, lax.Precision.HIGHEST)
        lse = lse_ref[0, :, pl.ds(qs, QB)]
        laneq = lax.broadcasted_iota(jnp.int32, (QB, e), 1) // HEAD_DIM
        for h in range(heads):
            qm_ref[h * QB : (h + 1) * QB, :] = jnp.where(laneq == h, q, jnp.zeros_like(q))
            gm_ref[h * QB : (h + 1) * QB, :] = jnp.where(laneq == h, g, jnp.zeros_like(g))
        dq_ref[...] = jnp.zeros_like(dq_ref)

        def body(j, dq):
            start = pl.multiple_of(j*KB, KB)
            s = dot(ks_ref[j].reshape(heads*KB, e), q, NT)
            dpt = dot(vs_ref[j].reshape(heads*KB, e), g, NT)
            segk = segk_ref[pl.ds(start, KB), :]
            same = jnp.concatenate([segk]*(QB//128), axis=1) == segq
            ps, dss = [], []
            for h in range(heads):
                p = jnp.exp(jnp.where(same, s[h*KB:(h+1)*KB], NEG) - lse[h:h+1])
                ds = (p*(dpt[h*KB:(h+1)*KB] - delta[h:h+1])).astype(BF16)
                ps.append(p.astype(BF16)); dss.append(ds)
            dv_ref[pl.ds(start, KB), :] += dot(jnp.concatenate(ps, axis=1), gm_ref[...])
            dk_ref[pl.ds(start, KB), :] += dot(jnp.concatenate(dss, axis=1), qm_ref[...])
            dq_ref[...] += dot(jnp.concatenate(dss, axis=0), ks_ref[j].reshape(heads*KB, e), TN)
            return dq
        lax.fori_loop(lo_ref[i], hi_ref[i], body, 0)
        dqf = dq_ref[...] * (HEAD_DIM**-0.5)
        cos = wide(cos_ref[pl.ds(qs, QB), :], e)
        sin = wide(sin_ref[pl.ds(qs, QB), :], e)
        gq_ref[pl.ds(qs, QB), :] = (dqf*cos - swap_halves(dqf)*sin).astype(BF16)
    dk = dk_ref[...]
    gk_ref[...] = (dk * wide(cos_ref[...], e) - swap_halves(dk) * wide(sin_ref[...], e)).astype(BF16)
    gv_ref[...] = dv_ref[...].astype(BF16)

def attn_bwd(q,k,v,att,g,lse,seg_row,seg_col,lo,hi,cos,sin,groups,QB=QB,KB=KB):
    t = q.shape[0]; e = q.shape[1]//groups; heads = e//HEAD_DIM
    col = pl.BlockSpec((t,e), lambda g,*_: (0,g)); full = lambda s: pl.BlockSpec(s, lambda g,*_: (0,0))
    return pl.pallas_call(functools.partial(bwd_kernel, heads, QB, KB), out_shape=[jax.ShapeDtypeStruct(q.shape,BF16)]*3,
        grid_spec=pltpu.PrefetchScalarGridSpec(num_scalar_prefetch=2, grid=(groups,),
            in_specs=[col]*5+[pl.BlockSpec((1,8,t), lambda g,*_: (g,0,0)), pl.BlockSpec((1,8,t), lambda g,*_: (0,0,0)), full((t,128)), full((t,128)), full((t,128))],
            out_specs=[col]*3,
            scratch_shapes=[pltpu.VMEM((t//KB,heads,KB,e),BF16), pltpu.VMEM((t//KB,heads,KB,e),BF16), pltpu.VMEM((t,e),F32), pltpu.VMEM((t,e),F32), pltpu.VMEM((heads*QB,e),BF16), pltpu.VMEM((heads*QB,e),BF16), pltpu.VMEM((QB,e),F32)]),
        compiler_params=pltpu.CompilerParams(vmem_limit_bytes=58<<20))(lo,hi,q,k,v,att,g,lse,seg_row,seg_col,cos,sin)


def time_freqs(width):
    half = width // 2
    return jnp.exp(-math.log(10000.0) * jnp.arange(half, dtype=F32) / half)


def time_embed(flow_time, width):
    angles = 1000.0 * flow_time[:, None] * time_freqs(width)[None, :]
    both = jnp.concatenate([jnp.cos(angles), jnp.sin(angles)], axis=1)
    return jax.nn.silu(both).astype(BF16)


def per_device(ndp, nz, *args):
    (
        frames,
        skip_in,
        flow_time,
        segment_ids,
        w_skip,
        b_skip,
        w_mod,
        b_mod,
        w_q,
        w_k,
        w_v,
        w_o,
        w_up,
        b_up,
        w_dn,
        b_dn,
        out_grad,
    ) = args
    t, d = frames.shape
    loc = w_q.shape[1]
    fl = w_up.shape[1]
    dp = lax.axis_index("dp")
    z = lax.axis_index("tensor")
    embed = time_embed(flow_time, d)
    mod_part = dot(embed, w_mod)[0] + b_mod
    bup_order = b_up.reshape(GROUP, fl // GROUP // R_B, R_B).transpose(1, 0, 2).reshape(-1)
    own_small = jnp.concatenate([mod_part, b_skip, bup_order])[None, :]

    seg = segment_ids[0]
    below = jnp.sum((seg[None, :] < seg[::QB][:, None]).astype(jnp.int32), axis=1)
    upto = jnp.sum((seg[None, :] <= seg[QB - 1 :: QB][:, None]).astype(jnp.int32), axis=1)
    lo = below // KB
    hi = (upto + KB - 1) // KB
    seg_row = jnp.broadcast_to(seg[None, None, :], (1, 8, t))
    seg_col = jnp.broadcast_to(seg[:, None], (t, 128))

    (hidden, normed, q, k, v, wqkv, wrows, att, g_mid, g_att, output, cos, sin, gw) = (
        forwarded := forward(
            frames,
            skip_in,
            out_grad,
            w_skip,
            w_q,
            w_k,
            w_v,
            w_o,
            w_up,
            w_dn,
            own_small,
            b_up[None, :],
            b_dn[None, :],
            seg_row,
            seg_col,
            nz,
        )
    )[:14]
    small, lse, sums, g_b_up, g_gate2_own = forwarded[18:]
    first_sum = lax.psum_scatter(gw, "dp", scatter_dimension=1, tiled=True)
    gq, gk, gv = attn_bwd(q, k, v, att, g_att, lse, seg_row, seg_col, lo, hi, cos, sin, nz)
    s_qkv, s_w_skip, vecs, total, grad_frames, grad_skip = third(
        normed,
        gq,
        gk,
        gv,
        w_q,
        w_k,
        w_v,
        wqkv,
        hidden,
        g_mid,
        frames,
        skip_in,
        wrows,
        small,
        sums,
        g_b_up,
        g_gate2_own,
        embed.astype(F32),
        ndp,
        nz,
    )
    nm = mod_part.shape[0]
    sizes = [nm, loc, fl, d]
    offs = [sum(sizes[:i]) for i in range(len(sizes) + 1)]

    def share(i):
        n = sizes[i] // ndp
        return lax.dynamic_slice_in_dim(total[0], offs[i] + dp * n, n, 0)

    rows = d // ndp
    embeds = lax.dynamic_slice_in_dim(vecs[:, 0], offs[4] + dp * rows, rows, 1)
    s_w_mod = dot(embeds.astype(BF16), vecs[:, 0, :nm].astype(BF16), TN)
    s_up = first_sum[:fl].T
    s_dn = first_sum[fl : 2 * fl]
    s_o = first_sum[2 * fl :]
    return (
        output,
        grad_frames,
        grad_skip,
        s_w_skip,
        share(1),
        s_w_mod,
        share(0),
        s_qkv[:, :loc],
        s_qkv[:, loc : 2 * loc],
        s_qkv[:, 2 * loc :],
        s_o,
        s_up,
        share(2),
        s_dn,
        share(3),
    )


def solution(mesh):
    in_specs = (
        P("dp", None),
        P("dp", None),
        P("dp"),
        P("dp", None),
        P(None, "tensor"),
        P("tensor"),
        P(None, "tensor"),
        P("tensor"),
        P(None, "tensor"),
        P(None, "tensor"),
        P(None, "tensor"),
        P("tensor", None),
        P(None, "tensor"),
        P("tensor"),
        P("tensor", None),
        P(),
        P("dp", None),
    )
    out_specs = (
        P("dp", "tensor"),
        P("dp", "tensor"),
        P("dp", "tensor"),
        P("dp", "tensor"),
        P(("tensor", "dp")),
        P("dp", "tensor"),
        P(("tensor", "dp")),
        P("dp", "tensor"),
        P("dp", "tensor"),
        P("dp", "tensor"),
        P("tensor", "dp"),
        P("dp", "tensor"),
        P(("tensor", "dp")),
        P("tensor", "dp"),
        P("dp"),
    )
    return jax.shard_map(
        functools.partial(per_device, mesh.shape["dp"], mesh.shape["tensor"]),
        mesh=mesh,
        in_specs=in_specs,
        out_specs=out_specs,
        check_vma=False,
    )
```

```python
import functools
import math

import jax
import jax.numpy as jnp
from jax import lax
from jax.experimental import pallas as pl
from jax.experimental.pallas import tpu as pltpu
from jax.sharding import PartitionSpec as P

HEAD_DIM = 64
EPS = 1e-06
F32 = jnp.float32
BF16 = jnp.bfloat16
MESH = pl.DeviceIdType.MESH
ANY = pl.BlockSpec(memory_space=pl.ANY)
VMEM = pl.BlockSpec(memory_space=pltpu.VMEM)
GROUP = 8
NT = (((1,), (1,)), ((), ()))
NN = (((1,), (0,)), ((), ()))


def dot(a, b, dims=NN, precision=None):
    return lax.dot_general(a, b, dims, precision=precision, preferred_element_type=F32)


def remote(src, dst, send, recv, device):
    return pltpu.make_async_remote_copy(
        src_ref=src,
        dst_ref=dst,
        send_sem=send,
        recv_sem=recv,
        device_id=device,
        device_id_type=MESH,
    )


class Spread:
    def __init__(self, nz, n, src, land, plane, double, sems, lags):
        self.nz, self.n, self.src, self.land, self.plane = nz, n, src, land, plane
        self.double = double
        self.lags = lags
        self.zs, self.zr, self.ps, self.pr, self.rs = sems
        dp = lax.axis_index("dp")
        z = lax.axis_index("tensor")
        self.z = z
        core = lax.rem(dp, 2)
        x = lax.rem(dp // 2, 2)
        y = lax.rem(dp // 4, 2)
        dx = 2 - 4 * x
        dy = 4 - 8 * y
        b1 = y + core * (x - y)
        b2 = x + core * (y - x)
        d1 = dy + core * (dx - dy)
        d2 = dx + core * (dy - dx)
        self.slot = core * 4 + 2 * b2 + b1
        self.b1 = b1
        self.pair = core * 4 + 2 * b2
        self.near = {1: (dp + d1, z), 2: (dp + d2, z), 3: (dp + 1 - 2 * core, z)}
        self.far = {k: (dp, lax.rem(z + nz - k, nz)) for k in range(1, nz)}
        base = core * 4
        self.out = {1: (self.slot, 1), 2: (base + 2 * b2, 2), 3: (base, 4)}
        self.come = {
            1: (self.slot + 1 - 2 * b1, 1),
            2: (base + 2 - 2 * b2, 2),
            3: (4 - base, 4),
        }
        self.t = 0
        self.ready = -1

    def barrier(self):
        bar = pltpu.get_barrier_semaphore()
        devices = list(self.near.values()) + list(self.far.values())
        for device in devices:
            pl.semaphore_signal(bar, inc=1, device_id=device, device_id_type=MESH)
        pl.semaphore_wait(bar, len(devices))

    def _plane(self, i, k):
        return self.plane(i, self.pair if self.double(i) else self.slot, k)

    def _far(self, i, k):
        return remote(
            self.src(i),
            self._plane(i, k - 1),
            self.zs.at[i, k - 1],
            self.zr.at[i, k - 1],
            self.far[k],
        )

    def _relay(self, i):
        at = 2 * (2 - self.z)
        return remote(
            self._plane(i, 1),
            self._plane(i, at),
            self.rs.at[i],
            self.zr.at[i, at],
            (lax.axis_index("dp"), 3 * (self.z - 1)),
        )

    def _near(self, i, stage, inward):
        at, size = (self.come if inward else self.out)[stage]
        ref = self.land(i).at[pl.ds(at, size)]
        return remote(
            ref, ref, self.ps.at[i, stage - 1], self.pr.at[i, stage - 1], self.near[stage]
        )

    def tick(self):
        t, n, z = self.t, self.n, self.z
        l1, l2, l3, l4 = self.lags
        if t < n:
            self._far(t, 2).start()
            pl.when(z != 0)(lambda: self._far(t, 1).start())
            pl.when(z != 3)(lambda: self._far(t, 3).start())
        if 0 <= t - l4 < n:
            self._near(t - l4, 3, True).wait_recv()
            self.ready = t - l4
        for stage, lag in ((3, l3), (2, l2)):
            if 0 <= t - lag < n:
                if not (stage == 2 and self.double(t - lag)):
                    self._near(t - lag, stage - 1, True).wait_recv()
                self._near(t - lag, stage, False).start()
        i = t - l1
        if 0 <= i < n:
            self._far(i, 1).wait_recv()
            self._far(i, 3).wait_recv()
            pl.when((z == 0) | (z == 3))(lambda: self._far(i, 2).wait_recv())
            if not self.double(i):
                self._near(i, 1, False).start()
        j = t - l1 + 1
        if 0 <= j < n:

            @pl.when((z == 1) | (z == 2))
            def _():
                self._far(j, 2).wait_recv()
                self._relay(j).start()

        self.t += 1

    def until(self, i):
        while self.ready < i:
            self.tick()

    def drain(self):
        z = self.z
        for i in range(self.n):
            self._far(i, 2).wait_send()
            pl.when(z != 0)(lambda: self._far(i, 1).wait_send())
            pl.when(z != 3)(lambda: self._far(i, 3).wait_send())
            pl.when((z == 1) | (z == 2))(lambda: self._relay(i).wait_send())
            for stage in (1, 2, 3):
                if not (stage == 1 and self.double(i)):
                    self._near(i, stage, False).wait_send()


def spread_sems(nz, n):
    dma = pltpu.SemaphoreType.DMA
    kk = nz - 1
    return [dma((n, kk)), dma((n, kk)), dma((n, 3)), dma((n, 3)), dma((n,))]


def flat(small_ref, nm, lo, hi):
    parts = []
    while lo < hi:
        zz = lo // nm
        end = min(hi, (zz + 1) * nm)
        parts.append(small_ref[zz, :, lo - zz * nm : end - zz * nm])
        lo = end
    return parts[0] if len(parts) == 1 else jnp.concatenate(parts, axis=1)


def layer_norm(v):
    centred = v - jnp.mean(v, axis=-1, keepdims=True)
    r = lax.rsqrt(jnp.mean(centred * centred, axis=-1, keepdims=True) + EPS)
    return centred * r, r


TB = 512
LB = 128
LAGS = (4, 6, 8, 9)
DOUBLE = 2
R_B = 8
STEPS = (4, 4, 4, 2, 2)
NEG = -1e30


def aligned(at, size):
    return pl.ds(pl.multiple_of(at, size), size)


def gelu_parts(v):
    c = math.sqrt(2.0 / math.pi)
    v2 = v * v
    th = jnp.tanh(c * v * (1.0 + 0.044715 * v2))
    half = 0.5 * (1.0 + th)
    act = v * half
    slope = half + (0.5 * c) * v * (1.0 - th * th) * (1.0 + 3.0 * 0.044715 * v2)
    return act, slope


TN = (((0,), (0,)), ((), ()))


def forward_kernel(nz, chunks, *refs):
    ni, no = 10, 13
    ins = refs[:ni]
    vec_ref, bup_ref, bdn_ref, segq_ref, segk_ref = refs[ni : ni + 5]
    outs = refs[ni + 5 : ni + 5 + no]
    (h_hid, h_norm, h_q, h_k, h_v, h_w16, h_row, h_att, h_gm, h_ga, h_out, h_cos, h_sin) = outs
    rest = refs[ni + 5 + no :]
    gw_ref, lskip, lqkv, lo_, land = rest[:5]
    small_ref, lse_ref, sums_ref, gbu_ref, gg2_ref = rest[5:10]
    vmem_in = rest[10 : 10 + ni]
    (wskip_ref, wq_ref, wk_ref, wv_ref, wo_ref, x_ref, y_ref) = vmem_in[:7]
    (up_ref, dn_ref, go_ref) = vmem_in[7:]
    rest = rest[10 + ni :]
    (hid_ref, norm_ref, q_ref, k_ref, v_ref, f1_ref, gm_ref, out_ref) = rest[:8]
    (wb, o16_ref, sta, stb, pskip, pqkv, po, pc) = rest[8:16]
    (ub, db, gws, vt_ref, cos_ref, sin_ref) = rest[16:22]
    in_sem, out_sem, w_sem, sa_sem, sb_sem, gw_sem, vs, vr = rest[22:30]
    sems = rest[30:35]
    row_ref = ub.at[pl.ds(0, h_row.shape[0])]
    t, d = x_ref.shape
    loc = wq_ref.shape[1]
    fl = up_ref.shape[1]
    kk = nz - 1
    nm = 6 * d // nz
    rs, rq, pr = pskip.shape[1], pqkv.shape[2], fl // GROUP
    heads = loc // HEAD_DIM

    def fetch(i):
        return pltpu.make_async_copy(ins[i], vmem_in[i], in_sem.at[i])

    for i in range(ni):
        fetch(i).start()

    double = lambda i: i % 3 == DOUBLE

    def src(i):
        name, a, c, r = chunks[i]
        which = slice(None) if double(i) else net.b1
        if name == "skip":
            return pskip.at[which, pl.ds(c * r, r)]
        if name == "qkv":
            return pqkv.at[which, a, pl.ds(c * r, r)]
        if name == "o":
            return po.at[which, c]
        return pc.at[which, :, pl.ds(c * r, r)]

    def place(i):
        name, a, c, r = chunks[i]
        return {"skip": lskip, "qkv": lqkv.at[a], "o": lo_, "ff": land}[name].at[c]

    def plane(i, s, k):
        if double(i):
            s = pl.ds(s, 2)
        if chunks[i][0] in ("skip", "qkv"):
            return place(i).at[s, k]
        return place(i).at[s, :, k]

    net = Spread(nz, len(chunks), src, place, plane, double, sems, LAGS)
    z = net.z
    count = lambda name: sum(c[0] == name for c in chunks)
    ns, nq, no_, nf = count("skip"), count("qkv") // 3, count("o"), count("ff")
    results = {
        "hid": (hid_ref, h_hid),
        "norm": (norm_ref, h_norm),
        "q": (q_ref, h_q),
        "k": (k_ref, h_k),
        "v": (v_ref, h_v),
        "row": (row_ref, h_row),
        "att": (y_ref, h_att),
        "gm": (gm_ref, h_gm),
        "ga": (k_ref, h_ga),
        "out": (out_ref, h_out),
        "cos": (cos_ref, h_cos),
        "sin": (sin_ref, h_sin),
    }
    order = list(results)

    def put(name):
        return pltpu.make_async_copy(*results[name], out_sem.at[order.index(name)])

    small_ref[z] = vec_ref[...]
    fetch(0).wait()
    part = lambda ref, j, r: ref[aligned((net.pair + j) * r, r), :].astype(F32)
    for j in range(2):
        pskip[j] = part(wskip_ref, j, rs)
    net.barrier()
    net.tick()

    def vec(k, zz):
        return remote(vec_ref, small_ref.at[zz], vs.at[k - 1], vr.at[k - 1], net.far[k])

    for k in range(1, nz):
        vec(k, z).start()
    net.tick()
    for i in (1, 2, 3, 4):
        fetch(i).wait()
    ro = loc // GROUP
    for j in range(2):
        for a, w in enumerate((wq_ref, wk_ref, wv_ref)):
            pqkv[j, a] = part(w, j, rq)
        po[j] = part(wo_ref, j, ro).reshape(po.shape[1:])
    net.tick()
    for k in range(1, nz):
        vec(k, lax.rem(z + k, nz)).wait_recv()
    for i in (5, 6):
        fetch(i).wait()

    def hidden_cols(w, zz):
        bias = small_ref[zz, :, nm : nm + loc]
        cols = aligned(zz * loc, loc)

        @pl.loop(0, t // TB)
        def _(b):
            rows = aligned(b * TB, TB)
            acc = dot(x_ref[rows, :], w[:d, :]) + dot(y_ref[rows, :], w[d:, :])
            hid_ref[rows, cols] = acc + bias

        row_ref[:loc, cols] = w[aligned(z * loc, loc), :]
        row_ref[loc:, cols] = w[aligned(d + z * loc, loc), :]

    net.tick()
    hidden_cols(wskip_ref, z)
    for i in (7, 8):
        fetch(i).wait()
    for j in range(2):
        pc[j, 0] = up_ref[:, aligned((net.pair + j) * pr, pr)].astype(F32).T
        pc[j, 1] = part(dn_ref, j, pr)

    segs = segq_ref[0, pl.ds(0, 1)]
    starts = [
        jnp.sum(jnp.where(segs < i, 1.0, 0.0), axis=1, keepdims=True) for i in range(1, 4)
    ]
    lane1 = lax.broadcasted_iota(jnp.int32, (1, 128), 1)
    half = HEAD_DIM // 2
    inv = jnp.exp((-math.log(10000.0) * 2.0 / HEAD_DIM) * (lane1 % half).astype(F32))
    sign = jnp.where(lane1 % HEAD_DIM < half, -1.0, 1.0)

    @pl.loop(0, t // LB)
    def _(b):
        rows = aligned(b * LB, LB)
        sk = segk_ref[rows, :]
        at = jnp.zeros(sk.shape, F32)
        for i in range(1, 4):
            at = jnp.where(sk >= i, starts[i - 1], at)
        idx = (lax.broadcasted_iota(jnp.int32, sk.shape, 0) + b * LB).astype(F32)
        ang = (idx - at) * inv
        cos_ref[rows, :] = jnp.cos(ang)
        sin_ref[rows, :] = jnp.sin(ang) * sign

    put("cos").start()
    put("sin").start()

    def stager(buf, sem, first_chunk, end):
        started = set()

        def copy(i):
            at = (i - first_chunk) % 2
            return pltpu.make_async_copy(place(i), buf.at[at], sem.at[at])

        def take(i):
            net.until(i)
            if i not in started:
                copy(i).start()
                started.add(i)
            copy(i).wait()
            if i + 1 < end and net.ready > i:
                copy(i + 1).start()
                started.add(i + 1)
            return buf.at[(i - first_chunk) % 2]

        return take

    nsq = ns + 3 * nq
    stage_a = stager(sta, sa_sem, 0, nsq)
    stage_b = stager(stb, sb_sem, nsq, net.n)
    r = rs // ns
    for c in range(ns):
        st = stage_a(c)
        for k in range(kk):
            for s in range(GROUP):
                wb[k, s * rs + c * r : s * rs + (c + 1) * r, :] = st[s, k].astype(BF16)
    for k in range(1, nz):
        hidden_cols(wb.at[k - 1], lax.rem(z + k, nz))
        net.tick()
    put("row").start()

    shift1, scale1 = flat(small_ref, nm, 0, d), flat(small_ref, nm, d, 2 * d)

    @pl.loop(0, t // LB)
    def _(b):
        rows = aligned(b * LB, LB)
        xn, _ = layer_norm(hid_ref[rows, :])
        norm_ref[rows, :] = (xn * (1.0 + scale1) + shift1).astype(BF16)

    put("hid").start()
    put("norm").start()
    net.tick()

    qb = 256
    nb = t // qb

    def attend(g):
        gc = slice(g * loc, (g + 1) * loc)
        lane = lax.broadcasted_iota(jnp.int32, (qb, loc), 1) // HEAD_DIM
        vt_ref[...] = v_ref[:, gc].T
        for j in range(nb):
            kj = k_ref[j * qb : (j + 1) * qb, gc]
            for h in range(heads):
                x_ref[h * qb : (h + 1) * qb, j * qb : (j + 1) * qb] = jnp.where(
                    lane == h, kj, jnp.zeros_like(kj)
                )

        def block(i):
            rows = aligned(i * qb, qb)
            qi = q_ref[rows, gc]
            segq = segq_ref[0, pl.ds(0, 1), rows]

            def first(j, mx):
                at = aligned(j * qb, qb)
                s = dot(x_ref[:, at], qi, NT)
                same = wide(segk_ref[at, :], qb) == segq
                out = []
                for h in range(heads):
                    sh = jnp.where(same, s[h * qb : (h + 1) * qb], NEG)
                    f1_ref[at, h * qb : (h + 1) * qb] = sh
                    out.append(
                        jnp.maximum(mx[h], jnp.max(sh.reshape(qb // 8, 8, qb), axis=0))
                    )
                return out

            mx = lax.fori_loop(0, nb, first, [jnp.full((8, qb), NEG, F32)] * heads)
            ms = [jnp.max(m, axis=0, keepdims=True) for m in mx]

            def second(j, carry):
                ls, os_ = carry
                at = aligned(j * qb, qb)
                nl, nx = [], []
                for h in range(heads):
                    p = jnp.exp(f1_ref[at, h * qb : (h + 1) * qb] - ms[h])
                    nl.append(ls[h] + jnp.sum(p.reshape(qb // 8, 8, qb), axis=0))
                    vt = vt_ref[pl.ds(h * HEAD_DIM, HEAD_DIM), at]
                    nx.append(os_[h] + dot(vt, p.astype(BF16)))
                return nl, nx

            ls, os_ = lax.fori_loop(
                0,
                nb,
                second,
                ([jnp.zeros((8, qb), F32)] * heads, [jnp.zeros((HEAD_DIM, qb), F32)] * heads),
            )
            l1 = [jnp.sum(v, axis=0, keepdims=True) for v in ls]
            o = jnp.concatenate([os_[h] / l1[h] for h in range(heads)], axis=0)
            y_ref[rows, gc] = o.astype(BF16).T
            lse = [ms[h] + jnp.log(l1[h]) for h in range(heads)]
            lse_ref[g, :, rows] = jnp.concatenate(lse + [jnp.zeros((8 - heads, qb), F32)], axis=0)

        for half in range(2):
            pl.loop(half * nb // 2, (half + 1) * nb // 2)(block)
            net.tick()

    def project(a, k, w):
        out = (q_ref, k_ref, v_ref)[a]

        @pl.loop(0, t // TB)
        def _(b):
            rows = aligned(b * TB, TB)
            u = dot(norm_ref[rows, :], w[...])
            if a < 2:
                u = u * wide(cos_ref[rows, :], loc) + swap_halves(u) * wide(sin_ref[rows, :], loc)
            if a == 0:
                u = u.astype(BF16).astype(F32) * (HEAD_DIM**-0.5)
            out[rows, k * loc : (k + 1) * loc] = u.astype(BF16)

    for a in range(3):
        project(a, 0, (wq_ref, wk_ref, wv_ref)[a])
    net.tick()
    attend(0)
    r = rq // nq

    def w_out(a):
        return pltpu.make_async_copy(
            wb.at[:, pl.ds((a % 2) * d, d)], h_w16.at[:, a], w_sem.at[a % 2]
        )

    for a in range(3):
        if a == 2:
            w_out(0).wait()
        base = (a % 2) * d
        for c in range(nq):
            st = stage_a(ns + nq * a + c)
            for k in range(kk):
                for s in range(GROUP):
                    at = base + s * rq + c * r
                    wb[k, at : at + r, :] = st[s, k].astype(BF16)
        for k in range(1, nz):
            project(a, k, wb.at[k - 1, pl.ds(base, d)])
        net.tick()
        w_out(a).start()
        put("qkv"[a]).start()

    for g in range(1, nz):
        attend(g)
    put("norm").wait()
    att_ref, br_ref, gf_ref, n2_ref, gb_ref, ga_ref = y_ref, f1_ref, x_ref, norm_ref, q_ref, k_ref
    put("att").start()

    for c in range(no_):
        st = stage_b(nsq + c)
        for k in range(kk):
            for s in range(GROUP):
                at = s * ro + c * 2 * R_B
                o16_ref[k, at : at + 2 * R_B, :] = jnp.concatenate(
                    [st[s, 0, k], st[s, 1, k]], axis=0
                ).astype(BF16)
    row = lambda i: flat(small_ref, nm, i * d, (i + 1) * d)
    gate1, shift2, scale2, gate2 = row(2), row(3), row(4), row(5)

    @pl.loop(0, t // TB)
    def _(b):
        rows = aligned(b * TB, TB)
        br_ref[rows, :] = dot(att_ref[rows, :loc], wo_ref[...]) + dot(
            att_ref[rows, loc:], o16_ref[...].reshape(kk * loc, d)
        )

    net.tick()
    sums_ref[...] = jnp.zeros_like(sums_ref)
    fetch(9).wait()

    @pl.loop(0, t // LB)
    def _(b):
        rows = aligned(b * LB, LB)
        x2, _ = layer_norm(hid_ref[rows, :] + gate1 * br_ref[rows, :])
        n2_ref[rows, :] = (x2 * (1.0 + scale2) + shift2).astype(BF16)
        go = go_ref[rows, :].astype(F32)
        sums_ref[3:4, :] += jnp.sum(go, axis=0, keepdims=True)
        gf_ref[rows, :] = (gate2 * go).astype(BF16)

    net.tick()

    own = aligned(z * loc, loc)

    def units(first_time, rows, pre, dnv, back):
        act, slope = gelu_parts(pre)
        act = act.astype(BF16)
        ffn = dot(act, dnv[:, own])
        g_pre = (dot(gf_ref[rows, :], dnv[...], NT) * slope).astype(BF16)
        gn = back(g_pre)
        if first_time:
            out_ref[rows, :] = ffn
            gm_ref[rows, :] = gn
        else:
            out_ref[rows, :] += ffn
            gm_ref[rows, :] += gn
        return act, g_pre

    parts = 4
    sub = fl // parts
    w_out(1).wait()
    w_out(2).wait()
    act_s, gp_s = wb.at[0, pl.ds(0, t), pl.ds(0, sub)], wb.at[1, pl.ds(0, t), pl.ds(0, sub)]
    gwc = lambda j, s: pltpu.make_async_copy(
        gws.at[s], gw_ref.at[pl.ds(s * fl + j * sub, sub)], gw_sem.at[s]
    )
    for j in range(parts):
        cs = slice(j * sub, (j + 1) * sub)

        @pl.loop(0, t // TB)
        def _(b):
            rows = aligned(b * TB, TB)
            pre = dot(n2_ref[rows, :], up_ref[:, cs]) + bup_ref[:, cs]
            a, g = units(
                j == 0, rows, pre, dn_ref.at[cs, :], lambda gp: dot(gp, up_ref[:, cs], NT)
            )
            act_s[rows, :] = a
            gp_s[rows, :] = g

        if j > 0:
            for s in range(2):
                gwc(j - 1, s).wait()
        gbu_ref[:, cs] = jnp.sum(gp_s[...].astype(F32), axis=0, keepdims=True)
        gws[0] = dot(gp_s[...], n2_ref[...], TN)
        gws[1] = dot(act_s[...], gf_ref[...], TN)
        for s in range(2):
            gwc(j, s).start()
        net.tick()
    put("row").wait()
    at = 0
    f0 = ns + 3 * nq + no_
    for per in STEPS:
        w = per * GROUP * R_B
        for c in range(per):
            st = stage_b(f0 + at + c)
            u = GROUP * R_B
            for k in range(kk):
                for half, dst in ((0, ub), (1, db)):
                    dst[k * w + c * u : k * w + (c + 1) * u, :] = jnp.concatenate(
                        [st[s, half, k] for s in range(GROUP)], axis=0
                    ).astype(BF16)
        bias = []
        for k in range(kk):
            lo = nm + loc + at * GROUP * R_B
            bias.append(small_ref[lax.rem(z + k + 1, nz), :, lo : lo + w])
        bias = jnp.concatenate(bias, axis=1)
        w = w * kk

        @pl.loop(0, t // TB)
        def _(b):
            rows = aligned(b * TB, TB)
            pre = dot(n2_ref[rows, :], ub[:w, :], NT) + bias
            units(False, rows, pre, db.at[:w, :], lambda gp: dot(gp, ub[:w, :]))

        if net.t < net.n + net.lags[3]:
            net.tick()
        at += per

    put("q").wait()
    put("k").wait()
    bdn = bdn_ref[:, own]
    stb[0, 0, 0, 0, 0:1] = gate1
    stb[0, 0, 0, 1, 0:1] = gate2
    gate1_own = stb[0, 0, 0, 0, 0:1, own]
    gate2_own = stb[0, 0, 0, 1, 0:1, own]
    gg2_ref[...] = jnp.zeros_like(gg2_ref)

    @pl.loop(0, t // LB)
    def _(b):
        rows = aligned(b * LB, LB)
        ffn = out_ref[rows, :] + bdn
        gg2_ref[...] += jnp.sum(go_ref[rows, own].astype(F32) * ffn, axis=0, keepdims=True)
        out_ref[rows, :] = hid_ref[rows, own] + gate1_own * br_ref[rows, own] + gate2_own * ffn
        br = br_ref[rows, :]
        x2, r2 = layer_norm(hid_ref[rows, :] + gate1 * br)
        gn = gm_ref[rows, :]
        sums_ref[0:1, :] += jnp.sum(gn, axis=0, keepdims=True)
        sums_ref[1:2, :] += jnp.sum(gn * x2, axis=0, keepdims=True)
        gp = gn * (1.0 + scale2)
        gm = go_ref[rows, :].astype(F32) + r2 * (
            gp
            - jnp.mean(gp, axis=-1, keepdims=True)
            - x2 * jnp.mean(gp * x2, axis=-1, keepdims=True)
        )
        gm_ref[rows, :] = gm
        sums_ref[2:3, :] += jnp.sum(gm * br, axis=0, keepdims=True)
        gb_ref[rows, :] = (gate1 * gm).astype(BF16)

    put("gm").start()
    put("out").start()

    @pl.loop(0, t // TB)
    def _(b):
        rows = aligned(b * TB, TB)
        ga_ref[rows, :loc] = dot(gb_ref[rows, :], wo_ref[...], NT).astype(BF16)
        ga_ref[rows, loc:] = dot(
            gb_ref[rows, :], o16_ref[...].reshape(kk * loc, d), NT
        ).astype(BF16)

    put("ga").start()
    for s in range(2):
        gwc(parts - 1, s).wait()
    gws[0, :loc, :] = dot(att_ref[:, :loc], gb_ref[...], TN)
    last = lambda: pltpu.make_async_copy(
        gws.at[0, pl.ds(0, loc)], gw_ref.at[pl.ds(2 * fl, loc)], gw_sem.at[0]
    )
    last().start()
    net.drain()
    for k in range(1, nz):
        vec(k, z).wait_send()
    last().wait()
    for name in ("hid", "v", "att", "gm", "ga", "out", "cos", "sin"):
        put(name).wait()


def forward(x, y, go, wskip, wq, wk, wv, wo, up, dn, vec, bup, bdn, segq, segk, nz):
    t, d = x.shape
    loc = wq.shape[1]
    fl = up.shape[1]
    kk = nz - 1
    rs, rq, ro = 2 * d // GROUP, d // GROUP, loc // GROUP
    ns, nq, no = 4, 2, ro // (2 * R_B)
    nf = fl // GROUP // R_B
    chunks = [("skip", 0, c, rs // ns) for c in range(ns)]
    chunks += [("qkv", a, c, rq // nq) for a in range(3) for c in range(nq)]
    chunks += [("o", 0, c, 2 * R_B) for c in range(no)]
    chunks += [("ff", 0, c, R_B) for c in range(nf)]
    sd = jax.ShapeDtypeStruct
    dma = pltpu.SemaphoreType.DMA
    ins = [wskip, wq, wk, wv, wo, x, y, up, dn, go]
    e = nz * loc
    per = max(STEPS)
    nu = per * kk * GROUP * R_B
    outs = [
        sd((t, d), F32),
        sd((t, d), BF16),
        sd((t, e), BF16),
        sd((t, e), BF16),
        sd((t, e), BF16),
        sd((kk, 3, d, loc), BF16),
        sd((2 * loc, d), BF16),
        sd((t, e), BF16),
        sd((t, d), F32),
        sd((t, e), BF16),
        sd((t, loc), F32),
        sd((t, 128), F32),
        sd((t, 128), F32),
    ]
    more = [
        sd((2 * fl + loc, d), F32),
        sd((ns, GROUP, kk, rs // ns, loc), F32),
        sd((3, nq, GROUP, kk, rq // nq, loc), F32),
        sd((no, GROUP, 2, kk, R_B, d), F32),
        sd((nf, GROUP, 2, kk, R_B, d), F32),
    ]
    small = [
        sd((nz,) + vec.shape, F32),
        sd((nz, 8, t), F32),
        sd((8, d), F32),
        sd((1, fl), F32),
        sd((1, loc), F32),
    ]
    scratch = [pltpu.VMEM(v.shape, v.dtype) for v in ins]
    scratch += [
        pltpu.VMEM((t, d), F32),
        pltpu.VMEM((t, d), BF16),
        pltpu.VMEM((t, e), BF16),
        pltpu.VMEM((t, e), BF16),
        pltpu.VMEM((t, e), BF16),
        pltpu.VMEM((t, d), F32),
        pltpu.VMEM((t, d), F32),
        pltpu.VMEM((t, loc), F32),
        pltpu.VMEM((kk, 2 * d, loc), BF16),
        pltpu.VMEM((kk, loc, d), BF16),
        pltpu.VMEM((2, GROUP, kk, rs // ns, loc), F32),
        pltpu.VMEM((2, GROUP, 2, kk, R_B, d), F32),
        pltpu.VMEM((2, rs, loc), F32),
        pltpu.VMEM((2, 3, rq, loc), F32),
        pltpu.VMEM((2, no, 2, R_B, d), F32),
        pltpu.VMEM((2, 2, fl // GROUP, d), F32),
        pltpu.VMEM((nu, d), BF16),
        pltpu.VMEM((nu, d), BF16),
        pltpu.VMEM((2, max(fl // 4, loc), d), F32),
        pltpu.VMEM((loc, t), BF16),
        pltpu.VMEM((t, 128), F32),
        pltpu.VMEM((t, 128), F32),
        dma((len(ins),)),
        dma((12,)),
        dma((2,)),
        dma((2,)),
        dma((2,)),
        dma((2,)),
        dma((kk,)),
        dma((kk,)),
    ] + spread_sems(nz, len(chunks))
    return pl.pallas_call(
        functools.partial(forward_kernel, nz, chunks),
        out_shape=outs + more + small,
        in_specs=[ANY] * len(ins) + [VMEM] * 5,
        out_specs=[ANY] * (len(outs) + len(more)) + [VMEM] * 5,
        scratch_shapes=scratch,
        compiler_params=pltpu.CompilerParams(
            collective_id=0, has_side_effects=True, vmem_limit_bytes=63 << 20
        ),
    )(*ins, vec, bup, bdn, segq, segk)


class Halving:
    def __init__(self, ndp, src, out, refs, mine, partner):
        self.bits = ndp.bit_length() - 1
        self.ndp, self.src, self.out, self.mine, self.partner = ndp, src, out, mine, partner
        self.recv0, self.lev0, self.s0, self.r0 = refs[:4]
        self.rest = refs[4:]
        self.cw = src.shape[2] // 2
        self.orders = [list(range(1, self.bits)), list(range(self.bits - 1, 0, -1))]
        self.step = -1
        self.sent = []

    def _first(self, i):
        give = 2 * i + 1 - self.mine[0]
        return remote(
            self.src.at[give], self.recv0.at[i], self.s0.at[i], self.r0.at[i], self.partner[0]
        )

    def start(self):
        for i in range(self.ndp // 2):
            self._first(i).start()

    def _items(self, h):
        src, free = self.state[h]
        b = self.orders[h][self.step]
        at = free.index(b)
        lo = 1 << at
        left = [f for f in free if f != b]
        recv, out, ss, rr = self.rest[4 * (2 * self.step + h) : 4 * (2 * self.step + h) + 4]
        items = []
        for i in range(1 << len(left)):
            base = (i // lo) * 2 * lo + i % lo
            give = base + lo * (1 - self.mine[b])
            keep = base + lo * self.mine[b]
            c = functools.partial(
                remote, src.at[give], recv.at[i], ss.at[i], rr.at[i], self.partner[b]
            )
            items.append((c, keep, i))
        return items, src, recv, out, left

    def advance(self):
        if self.step < 0:
            for i in range(self.ndp // 2):
                self._first(i).wait_recv()
                self.lev0[i] = self.src[2 * i + self.mine[0]] + self.recv0[i]
            free = list(range(1, self.bits))
            self.state = [(self.lev0.at[:, :, pl.ds(h * self.cw, self.cw)], free) for h in (0, 1)]
        else:
            for h in (0, 1):
                items, src, recv, out, left = self.now[h]
                for c, keep, i in items:
                    c().wait_recv()
                    total = src[keep] + recv[i]
                    if self.step == self.bits - 2:
                        self.out[:, pl.ds(h * self.cw, self.cw)] = total
                    else:
                        out[i] = total
                    self.sent.append(c)
                self.state[h] = (out, left)
        self.step += 1
        if self.step < self.bits - 1:
            self.now = [self._items(h) for h in (0, 1)]
            for h in (0, 1):
                for c, _, _ in self.now[h][0]:
                    c().start()

    def finish(self):
        while self.step < self.bits - 1:
            self.advance()

    def drain(self):
        for c in self.sent:
            c().wait_send()
        for i in range(self.ndp // 2):
            self._first(i).wait_send()


def halving_refs(ndp, r, c):
    dma = pltpu.SemaphoreType.DMA
    bits = ndp.bit_length() - 1
    half = ndp // 2
    out = [pltpu.VMEM((half, r, c), F32), pltpu.VMEM((half, r, c), F32), dma((half,)), dma((half,))]
    for step in range(bits - 1):
        n = ndp >> (step + 2)
        for _ in range(2):
            out += [pltpu.VMEM((n, r, c // 2), F32), pltpu.VMEM((n, r, c // 2), F32), dma((n,)), dma((n,))]
    return out


def third_kernel(ndp, nz, nh, *refs):
    ni = 13
    ins = refs[:ni]
    small_ref, sums_ref, gbu_ref, gg2_ref, emb_ref = refs[ni : ni + 5]
    sqkv_ref, sskip_ref, all_ref, tot_ref = refs[ni + 5 : ni + 9]
    hbm = refs[ni + 9 : ni + 11]
    rest = refs[ni + 11 :]
    vmem_in = rest[:ni]
    (norm_ref, gq_ref, gk_ref, gv_ref, wq_ref, wk_ref, wv_ref, w_ref) = vmem_in[:8]
    (hid_ref, gm_ref, x_ref, y_ref, row_ref) = vmem_in[8:]
    gf_ref, gs_ref, gn_ref, low_ref, gwq, gws, vec, gz, mod_s = rest[ni : ni + 9]
    in_sem, out_sem, z_send, z_recv, q_send, q_recv = rest[ni + 9 : ni + 15]
    h1 = rest[ni + 15 : ni + 15 + nh]
    h2 = rest[ni + 15 + nh :]
    t, d = hid_ref.shape
    loc = wq_ref.shape[1]
    fl = gbu_ref.shape[1]
    nm = 6 * d // nz
    dp = lax.axis_index("dp")
    z = lax.axis_index("tensor")

    def fetch(i):
        return pltpu.make_async_copy(ins[i], vmem_in[i], in_sem.at[i])

    for i in range(ni):
        fetch(i).start()
    bits = ndp.bit_length() - 1
    mine = [lax.rem(dp // (1 << b), 2) for b in range(bits)]
    partner = [(dp + (1 << b) * (1 - 2 * mine[b]), z) for b in range(bits)]
    others = lambda j: (lax.rem(dp + j, ndp), z)
    bar = pltpu.get_barrier_semaphore()
    for j in range(1, ndp):
        pl.semaphore_signal(bar, inc=1, device_id=others(j), device_id_type=MESH)
    for k in range(1, nz):
        pl.semaphore_signal(
            bar, inc=1, device_id=(dp, lax.rem(z + k, nz)), device_id_type=MESH
        )
    grads = (gq_ref, gk_ref, gv_ref)
    for i in range(4):
        fetch(i).wait()
    for a in range(3):
        gwq[:, :, a * loc : (a + 1) * loc] = dot(
            norm_ref[...], grads[a][:, :loc], TN
        ).reshape(ndp, d // ndp, loc)
    pl.semaphore_wait(bar, ndp - 1 + nz - 1)
    one = Halving(ndp, gwq, sqkv_ref, h1, mine, partner)
    one.start()

    def part(k, zz):
        return remote(
            gg2_ref, gz.at[zz], z_send.at[k - 1], z_recv.at[k - 1], (dp, lax.rem(z + nz - k, nz))
        )

    for k in range(1, nz):
        part(k, z).start()
    gz[z] = gg2_ref[...]
    for i in range(4, 8):
        fetch(i).wait()
    own = (wq_ref, wk_ref, wv_ref)

    def product(b):
        rows = pl.ds(b * TB, TB)
        acc = dot(gq_ref[rows, :loc], wq_ref[...], NT)
        for k in range(nz):
            for a in range(3):
                if k == 0 and a == 0:
                    continue
                w = own[a][...] if k == 0 else w_ref[k - 1, a]
                acc = acc + dot(grads[a][rows, k * loc : (k + 1) * loc], w, NT)
        gn_ref[rows, :] = acc

    for b in range(t // TB):
        product(b)
        if b == 0:
            one.advance()
    one.advance()
    scale1 = flat(small_ref, nm, d, 2 * d)
    mod_s[...] = jnp.zeros_like(mod_s)
    for i in (8, 9):
        fetch(i).wait()

    @pl.loop(0, t // LB)
    def _(b):
        rows = aligned(b * LB, LB)
        x1, r1 = layer_norm(hid_ref[rows, :])
        gn = gn_ref[rows, :]
        mod_s[:, :d] += jnp.sum(gn, axis=0, keepdims=True)
        mod_s[:, d : 2 * d] += jnp.sum(gn * x1, axis=0, keepdims=True)
        gp = gn * (1.0 + scale1)
        gh = gm_ref[rows, :] + r1 * (
            gp
            - jnp.mean(gp, axis=-1, keepdims=True)
            - x1 * jnp.mean(gp * x1, axis=-1, keepdims=True)
        )
        mod_s[:, 6 * d :] += jnp.sum(gh, axis=0, keepdims=True)
        low_ref[rows, :] = gh.astype(BF16)

    one.advance()
    for i in (10, 11, 12):
        fetch(i).wait()
    cols = aligned(z * loc, loc)
    low_own = low_ref[:, cols]
    half = ndp // 2
    gws[:half] = dot(x_ref[...], low_own, TN).reshape(half, 2 * d // ndp, loc)
    gws[half:] = dot(y_ref[...], low_own, TN).reshape(half, 2 * d // ndp, loc)
    two = Halving(ndp, gws, sskip_ref, h2, mine, partner)
    two.start()
    for k in range(1, nz):
        part(k, lax.rem(z + k, nz)).wait_recv()
    gate2 = flat(small_ref, nm, 5 * d, 6 * d)
    mod_s[:, 2 * d : 3 * d] = sums_ref[2:3, :]
    mod_s[:, 3 * d : 4 * d] = sums_ref[0:1, :]
    mod_s[:, 4 * d : 5 * d] = sums_ref[1:2, :]
    for zz in range(nz):
        mod_s[:, 5 * d + zz * loc : 5 * d + (zz + 1) * loc] = gz[zz]
    o = nm
    vec[:, :o] = mod_s[:, aligned(z * nm, nm)]
    vec[:, o : o + loc] = mod_s[:, pl.ds(pl.multiple_of(6 * d + z * loc, loc), loc)]
    o += loc
    vec[:, o : o + fl] = gbu_ref[...]
    o += fl
    vec[:, o : o + d] = gate2 * sums_ref[3:4, :]
    o += d
    vec[:, o : o + d] = emb_ref[...]
    all_ref[dp] = vec[...]

    def give(j, row):
        return remote(vec, all_ref.at[row], q_send.at[j - 1], q_recv.at[j - 1], others(j))

    for j in range(1, ndp):
        give(j, dp).start()

    outs = (gf_ref, gs_ref)

    def put(i):
        return pltpu.make_async_copy(outs[i], hbm[i], out_sem.at[i])

    def back(i):
        w = row_ref[i * loc : (i + 1) * loc, :]
        for b in range(t // TB):
            rows = pl.ds(b * TB, TB)
            outs[i][rows, :] = dot(low_ref[rows, :], w, NT)
        put(i).start()

    two.advance()
    back(0)
    two.advance()
    one.finish()
    back(1)
    two.finish()
    for j in range(1, ndp):
        give(j, lax.rem(dp + ndp - j, ndp)).wait_recv()
    tot_ref[...] = jnp.sum(all_ref[...], axis=0)
    one.drain()
    two.drain()
    for k in range(1, nz):
        part(k, z).wait_send()
    for j in range(1, ndp):
        give(j, dp).wait_send()
    for i in range(2):
        put(i).wait()


def third(norm, gq, gk, gv, wq, wk, wv, w, hid, gm, x, y, row, small, sums, gbu, gg2, emb, ndp, nz):
    t, d = hid.shape
    loc = wq.shape[1]
    fl = gbu.shape[1]
    n = 6 * d // nz + loc + fl + 2 * d
    sd = jax.ShapeDtypeStruct
    dma = pltpu.SemaphoreType.DMA
    ins = [norm, gq, gk, gv, wq, wk, wv, w, hid, gm, x, y, row]
    scratch = [pltpu.VMEM(v.shape, v.dtype) for v in ins]
    scratch += [
        pltpu.VMEM((t, loc), F32),
        pltpu.VMEM((t, loc), F32),
        pltpu.VMEM((t, d), F32),
        pltpu.VMEM((t, d), BF16),
        pltpu.VMEM((ndp, d // ndp, 3 * loc), F32),
        pltpu.VMEM((ndp, 2 * d // ndp, loc), F32),
        pltpu.VMEM((1, n), F32),
        pltpu.VMEM((nz, 1, loc), F32),
        pltpu.VMEM((1, 7 * d), F32),
        dma((len(ins),)),
        dma((2,)),
        dma((nz - 1,)),
        dma((nz - 1,)),
        dma((ndp - 1,)),
        dma((ndp - 1,)),
    ]
    h1 = halving_refs(ndp, d // ndp, 3 * loc)
    h2 = halving_refs(ndp, 2 * d // ndp, loc)
    return pl.pallas_call(
        functools.partial(third_kernel, ndp, nz, len(h1)),
        out_shape=[
            sd((d // ndp, 3 * loc), F32),
            sd((2 * d // ndp, loc), F32),
            sd((ndp, 1, n), F32),
            sd((1, n), F32),
            sd((t, loc), F32),
            sd((t, loc), F32),
        ],
        in_specs=[ANY] * len(ins) + [VMEM] * 5,
        out_specs=[VMEM] * 4 + [ANY] * 2,
        scratch_shapes=scratch + h1 + h2,
        compiler_params=pltpu.CompilerParams(
            collective_id=1, has_side_effects=True, vmem_limit_bytes=62 << 20
        ),
    )(*ins, small, sums, gbu, gg2, emb)


def wide(table, lanes):
    return jnp.concatenate([table] * (lanes // 128), axis=1)


def swap_halves(u):
    n = u.shape[1]
    lane = lax.broadcasted_iota(jnp.int32, u.shape, 1)
    half = HEAD_DIM // 2
    return jnp.where(
        lane % HEAD_DIM < half, pltpu.roll(u, n - half, 1), pltpu.roll(u, half, 1)
    )


QB = 256
KB = 256


def stack_heads(dst, src, heads):
    lane = lax.broadcasted_iota(jnp.int32, src.shape, 1) // HEAD_DIM
    for h in range(heads):
        dst[:, h] = jnp.where(lane == h, src, jnp.zeros_like(src)).reshape(dst.shape[0], dst.shape[2], dst.shape[3])

def bwd_kernel(heads, QB, KB, lo_ref, hi_ref, q_ref, k_ref, v_ref, att_ref, g_ref, lse_ref, segq_ref, segk_ref, cos_ref, sin_ref, gq_ref, gk_ref, gv_ref,
               ks_ref, vs_ref, dk_ref, dv_ref, qm_ref, gm_ref, dq_ref):
    t, e = k_ref.shape
    stack_heads(ks_ref, k_ref[...], heads)
    stack_heads(vs_ref, v_ref[...], heads)
    dk_ref[...] = jnp.zeros_like(dk_ref); dv_ref[...] = jnp.zeros_like(dv_ref)
    row = lax.broadcasted_iota(jnp.int32, (8, e), 0); lane = lax.broadcasted_iota(jnp.int32, (8, e), 1)
    ind = jnp.where(lane//HEAD_DIM == row, 1.0, 0.0).astype(F32)
    @pl.loop(0, t//QB)
    def _(i):
        qs = pl.multiple_of(i*QB, QB)
        q = q_ref[pl.ds(qs, QB), :]; g = g_ref[pl.ds(qs, QB), :]
        segq = segq_ref[0, pl.ds(0,1), pl.ds(qs, QB)]
        prod = g.astype(F32)*att_ref[pl.ds(qs, QB), :].astype(F32)
        delta = dot(ind, prod, NT, lax.Precision.HIGHEST)
        lse = lse_ref[0, :, pl.ds(qs, QB)]
        laneq = lax.broadcasted_iota(jnp.int32, (QB, e), 1) // HEAD_DIM
        for h in range(heads):
            qm_ref[h * QB : (h + 1) * QB, :] = jnp.where(laneq == h, q, jnp.zeros_like(q))
            gm_ref[h * QB : (h + 1) * QB, :] = jnp.where(laneq == h, g, jnp.zeros_like(g))
        dq_ref[...] = jnp.zeros_like(dq_ref)

        def body(j, dq):
            start = pl.multiple_of(j*KB, KB)
            s = dot(ks_ref[j].reshape(heads*KB, e), q, NT)
            dpt = dot(vs_ref[j].reshape(heads*KB, e), g, NT)
            segk = segk_ref[pl.ds(start, KB), :]
            same = jnp.concatenate([segk]*(QB//128), axis=1) == segq
            ps, dss = [], []
            for h in range(heads):
                p = jnp.exp(jnp.where(same, s[h*KB:(h+1)*KB], NEG) - lse[h:h+1])
                ds = (p*(dpt[h*KB:(h+1)*KB] - delta[h:h+1])).astype(BF16)
                ps.append(p.astype(BF16)); dss.append(ds)
            dv_ref[pl.ds(start, KB), :] += dot(jnp.concatenate(ps, axis=1), gm_ref[...])
            dk_ref[pl.ds(start, KB), :] += dot(jnp.concatenate(dss, axis=1), qm_ref[...])
            dq_ref[...] += dot(jnp.concatenate(dss, axis=0), ks_ref[j].reshape(heads*KB, e), TN)
            return dq
        lax.fori_loop(lo_ref[i], hi_ref[i], body, 0)
        dqf = dq_ref[...] * (HEAD_DIM**-0.5)
        cos = wide(cos_ref[pl.ds(qs, QB), :], e)
        sin = wide(sin_ref[pl.ds(qs, QB), :], e)
        gq_ref[pl.ds(qs, QB), :] = (dqf*cos - swap_halves(dqf)*sin).astype(BF16)
    dk = dk_ref[...]
    gk_ref[...] = (dk * wide(cos_ref[...], e) - swap_halves(dk) * wide(sin_ref[...], e)).astype(BF16)
    gv_ref[...] = dv_ref[...].astype(BF16)

def attn_bwd(q,k,v,att,g,lse,seg_row,seg_col,lo,hi,cos,sin,groups,QB=QB,KB=KB):
    t = q.shape[0]; e = q.shape[1]//groups; heads = e//HEAD_DIM
    col = pl.BlockSpec((t,e), lambda g,*_: (0,g)); full = lambda s: pl.BlockSpec(s, lambda g,*_: (0,0))
    return pl.pallas_call(functools.partial(bwd_kernel, heads, QB, KB), out_shape=[jax.ShapeDtypeStruct(q.shape,BF16)]*3,
        grid_spec=pltpu.PrefetchScalarGridSpec(num_scalar_prefetch=2, grid=(groups,),
            in_specs=[col]*5+[pl.BlockSpec((1,8,t), lambda g,*_: (g,0,0)), pl.BlockSpec((1,8,t), lambda g,*_: (0,0,0)), full((t,128)), full((t,128)), full((t,128))],
            out_specs=[col]*3,
            scratch_shapes=[pltpu.VMEM((t//KB,heads,KB,e),BF16), pltpu.VMEM((t//KB,heads,KB,e),BF16), pltpu.VMEM((t,e),F32), pltpu.VMEM((t,e),F32), pltpu.VMEM((heads*QB,e),BF16), pltpu.VMEM((heads*QB,e),BF16), pltpu.VMEM((QB,e),F32)]),
        compiler_params=pltpu.CompilerParams(vmem_limit_bytes=58<<20))(lo,hi,q,k,v,att,g,lse,seg_row,seg_col,cos,sin)


def time_freqs(width):
    half = width // 2
    return jnp.exp(-math.log(10000.0) * jnp.arange(half, dtype=F32) / half)


def time_embed(flow_time, width):
    angles = 1000.0 * flow_time[:, None] * time_freqs(width)[None, :]
    both = jnp.concatenate([jnp.cos(angles), jnp.sin(angles)], axis=1)
    return jax.nn.silu(both).astype(BF16)


def per_device(ndp, nz, *args):
    (
        frames,
        skip_in,
        flow_time,
        segment_ids,
        w_skip,
        b_skip,
        w_mod,
        b_mod,
        w_q,
        w_k,
        w_v,
        w_o,
        w_up,
        b_up,
        w_dn,
        b_dn,
        out_grad,
    ) = args
    t, d = frames.shape
    loc = w_q.shape[1]
    fl = w_up.shape[1]
    dp = lax.axis_index("dp")
    z = lax.axis_index("tensor")
    embed = time_embed(flow_time, d)
    mod_part = dot(embed, w_mod)[0] + b_mod
    bup_order = b_up.reshape(GROUP, fl // GROUP // R_B, R_B).transpose(1, 0, 2).reshape(-1)
    own_small = jnp.concatenate([mod_part, b_skip, bup_order])[None, :]

    seg = segment_ids[0]
    below = jnp.sum((seg[None, :] < seg[::QB][:, None]).astype(jnp.int32), axis=1)
    upto = jnp.sum((seg[None, :] <= seg[QB - 1 :: QB][:, None]).astype(jnp.int32), axis=1)
    lo = below // KB
    hi = (upto + KB - 1) // KB
    seg_row = jnp.broadcast_to(seg[None, None, :], (1, 8, t))
    seg_col = jnp.broadcast_to(seg[:, None], (t, 128))

    (hidden, normed, q, k, v, wqkv, wrows, att, g_mid, g_att, output, cos, sin, gw) = (
        forwarded := forward(
            frames,
            skip_in,
            out_grad,
            w_skip,
            w_q,
            w_k,
            w_v,
            w_o,
            w_up,
            w_dn,
            own_small,
            b_up[None, :],
            b_dn[None, :],
            seg_row,
            seg_col,
            nz,
        )
    )[:14]
    small, lse, sums, g_b_up, g_gate2_own = forwarded[18:]
    first_sum = lax.psum_scatter(gw, "dp", scatter_dimension=1, tiled=True)
    gq, gk, gv = attn_bwd(q, k, v, att, g_att, lse, seg_row, seg_col, lo, hi, cos, sin, nz)
    s_qkv, s_w_skip, vecs, total, grad_frames, grad_skip = third(
        normed,
        gq,
        gk,
        gv,
        w_q,
        w_k,
        w_v,
        wqkv,
        hidden,
        g_mid,
        frames,
        skip_in,
        wrows,
        small,
        sums,
        g_b_up,
        g_gate2_own,
        embed.astype(F32),
        ndp,
        nz,
    )
    nm = mod_part.shape[0]
    sizes = [nm, loc, fl, d]
    offs = [sum(sizes[:i]) for i in range(len(sizes) + 1)]

    def share(i):
        n = sizes[i] // ndp
        return lax.dynamic_slice_in_dim(total[0], offs[i] + dp * n, n, 0)

    rows = d // ndp
    embeds = lax.dynamic_slice_in_dim(vecs[:, 0], offs[4] + dp * rows, rows, 1)
    s_w_mod = dot(embeds.astype(BF16), vecs[:, 0, :nm].astype(BF16), TN)
    s_up = first_sum[:fl].T
    s_dn = first_sum[fl : 2 * fl]
    s_o = first_sum[2 * fl :]
    return (
        output,
        grad_frames,
        grad_skip,
        s_w_skip,
        share(1),
        s_w_mod,
        share(0),
        s_qkv[:, :loc],
        s_qkv[:, loc : 2 * loc],
        s_qkv[:, 2 * loc :],
        s_o,
        s_up,
        share(2),
        s_dn,
        share(3),
    )


def solution(mesh):
    in_specs = (
        P("dp", None),
        P("dp", None),
        P("dp"),
        P("dp", None),
        P(None, "tensor"),
        P("tensor"),
        P(None, "tensor"),
        P("tensor"),
        P(None, "tensor"),
        P(None, "tensor"),
        P(None, "tensor"),
        P("tensor", None),
        P(None, "tensor"),
        P("tensor"),
        P("tensor", None),
        P(),
        P("dp", None),
    )
    out_specs = (
        P("dp", "tensor"),
        P("dp", "tensor"),
        P("dp", "tensor"),
        P("dp", "tensor"),
        P(("tensor", "dp")),
        P("dp", "tensor"),
        P(("tensor", "dp")),
        P("dp", "tensor"),
        P("dp", "tensor"),
        P("dp", "tensor"),
        P("tensor", "dp"),
        P("dp", "tensor"),
        P(("tensor", "dp")),
        P("tensor", "dp"),
        P("dp"),
    )
    return jax.shard_map(
        functools.partial(per_device, mesh.shape["dp"], mesh.shape["tensor"]),
        mesh=mesh,
        in_specs=in_specs,
        out_specs=out_specs,
        check_vma=False,
    )
```
